32 devices in a mesh: dp: 16 (over z, x, core), tensor: 2 (over y).
Axes of the slice: x: 2, y: 2, z: 4, core: 2. Of those that a mesh axis runs over, the one named last changes fastest.
Arguments:
- tokens: bfloat16 [16384, 1024], P(('dp', 'tensor')), may hold values from -6 to 6
- teacher: float32 [16384, 1024], P(('dp', 'tensor')), may hold values from -6 to 6
- valid_mask: int32 [16384], P(('dp', 'tensor')), may hold values from 0 to 1, as said below
- segments: int32 [16384], P('dp'), may hold values from 0 to 255, never falling along the last dimension, each value on 1 to 512 neighbouring positions
- loss_scale: float32 [], replicated, may hold values from 8388608 to 33554432
- qkv_weight: bfloat16 [3, 1024, 1024], P(None, 'dp', 'tensor'), may hold values from -0.1875 to 0.1875
- qv_bias: bfloat16 [2, 16, 64], P(None, 'tensor', 'dp'), may hold values from -3 to 3
- out_weight: bfloat16 [1024, 1024], P('tensor', 'dp'), may hold values from -0.75 to 0.75
- out_bias: bfloat16 [16, 64], P('tensor', 'dp'), may hold values from -2 to 2
- first_gain: bfloat16 [16, 64], P('tensor', 'dp'), may hold values from 0.25 to 1.75
- first_shift: bfloat16 [16, 64], P('tensor', 'dp'), may hold values from -2 to 2
- up_weight: bfloat16 [1024, 4096], P('dp', 'tensor'), may hold values from -0.1875 to 0.1875
- up_bias: bfloat16 [64, 64], P('tensor', 'dp'), may hold values from -3 to 3
- down_weight: bfloat16 [4096, 1024], P('tensor', 'dp'), may hold values from -0.09375 to 0.09375
- down_bias: bfloat16 [16, 64], P('tensor', 'dp'), may hold values from -2 to 2
- second_gain: bfloat16 [16, 64], P('tensor', 'dp'), may hold values from 0.25 to 1.75
- second_shift: bfloat16 [16, 64], P('tensor', 'dp'), may hold values from -2 to 2
Outputs:
- layer_output: bfloat16 [16384, 1024], P(('dp', 'tensor'))
- loss_value: float32 [], replicated
- grad_tokens: float32 [16384, 1024], P(('dp', 'tensor'))
- grad_qkv_weight: float32 [3, 1024, 1024], P(None, 'dp', 'tensor')
- grad_qv_bias: float32 [2, 16, 64], P(None, 'tensor', 'dp')
- grad_out_weight: float32 [1024, 1024], P('tensor', 'dp')
- grad_out_bias: float32 [16, 64], P('tensor', 'dp')
- grad_first_gain: float32 [16, 64], P('tensor', 'dp')
- grad_first_shift: float32 [16, 64], P('tensor', 'dp')
- grad_up_weight: float32 [1024, 4096], P('dp', 'tensor')
- grad_up_bias: float32 [64, 64], P('tensor', 'dp')
- grad_down_weight: float32 [4096, 1024], P('tensor', 'dp')
- grad_down_bias: float32 [16, 64], P('tensor', 'dp')
- grad_second_gain: float32 [16, 64], P('tensor', 'dp')
- grad_second_shift: float32 [16, 64], P('tensor', 'dp')
The draws below stay inside these ranges and needn't reach their ends.
Inputs may be any that keep to these rules, and one draw needn't show every extreme that they name: `valid_mask`: token t counts whenever t is a multiple of 64. `segments`: document numbers never fall along the tokens; a document has 1 to 512 tokens, and one has exactly 512.
All inputs are finite; a program needn't handle non-finite values.
Results may differ from the reference program's by a relative error of at most 0.015.
Values may be sent and summed in bfloat16 or wider, within the bound.
No kernel may reach another device: no remote copies, remote signals or barrier semaphores. Data moves between devices by JAX's collectives and lax.ppermute only.
A program may use at most 192 MiB of HBM per device.

```python
import math
import jax
import jax.numpy as jnp
import numpy as np
from jax import lax

D = 1024
HEADS = 16
HD = 64
FF = 4096
SEQ = 512
TOK_DEV = 512
TOKENS = 16384
N_TENSOR = 2


def draw_valid_mask(key, part):
    position = jnp.arange(TOKENS, dtype=jnp.int32)
    threshold = 300 + 600 * position // TOKENS
    dice_rolls = jax.random.randint(key, (TOKENS,), 0, 1000, dtype=jnp.int32)
    forced = position % 64 == 0
    return jnp.where((dice_rolls < threshold) | forced, 1, 0).astype(jnp.int32)


def shard_levels(key, extent, shards, low, top_value):
    gain, own = 1.0, jax.random.fold_in(key, 6)
    for dim, parts in shards:
        draws = jnp.exp(jax.random.uniform(jax.random.fold_in(own, dim), (parts,), jnp.float32, low / len(shards), top_value / len(shards)))
        gain = gain * jnp.repeat(draws, extent[dim] // parts).reshape([-1 if axis == dim else 1 for axis in range(len(extent))])
    return gain


def split_up(amount, total, limit, slope):
    portions = [(1 << 20) // math.isqrt(rank ** slope) + 1 for rank in range(2, amount + 1)]
    rest, holding = total - limit - (amount - 1), [1] * (amount - 1)
    while rest > 0:
        free = [i for i in range(amount - 1) if holding[i] < limit]
        pool, remaining = sum([portions[i] for i in free]), rest
        for i in free:
            extra = min(limit - holding[i], max(1, remaining * portions[i] // pool), rest)
            holding[i] = holding[i] + extra
            rest = rest - extra
    return np.array([limit] + holding)


def uneven(stream_key, number_of, total, most, lean):
    if number_of == 2:
        one = jax.random.randint(stream_key, (), max(1, total - most), min(most, total - 1) + 1)
        return jnp.stack([one, total - one])
    sizes = jnp.asarray(split_up(number_of, total, most, lean), jnp.int32)
    twos = (number_of - 1) // 2
    giver, taker = sizes[1:1 + 2 * twos:2], sizes[2:2 + 2 * twos:2]
    room = jnp.minimum(giver - 1, most - taker)
    passed = jax.random.randint(jax.random.fold_in(stream_key, 1), (twos,), 0, 1 << 20) % (room + 1)
    sizes = sizes.at[1:1 + 2 * twos:2].set(giver - passed).at[2:2 + 2 * twos:2].set(taker + passed)
    return sizes[jax.random.permutation(jax.random.fold_in(stream_key, 2), number_of)]


def gaussian(own_key, extent, scale, limit, shards=(), kind=jnp.bfloat16):
    gain = shard_levels(own_key, extent, shards, -0.22, 0.18) if shards else 1.0
    drawn = jax.random.normal(own_key, extent, jnp.float32) * scale * gain
    return jnp.minimum(jnp.maximum(drawn, -limit), limit).astype(kind)


def setup_inputs(seed: int = 0) -> dict:
    keys = jax.random.split(jax.random.key(seed), 18)
    return {
        "tokens": gaussian(keys[0], (TOKENS, D), 1.0, 6.0, ((0, 32),)),
        "teacher": gaussian(keys[1], (TOKENS, D), 1.0, 6.0, ((0, 32),), jnp.float32),
        "valid_mask": draw_valid_mask(jax.random.fold_in(keys[17], 71), 0),
        "segments": jnp.searchsorted(jnp.cumsum(uneven(keys[3], TOKENS // (SEQ // 8), TOKENS, SEQ, 2)), jnp.arange(TOKENS), side="right").astype(jnp.int32),
        "loss_scale": jnp.clip(jnp.exp(jax.random.uniform(keys[4], (), jnp.float32, math.log(8388608), math.log(33554432))), 8388608, 33554432),
        "qkv_weight": gaussian(keys[5], (3, D, D), D ** -0.5, 0.1875, ((1, 16), (2, 2))),
        "qv_bias": gaussian(keys[6], (2, HEADS, HD), 0.5, 3.0, ((1, 2), (2, 16))),
        "out_weight": gaussian(keys[7], (D, D), (D // 16) ** -0.5, 0.75, ((0, 2), (1, 16))),
        "out_bias": gaussian(keys[8], (HEADS, HD), 0.3, 2.0, ((0, 2), (1, 16))),
        "first_gain": jnp.clip(1.0 + 0.15 * jax.random.normal(keys[9], (HEADS, HD), jnp.float32), 0.25, 1.75).astype(jnp.bfloat16),
        "first_shift": gaussian(keys[10], (HEADS, HD), 0.3, 2.0, ((0, 2), (1, 16))),
        "up_weight": gaussian(keys[11], (D, FF), D ** -0.5, 0.1875, ((0, 16), (1, 2))),
        "up_bias": gaussian(keys[12], (FF // HD, HD), 0.5, 3.0, ((0, 2), (1, 16))),
        "down_weight": gaussian(keys[13], (FF, D), FF ** -0.5, 0.09375, ((0, 2), (1, 16))),
        "down_bias": gaussian(keys[14], (HEADS, HD), 0.3, 2.0, ((0, 2), (1, 16))),
        "second_gain": jnp.clip(1.0 + 0.15 * jax.random.normal(keys[15], (HEADS, HD), jnp.float32), 0.25, 1.75).astype(jnp.bfloat16),
        "second_shift": gaussian(keys[16], (HEADS, HD), 0.3, 2.0, ((0, 2), (1, 16))),
    }


@jax.custom_vjp
def low(v):
    return lax.optimization_barrier(v.astype(jnp.bfloat16)).astype(jnp.float32)

@jax.custom_vjp
def low_back(v):
    return v

def low_keep(v):
    return (low(v), None)

def low_pass(kept, grad):
    return (grad,)

def back_keep(v):
    return (v, None)

def back_low(kept, grad):
    return (low(grad),)
low.defvjp(low_keep, low_pass)
low_back.defvjp(back_keep, back_low)
layer_eps = 1e-06
masked_score = -1e+30

def product(left, right):
    return jnp.dot(left, right, precision=lax.Precision.HIGHEST)

def layer_norm(inputs, gain_vec, shift_vec):
    center = inputs - lax.optimization_barrier(jnp.mean(inputs, axis=-1, keepdims=True))
    inv_scale = lax.rsqrt(lax.optimization_barrier(jnp.mean(center * center, axis=-1, keepdims=True)) + layer_eps)
    return center * inv_scale * gain_vec + shift_vec

def attend(pieces):
    queries, key_rows, values, segment_ids = pieces
    scores = jnp.einsum('qhd,khd->hqk', queries, key_rows, precision=lax.Precision.HIGHEST) * 0.125
    scores = low_back(scores)
    same_doc = segment_ids[:, None] == segment_ids[None, :]
    scores = jnp.where(same_doc[None, :, :], scores, masked_score)
    prob_rows = low(jax.nn.softmax(scores, axis=-1))
    return jnp.einsum('hqk,khd->qhd', prob_rows, values, precision=lax.Precision.HIGHEST)

def forward(row_block, params, segment_ids):
    qkv_w, qv_b, out_w, out_b, gain_one, shift_one, up_w, up_b, down_w, down_b, gain_two, shift_two = params
    row_count = row_block.shape[0]
    seq_count = row_count // SEQ
    queries = low_back(low(product(row_block, qkv_w[0]) + qv_b[0]))
    key_rows = low_back(low(product(row_block, qkv_w[1])))
    values = low_back(low(product(row_block, qkv_w[2]) + qv_b[1]))

    def split_heads(block_rows):
        return block_rows.reshape(seq_count, SEQ, HEADS, HD)
    mixed_rows = lax.map(jax.checkpoint(attend), (split_heads(queries), split_heads(key_rows), split_heads(values), segment_ids.reshape(seq_count, SEQ)))
    context = low_back(low(mixed_rows.reshape(row_count, D)))
    attn_out = low_back(product(context, out_w)) + out_b
    first_norm = layer_norm(row_block + attn_out, gain_one, shift_one)
    hidden_pre = low_back(product(low(first_norm), up_w) + up_b)
    hidden_act = low(jax.nn.gelu(hidden_pre, approximate=False))
    ffn_out = low_back(product(hidden_act, down_w)) + down_b
    return layer_norm(first_norm + ffn_out, gain_two, shift_two)

def reference(tokens, teacher, valid_mask, segments, loss_scale, qkv_weight, qv_bias, out_weight, out_bias, first_gain, first_shift, up_weight, up_bias, down_weight, down_bias, second_gain, second_shift):
    flat = jnp.float32
    params = (qkv_weight.astype(flat), qv_bias.astype(flat).reshape(2, D), out_weight.astype(flat), out_bias.astype(flat).reshape(D), first_gain.astype(flat).reshape(D), first_shift.astype(flat).reshape(D), up_weight.astype(flat), up_bias.astype(flat).reshape(FF), down_weight.astype(flat), down_bias.astype(flat).reshape(D), second_gain.astype(flat).reshape(D), second_shift.astype(flat).reshape(D))
    keep_all = valid_mask.astype(flat)
    count_all = jnp.sum(keep_all)
    norm_scale = count_all * D
    block_rows = TOK_DEV * N_TENSOR
    block_count = TOKENS // block_rows
    pieces = (tokens.astype(flat).reshape(block_count, block_rows, D), teacher.astype(flat).reshape(block_count, block_rows, D), keep_all.reshape(block_count, block_rows), segments.reshape(block_count, block_rows))
    zero_grads = jax.tree.map(jnp.zeros_like, params)

    def scan_step(carry, piece_set):
        loss_sum, gradients = carry
        row_block, targets, keep_rows, segment_ids = piece_set

        def run_block(inputs, weights):
            return forward(inputs, weights, segment_ids)
        out_rows, pullback = jax.vjp(run_block, row_block, params)
        errors = out_rows - targets
        loss_sum = loss_sum + jnp.sum(keep_rows * lax.optimization_barrier(jnp.sum(errors * errors, axis=-1)))
        seed_grad = 2.0 * loss_scale / norm_scale * keep_rows[:, None] * errors
        d_rows, d_params = pullback(seed_grad)
        gradients = jax.tree.map(jnp.add, gradients, d_params)
        return ((loss_sum, gradients), (out_rows.astype(jnp.bfloat16), d_rows))
    (loss_sum, gradients), (out_rows, d_rows) = lax.scan(scan_step, (jnp.zeros((), flat), zero_grads), pieces)
    return (out_rows.reshape(TOKENS, D), loss_sum / norm_scale, d_rows.reshape(TOKENS, D), gradients[0], gradients[1].reshape(2, HEADS, HD), gradients[2], gradients[3].reshape(HEADS, HD), gradients[4].reshape(HEADS, HD), gradients[5].reshape(HEADS, HD), gradients[6], gradients[7].reshape(FF // HD, HD), gradients[8], gradients[9].reshape(HEADS, HD), gradients[10].reshape(HEADS, HD), gradients[11].reshape(HEADS, HD))
```

```python
import functools

import jax
import jax.numpy as jnp
from jax import lax
from jax.experimental import pallas as pl
from jax.experimental.pallas import tpu as pltpu
from jax.sharding import PartitionSpec as P

HD = 64
SEQ = 512
EPS = 1e-06
MASKED = -1e30
F32 = jnp.float32
BF16 = jnp.bfloat16
ANY = pl.BlockSpec(memory_space=pl.ANY)
SMEM = pl.BlockSpec(memory_space=pltpu.SMEM)
VMEM = pl.BlockSpec(memory_space=pltpu.VMEM)


def cost(flops, nbytes, trans=0):
    return pl.CostEstimate(flops=int(flops), bytes_accessed=int(nbytes), transcendentals=int(trans))


class Grid:
    def __init__(self, dp, tensor):
        self.dp, self.T, self.Z = dp, tensor, dp // 4
        assert dp == self.Z * 4
        Z = self.Z
        self.cycle = [0] + list(range(1, Z, 2)) + list(range(2, Z, 2))[::-1]
        self.place = [self.cycle.index(z) for z in range(Z)]
        after = {self.cycle[i]: self.cycle[(i + 1) % Z] for i in range(Z)}
        cells = [(z, x, c) for z in range(Z) for x in range(2) for c in range(2)]
        self.to_z = [(self.rank(z, x, c), self.rank(after[z], x, c)) for z, x, c in cells]
        self.to_x = [(self.rank(z, x, c), self.rank(z, 1 - x, c)) for z, x, c in cells]
        self.to_c = [(self.rank(z, x, c), self.rank(z, x, 1 - c)) for z, x, c in cells]
        self.to_t = [(t, (t + 1) % tensor) for t in range(tensor)]

    @staticmethod
    def rank(z, x, c):
        return z * 4 + x * 2 + c

    def here(self):
        d = lax.axis_index("dp")
        self.z, self.x, self.c, self.t = d // 4, (d // 2) % 2, d % 2, lax.axis_index("tensor")
        place = jnp.array(self.place, jnp.int32)[self.z]
        cycle = jnp.array(self.cycle, jnp.int32)
        self.back = cycle[(place - jnp.arange(self.Z)) % self.Z]
        self.slot = (place - jnp.array(self.place, jnp.int32)) % self.Z
        self.info = jnp.concatenate(
            [jnp.stack([self.t, self.x, self.c, self.z]).astype(jnp.int32), self.back.astype(jnp.int32)]
        )

    def zs(self, a):
        return lax.ppermute(a, "dp", self.to_z)

    def xs(self, a):
        return lax.ppermute(a, "dp", self.to_x)

    def cs(self, a):
        return lax.ppermute(a, "dp", self.to_c)

    def ts(self, a):
        return lax.ppermute(a, "tensor", self.to_t)

    def gather(self, own):
        ring = [own]
        for _ in range(self.Z - 1):
            ring.append(self.zs(ring[-1]))
        line = jnp.stack(ring)
        half = self.Z // 2
        chips = {(0, 0): [line], (0, 1): [self.xs(line)]}
        rows = line
        for rt in range(1, self.T):
            rows = self.ts(rows)
            chips[rt, 0] = [rows]
            if self.T == 2:
                chips[rt, 1] = [self.xs(rows[:half]), self.ts(chips[0, 1][0][half:])]
            else:
                chips[rt, 1] = [self.xs(rows)]
        blocks = {}
        for (rt, rx), arrays in chips.items():
            blocks[rt, rx, 0] = arrays
            blocks[rt, rx, 1] = [self.cs(a) for a in arrays]
        return blocks

    def gather_small(self, own):
        a = jnp.stack([own, self.cs(own)])
        a = jnp.stack([a, self.xs(a)])
        rows, parts = a, [a]
        for _ in range(1, self.T):
            rows = self.ts(rows)
            parts.append(rows)
        a = jnp.stack(parts)
        rows, parts = a, [a]
        for _ in range(1, self.Z):
            rows = self.zs(rows)
            parts.append(rows)
        a = jnp.stack(parts)
        two = jnp.arange(2)
        rt = ((self.t - jnp.arange(self.T)) % self.T)[:, None, None, None]
        rz = self.slot[None, :, None, None]
        rx = (two ^ self.x)[None, None, :, None]
        rc = (two ^ self.c)[None, None, None, :]
        index = ((rz * self.T + rt) * 2 + rx) * 2 + rc
        flat = a.reshape((-1,) + own.shape)
        return jnp.take(flat, index.reshape(-1), axis=0, mode="clip").reshape((self.T, self.dp) + own.shape)

    def scatter_line(self, own, cast):
        held = None
        for step in range(1, self.Z):
            block = lax.dynamic_index_in_dim(own, self.back[step], 0, keepdims=False)
            if held is not None:
                block = block + held.astype(F32)
            held = self.zs(block.astype(cast))
        return lax.dynamic_index_in_dim(own, self.z, 0, keepdims=False) + held.astype(F32)

    def scatter(self, g):
        half = self.Z // 2

        def add(a, b):
            return (a.astype(F32) + b.astype(F32)).astype(BF16)

        if self.T == 2:
            far = g[1, 1]
            from_x = self.xs(far[:half])
            from_t = self.ts(far[half:])
            x_near, t_near = g[0, 1], g[1, 0]
            x_low = self.xs(x_near[:half])
            t_high = self.ts(t_near[half:])
            x_high = self.xs(add(x_near[half:], from_t))
            t_low = self.ts(add(t_near[:half], from_x))
            own = g[0, 0].astype(F32) + jnp.concatenate([x_low, x_high]).astype(F32)
            own = own + jnp.concatenate([t_low, t_high]).astype(F32)
        else:
            cols = g[:, 0].astype(F32) + self.xs(g[:, 1]).astype(F32)
            held = None
            for step in range(1, self.T):
                block = cols[(self.T - step) % self.T]
                if held is not None:
                    block = block + held.astype(F32)
                held = self.ts(block.astype(BF16))
            own = cols[0] + held.astype(F32)
        return self.scatter_line(own, BF16)

    def scatter_small(self, v):
        v = v.reshape((self.T, self.Z, 2, 2) + v.shape[2:])

        def pick(a, i, axis):
            return lax.dynamic_index_in_dim(a, i, axis, keepdims=False)

        v = pick(v, self.c, 3) + self.cs(pick(v, 1 - self.c, 3))
        v = pick(v, self.x, 2) + self.xs(pick(v, 1 - self.x, 2))
        held = None
        for step in range(1, self.T):
            block = pick(v, (self.t - step) % self.T, 0)
            held = self.ts(block if held is None else block + held)
        v = pick(v, self.t, 0) + held
        return self.scatter_line(v, F32)


def fetch_blocks(info, refs, shapes, keys, out, sem, R):
    copies = []
    for (rt, rx, rc), ref, first, count in keys:
        T = shapes[0]
        t = lax.rem(info[0] - rt + T, T)
        for i in range(count):
            z = info[4 + first + i]
            row = (z * 4 + (info[1] ^ rx) * 2 + (info[2] ^ rc)) * R
            copies.append(
                pltpu.make_async_copy(refs[ref].at[i], out.at[t, pl.ds(pl.multiple_of(row, R), R), :], sem)
            )
    for copy in copies:
        copy.start()
    return copies


def flatten_blocks(blocks):
    arrays, keys = [], []
    for key, parts in blocks.items():
        first = 0
        for a in parts:
            keys.append((key, len(arrays), first, a.shape[0]))
            arrays.append(a)
            first += a.shape[0]
    return arrays, keys


def whole(grid, blocks, depth):
    arrays, keys = flatten_blocks(blocks)
    _, R, n = arrays[0].shape

    def kernel(info, *rest):
        *refs, out, sem = rest
        for copy in fetch_blocks(info, refs, (grid.T,), keys, out, sem, R):
            copy.wait()

    return pl.pallas_call(
        kernel,
        out_shape=jax.ShapeDtypeStruct((grid.T, depth, n), BF16),
        in_specs=[SMEM] + [ANY] * len(arrays),
        out_specs=VMEM,
        scratch_shapes=[pltpu.SemaphoreType.DMA],
        cost_estimate=cost(0, 4 * grid.T * depth * n),
        compiler_params=pltpu.CompilerParams(vmem_limit_bytes=20 << 20),
        name="whole",
    )(grid.info, *arrays)


def weight_grad(grid, lefts, rights, core, received=None):
    T, Z = grid.T, grid.Z
    D, S = lefts[0].shape
    R = D // grid.dp
    tile = D // T
    spans, first = [], 0
    for which, b in rights:
        count = b.shape[1] // T // tile
        spans.append((which, first, count))
        first += count
    steps = first

    def kernel(info, *rest):
        left_refs = rest[: len(lefts)]
        right_refs = rest[len(lefts) : len(lefts) + len(rights)]
        rest = rest[len(lefts) + len(rights) :]
        if received is not None:
            got, out, rows = rest
        else:
            out, rows = rest
        rt, j = pl.program_id(0), pl.program_id(1)

        @pl.when((rt == 0) & (j == 0))
        def _():
            for a in range(len(lefts)):
                for rx in range(2):
                    for z in range(Z):
                        at = (z * 4 + (info[1] ^ rx) * 2 + (info[2] ^ core)) * R
                        rows[a, pl.ds((rx * Z + z) * R, R), :] = left_refs[a][pl.ds(pl.multiple_of(at, R), R), :]

        for (which, lo, count), right in zip(spans, right_refs):

            @pl.when((j >= lo) & (j < lo + count))
            def _(which=which, right=right):
                g = jnp.dot(rows[which], right[...], preferred_element_type=F32)
                g = g.reshape(out.shape)
                if received is not None:
                    g = g + got[...].astype(F32)
                out[...] = g.astype(BF16)

    def right_map(lo, count):
        def index(rt, j, info):
            t = lax.rem(info[0] - rt + T, T)
            return (0, t * count + jnp.clip(j - lo, 0, count - 1))

        return index

    block = pl.BlockSpec((1, 2, Z, R, tile), lambda rt, j, info: (rt, 0, 0, 0, j))
    in_specs = [pl.BlockSpec((D, S), lambda rt, j, info: (0, 0)) for _ in lefts]
    in_specs += [pl.BlockSpec((S, tile), right_map(lo, count)) for _, lo, count in spans]
    operands = list(lefts) + [b for _, b in rights]
    if received is not None:
        in_specs.append(block)
        operands.append(received)
    width = steps * tile
    return pl.pallas_call(
        kernel,
        out_shape=jax.ShapeDtypeStruct((T, 2, Z, R, width), BF16),
        grid_spec=pltpu.PrefetchScalarGridSpec(
            num_scalar_prefetch=1,
            grid=(T, steps),
            in_specs=in_specs,
            out_specs=block,
            scratch_shapes=[pltpu.VMEM((len(lefts), D // 2, S), BF16)],
        ),
        cost_estimate=cost(D * S * width * T, 4 * S * width * T + 2 * D * width * T),
        compiler_params=pltpu.CompilerParams(vmem_limit_bytes=24 << 20),
        name="weight_grad",
    )(grid.info, *operands)


def attention_forward(q, k, v, seg_col, seg_row):
    S, D = q.shape
    pairs = D // (2 * HD)

    def kernel(q, k, v, col, row, ctx, probs, bias):
        @pl.when(pl.program_id(0) == 0)
        def _():
            bias[...] = jnp.where(col[...] == row[...], 0.0, MASKED)

        lane = lax.broadcasted_iota(jnp.int32, (S, 2 * HD), 1) < HD
        query = q[...] * jnp.asarray(0.125, BF16)
        zero = jnp.zeros_like(query)
        outs = []
        for h in range(2):
            mine = jnp.where(lane == (h == 0), query, zero)
            s = lax.dot_general(mine, k[...], (((1,), (1,)), ((), ())), preferred_element_type=F32) + bias[...]
            e = jnp.exp(s - jnp.max(s, axis=-1, keepdims=True))
            p = (e * (1.0 / jnp.sum(e, axis=-1, keepdims=True))).astype(BF16)
            probs[h] = p
            outs.append(jnp.dot(p, v[...], preferred_element_type=F32))
        ctx[...] = jnp.where(lane, outs[0], outs[1]).astype(BF16)

    rows = pl.BlockSpec((S, 2 * HD), lambda i: (0, i))
    return pl.pallas_call(
        kernel,
        grid=(pairs,),
        out_shape=(jax.ShapeDtypeStruct((S, D), BF16), jax.ShapeDtypeStruct((2 * pairs, S, S), BF16)),
        in_specs=[rows, rows, rows, pl.BlockSpec((S, 1), lambda i: (0, 0)), pl.BlockSpec((1, S), lambda i: (0, 0))],
        out_specs=(rows, pl.BlockSpec((2, S, S), lambda i: (i, 0, 0))),
        scratch_shapes=[pltpu.VMEM((S, S), F32)],
        cost_estimate=cost(16 * S * S * D, 8 * S * D + 4 * pairs * S * S, 2 * pairs * S * S),
        compiler_params=pltpu.CompilerParams(vmem_limit_bytes=32 << 20),
        name="attention_forward",
    )(q, k, v, seg_col, seg_row)


def attention_backward(q, k, v, ctx, d_ctx, probs):
    S, D = q.shape
    pairs = D // (2 * HD)
    nt = (((1,), (1,)), ((), ()))
    tn = (((0,), (0,)), ((), ()))

    def kernel(q, k, v, ctx, d_ctx, probs, dq, dk, dv, sums):
        lane = lax.broadcasted_iota(jnp.int32, (S, 2 * HD), 1) < HD
        grad = d_ctx[...]
        both = grad.astype(F32) * ctx[...].astype(F32)
        dqs, dks, dvs = [], [], []
        for h in range(2):
            mask = lane == (h == 0)
            inner = jnp.sum(jnp.where(mask, both, 0.0), axis=-1, keepdims=True)
            mine = jnp.where(mask, grad, jnp.zeros_like(grad))
            d_prob = lax.dot_general(mine, v[...], nt, preferred_element_type=F32)
            p = probs[h]
            ds = (p.astype(F32) * (d_prob - inner)).astype(BF16)
            dvs.append(lax.dot_general(p, grad, tn, preferred_element_type=F32))
            dqs.append(jnp.dot(ds, k[...], preferred_element_type=F32))
            dks.append(lax.dot_general(ds, q[...], tn, preferred_element_type=F32))
        a = (jnp.where(lane, dqs[0], dqs[1]) * 0.125).astype(BF16)
        b = jnp.where(lane, dvs[0], dvs[1]).astype(BF16)
        dq[...] = a
        dk[...] = (jnp.where(lane, dks[0], dks[1]) * 0.125).astype(BF16)
        dv[...] = b
        total_a = jnp.sum(a.astype(F32), axis=0, keepdims=True)
        total_b = jnp.sum(b.astype(F32), axis=0, keepdims=True)
        sums[...] = jnp.concatenate([total_a, total_b, jnp.zeros((6, 2 * HD), F32)], axis=0)

    rows = pl.BlockSpec((S, 2 * HD), lambda i: (0, i))
    out = jax.ShapeDtypeStruct((S, D), BF16)
    return pl.pallas_call(
        kernel,
        grid=(pairs,),
        out_shape=(out, out, out, jax.ShapeDtypeStruct((8, D), F32)),
        in_specs=[rows] * 5 + [pl.BlockSpec((2, S, S), lambda i: (i, 0, 0))],
        out_specs=(rows, rows, rows, pl.BlockSpec((8, 2 * HD), lambda i: (0, i))),
        cost_estimate=cost(32 * S * S * D, 16 * S * D + 4 * pairs * S * S),
        compiler_params=pltpu.CompilerParams(vmem_limit_bytes=32 << 20),
        name="attention_backward",
    )(q, k, v, ctx, d_ctx, probs)


def norm_parts(rows):
    center = rows - jnp.mean(rows, axis=-1, keepdims=True)
    inv = lax.rsqrt(jnp.mean(center * center, axis=-1, keepdims=True) + EPS)
    return center * inv, inv


def norm_back(grad, gain, n, inv):
    d = grad * gain
    d = d - jnp.mean(d, axis=-1, keepdims=True) - n * jnp.mean(d * n, axis=-1, keepdims=True)
    return d * inv


def body(
    sizes,
    tokens,
    teacher,
    valid_mask,
    segments,
    loss_scale,
    qkv_weight,
    qv_bias,
    out_weight,
    out_bias,
    first_gain,
    first_shift,
    up_weight,
    up_bias,
    down_weight,
    down_bias,
    second_gain,
    second_shift,
):
    grid = Grid(*sizes)
    grid.here()
    T, dp = grid.T, grid.dp
    S, D = tokens.shape
    assert S == SEQ
    FF = up_weight.shape[1] * T
    tile = D // T
    keep = valid_mask.astype(F32)

    small = [out_bias, first_gain, first_shift, down_bias, second_gain, second_shift]
    h, w = out_bias.shape
    hu = up_bias.shape[0]
    flat = jnp.concatenate([v.astype(F32).reshape(-1) for v in small + [qv_bias, up_bias]])
    n_own = flat.shape[0]
    k_rows = (n_own + 1 + 127) // 128
    flat = jnp.concatenate([flat, jnp.sum(keep)[None], jnp.zeros((k_rows * 128 - n_own - 1,), F32)])
    table = grid.gather_small(flat.reshape(k_rows, 128)).reshape(T, dp, k_rows * 128)
    eight = table[:, :, : 8 * h * w].reshape(T, dp, 8, h, w).transpose(2, 0, 3, 1, 4).reshape(8, D)
    up_b = table[:, :, 8 * h * w : n_own].reshape(T, dp, hu, w).transpose(0, 2, 1, 3).reshape(FF)
    count_all = jnp.sum(table[:, :, n_own])

    first_own = jnp.concatenate([qkv_weight[0], qkv_weight[1], qkv_weight[2], out_weight.T], axis=1)
    blocks_first = grid.gather(first_own)
    blocks_up = grid.gather(up_weight)
    blocks_down = grid.gather(down_weight.T)

    mine = lax.dynamic_slice_in_dim(segments, grid.t * S, S)
    w_first = whole(grid, blocks_first, D)

    def product(a, weights):
        return jnp.einsum("sd,tdc->stc", a, weights, preferred_element_type=F32).reshape(a.shape[0], -1)

    def product_back(a, weights):
        return jnp.einsum("stc,tdc->sd", a.reshape(a.shape[0], T, -1), weights, preferred_element_type=F32)

    wq, wk, wv, wo = (w_first[:, :, i * tile : (i + 1) * tile] for i in range(4))
    q = (product(tokens, wq) + eight[6]).astype(BF16)
    k = product(tokens, wk).astype(BF16)
    v = (product(tokens, wv) + eight[7]).astype(BF16)
    ctx, probs = attention_forward(q, k, v, mine[:, None], mine[None, :])
    n1, inv1 = norm_parts(tokens.astype(F32) + (product_back(ctx, wo) + eight[0]))
    first_norm = n1 * eight[1] + eight[2]
    first_low = first_norm.astype(BF16)

    w_up = whole(grid, blocks_up, D)
    pre = product(first_low, w_up) + up_b
    cdf = 0.5 * (1.0 + lax.erf(pre * (2.0**-0.5)))
    act = (pre * cdf).astype(BF16)
    slope = (cdf + pre * (jnp.exp(-0.5 * pre * pre) * 0.3989422804014327)).astype(BF16)

    w_down = whole(grid, blocks_down, D)
    n2, inv2 = norm_parts(first_norm + (product_back(act, w_down) + eight[3]))
    out_full = n2 * eight[4] + eight[5]
    errors = out_full - teacher
    norm_scale = count_all * D
    loss_part = jnp.sum(keep * jnp.sum(errors * errors, axis=-1))
    grad_out = 2.0 * loss_scale / norm_scale * keep[:, None] * errors
    d_two = norm_back(grad_out, eight[4], n2, inv2)
    d_ffn = d_two.astype(BF16)

    def scattered(lefts, rights):
        theirs = weight_grad(grid, lefts, rights, 1)
        ours = weight_grad(grid, lefts, rights, 0, grid.cs(theirs))
        return grid.scatter(ours)

    g_down = scattered([d_ffn.T], [(0, act)])
    d_hidden = (product(d_ffn, w_down) * slope.astype(F32)).astype(BF16)
    d_first = d_two + product_back(d_hidden, w_up)
    d_one = norm_back(d_first, eight[1], n1, inv1)
    d_attn = d_one.astype(BF16)
    g_up = scattered([first_low.T, d_attn.T], [(0, d_hidden), (1, ctx)])
    d_ctx = product(d_attn, wo).astype(BF16)
    dq, dk, dv, sums = attention_backward(q, k, v, ctx, d_ctx, probs)
    g_qkv = scattered([tokens.T], [(0, dq), (0, dk), (0, dv)])

    def total(a):
        return jnp.sum(a, axis=0)

    vec = jnp.stack(
        [total(d_one), total(d_first * n1), total(d_first), total(d_two), total(grad_out * n2), total(grad_out), sums[0], sums[1]]
    )
    vec = vec.reshape(8, T, h, dp, w).transpose(1, 3, 0, 2, 4).reshape(T, dp, 8 * h * w)
    vec_up = total(d_hidden.astype(F32)).reshape(T, hu, dp, w).transpose(0, 2, 1, 3).reshape(T, dp, hu * w)
    rest = jnp.zeros((T, dp, k_rows * 128 - n_own - 1), F32)
    vec = jnp.concatenate([vec, vec_up, jnp.full((T, dp, 1), loss_part), rest], axis=2)
    vec = grid.scatter_small(vec.reshape(T, dp, k_rows, 128)).reshape(-1)
    g8 = vec[: 8 * h * w].reshape(8, h, w)
    loss_value = vec[n_own] / norm_scale

    row_terms = product_back(dq, wq) + product_back(dk, wk) + product_back(dv, wv)
    grad_tokens = d_one + row_terms
    up_cols = FF // T
    R = D // dp
    return (
        out_full.astype(BF16),
        loss_value,
        grad_tokens,
        g_qkv.reshape(R, 3, tile).transpose(1, 0, 2),
        g8[6:8],
        g_up[:, up_cols:].T,
        g8[0],
        g8[1],
        g8[2],
        g_up[:, :up_cols],
        vec[8 * h * w : n_own].reshape(hu, w),
        g_down.T,
        g8[3],
        g8[4],
        g8[5],
    )


def solution(mesh):
    vector = P("tensor", "dp")
    rows = P(("dp", "tensor"), None)
    qkv, qv, cols = P(None, "dp", "tensor"), P(None, "tensor", "dp"), P("dp", "tensor")
    return jax.shard_map(
        functools.partial(body, (mesh.shape["dp"], mesh.shape["tensor"])),
        mesh=mesh,
        in_specs=(
            rows, rows, P(("dp", "tensor")), P("dp"), P(), qkv, qv, vector, vector, vector, vector, cols,
            vector, vector, vector, vector, vector,
        ),
        out_specs=(
            rows, P(), rows, qkv, qv, vector, vector, vector, vector, cols, vector, vector, vector, vector, vector,
        ),
        check_vma=False,
    )
```

```python
import functools

import jax
import jax.numpy as jnp
from jax import lax
from jax.experimental import pallas as pl
from jax.experimental.pallas import tpu as pltpu
from jax.sharding import PartitionSpec as P

HD = 64
SEQ = 512
EPS = 1e-06
MASKED = -1e30
F32 = jnp.float32
BF16 = jnp.bfloat16
ANY = pl.BlockSpec(memory_space=pl.ANY)
NT = (((1,), (1,)), ((), ()))
TN = (((0,), (0,)), ((), ()))


def cost(flops, nbytes, trans=0):
    return pl.CostEstimate(flops=int(flops), bytes_accessed=int(nbytes), transcendentals=int(trans))


def nt_dot(a, b):
    return lax.dot_general(a, b, NT, preferred_element_type=F32)


def dot(a, b):
    return jnp.dot(a, b, preferred_element_type=F32)


class Pieces:
    def __init__(self, parts):
        self.arrays = [a for a, _ in parts]
        self.places = [p for _, p in parts]


class Grid:
    def __init__(self, dp, tensor):
        self.dp, self.T, self.Z = dp, tensor, dp // 4
        assert dp == self.Z * 4
        Z = self.Z
        self.cycle = [0] + list(range(1, Z, 2)) + list(range(2, Z, 2))[::-1]
        self.place = [self.cycle.index(z) for z in range(Z)]
        after = {self.cycle[i]: self.cycle[(i + 1) % Z] for i in range(Z)}
        cells = [(z, x, c) for z in range(Z) for x in range(2) for c in range(2)]
        self.to_z = [(self.rank(z, x, c), self.rank(after[z], x, c)) for z, x, c in cells]
        self.to_x = [(self.rank(z, x, c), self.rank(z, 1 - x, c)) for z, x, c in cells]
        self.to_c = [(self.rank(z, x, c), self.rank(z, x, 1 - c)) for z, x, c in cells]
        self.to_t = [(t, (t + 1) % tensor) for t in range(tensor)]
        self.square = tensor == 2 and Z == 4

    @staticmethod
    def rank(z, x, c):
        return z * 4 + x * 2 + c

    def here(self):
        d = lax.axis_index("dp")
        self.d, self.z, self.x, self.c, self.t = d, d // 4, (d // 2) % 2, d % 2, lax.axis_index("tensor")
        back = []
        for k in range(self.Z):
            options = [self.cycle[(p - k) % self.Z] for p in self.place]
            back.append(sum(jnp.where(self.z == z, o, 0) for z, o in enumerate(options)))
        self.back = back
        self.info = jnp.stack([v.astype(jnp.int32) for v in [self.t, self.x, self.c, self.z] + back])

    def zs(self, a):
        return lax.ppermute(a, "dp", self.to_z)

    def xs(self, a):
        return lax.ppermute(a, "dp", self.to_x)

    def cs(self, a):
        return lax.ppermute(a, "dp", self.to_c)

    def ts(self, a):
        return lax.ppermute(a, "tensor", self.to_t)

    def both_cores(self, parts):
        twins = [(self.cs(a), [(t, x, 1, k) for t, x, _, k in places]) for a, places in parts]
        return Pieces(parts + twins)

    def gather_general(self, own):
        ring = [own]
        for _ in range(self.Z - 1):
            ring.append(self.zs(ring[-1]))
        line, slots = jnp.stack(ring), range(self.Z)
        parts = [(line, [(0, 0, 0, k) for k in slots]), (self.xs(line), [(0, 1, 0, k) for k in slots])]
        rows = line
        for rt in range(1, self.T):
            rows = self.ts(rows)
            parts.append((rows, [(rt, 0, 0, k) for k in slots]))
            parts.append((self.xs(rows), [(rt, 1, 0, k) for k in slots]))
        return self.both_cores(parts)

    def gather(self, first, middle, last):
        if not self.square:
            return tuple(self.gather_general(a) for a in (first, middle, last))
        half = last.shape[0] // 2
        a0, b0, d = first[None], middle, last
        d_x, d_t = self.xs(d), self.ts(d)
        a1 = self.zs(a0)
        a0_x, a0_t = self.xs(a0), self.ts(a0)
        d_far = [self.xs(d_t[:half]), self.ts(d_x[half:])]
        a2 = self.zs(a1)
        a1_x, a1_t = self.xs(a1), self.ts(a1)
        plane = jnp.stack([d, d_x, d_t, jnp.concatenate(d_far)])
        a3 = self.zs(a2)
        b1 = self.zs(b0)
        a23 = jnp.concatenate([a2, a3])
        a23_x, a23_t = self.xs(a23), self.ts(a23)
        b2 = self.zs(b1)
        a_far = [self.xs(a0_t), self.xs(a1_t), self.ts(a23_x)]
        b3 = self.zs(b2)
        line = jnp.stack([b0, b1, b2, b3])
        p1 = self.zs(plane)
        b_x, b_t = self.xs(line), self.ts(line)
        p2 = self.zs(p1)
        b_far = [self.xs(b_t[:2]), self.ts(b_x[2:])]
        p3 = self.zs(p2)

        def at(t, x, *slots):
            return [(t, x, 0, k) for k in slots]

        a_parts = [
            (a0, at(0, 0, 0)), (a1, at(0, 0, 1)), (a23, at(0, 0, 2, 3)),
            (a0_x, at(0, 1, 0)), (a1_x, at(0, 1, 1)), (a23_x, at(0, 1, 2, 3)),
            (a0_t, at(1, 0, 0)), (a1_t, at(1, 0, 1)), (a23_t, at(1, 0, 2, 3)),
            (a_far[0], at(1, 1, 0)), (a_far[1], at(1, 1, 1)), (a_far[2], at(1, 1, 2, 3)),
        ]
        b_parts = [
            (line, at(0, 0, 0, 1, 2, 3)), (b_x, at(0, 1, 0, 1, 2, 3)), (b_t, at(1, 0, 0, 1, 2, 3)),
            (b_far[0], at(1, 1, 0, 1)), (b_far[1], at(1, 1, 2, 3)),
        ]
        d_parts = [
            (p, [(0, 0, 0, k), (0, 1, 0, k), (1, 0, 0, k), (1, 1, 0, k)]) for k, p in enumerate([plane, p1, p2, p3])
        ]
        return self.both_cores(a_parts), self.both_cores(b_parts), self.both_cores(d_parts)

    def total_small(self, v):
        v = v + self.cs(v)
        v = v + self.xs(v)
        held = v
        for _ in range(1, self.T):
            held = self.ts(held)
            v = v + held
        held = v
        for _ in range(1, self.Z):
            held = self.zs(held)
            v = v + held
        return v

    def scatter_line(self, own):
        held = None
        for step in range(1, self.Z):
            block = lax.dynamic_index_in_dim(own, self.back[step], 0, keepdims=False)
            if held is not None:
                block = block.astype(F32) + held.astype(F32)
            held = self.zs(block.astype(BF16))
        return lax.dynamic_index_in_dim(own, self.z, 0, keepdims=False).astype(F32) + held.astype(F32)

    def scatter_plane(self, own, x_near, t_near, far, cols):
        def add(a, b):
            return (a.astype(F32) + b.astype(F32)).astype(BF16)

        half = own.shape[0] // 2
        from_x = self.xs(far[:half])
        from_t = self.ts(far[half:])
        x_low = self.xs(x_near[:half])
        t_high = self.ts(t_near[half:])
        x_high = self.xs(add(x_near[half:], from_t))
        t_low = self.ts(add(t_near[:half], from_x))
        low = own[:half].astype(F32) + x_low.astype(F32) + t_low.astype(F32)
        high = own[half:].astype(F32) + x_high.astype(F32) + t_high.astype(F32)
        return jnp.concatenate([low, high])

    def scatter_general(self, g):
        rows = g[:, 0].astype(F32) + self.xs(g[:, 1]).astype(F32)
        held = None
        for step in range(1, self.T):
            block = rows[(self.T - step) % self.T]
            if held is not None:
                block = block + held.astype(F32)
            held = self.ts(block.astype(BF16))
        return rows[0] + held.astype(F32)

    def scatter(self, g):
        if self.square:
            own = self.scatter_plane(g[0, 0], g[0, 1], g[1, 0], g[1, 1], None)
        else:
            own = self.scatter_general(g)
        return self.scatter_line(own.astype(BF16))

    def scatter_line_first(self, g):
        g = self.scatter_line(g).astype(BF16)
        if self.square:
            return self.scatter_plane(g[0, 0], g[0, 1], g[1, 0], g[1, 1], None)
        return self.scatter_general(g)


class Weights:
    def __init__(self, grid, D, sources):
        self.T, self.D, self.R = grid.T, D, D // grid.dp
        self.sources = sources
        self.width = sum(s[2] for s in sources)
        seen = []
        for pieces, *_ in sources:
            if pieces not in seen:
                seen.append(pieces)
        self.operands = [a for pieces in seen for a in pieces.arrays]
        self.first = {id(p): sum(len(q.arrays) for q in seen[:i]) for i, p in enumerate(seen)}
        self.specs = [ANY] * len(self.operands)
        self.scratch = [pltpu.VMEM((self.T, D, self.width), BF16), pltpu.SemaphoreType.DMA((self.T,))]

    def copies(self, info, refs, w, sem, want):
        out = []
        for pieces, lo, count, to in self.sources:
            base = self.first[id(pieces)]
            for i, places in enumerate(pieces.places):
                for entry, (rt, rx, rc, k) in enumerate(places):
                    if rt != want:
                        continue
                    row = (info[4 + k] * 4 + (info[1] ^ rx) * 2 + (info[2] ^ rc)) * self.R
                    src = refs[base + i].at[entry, :, pl.ds(lo, count)]
                    dst = w.at[rt, pl.ds(pl.multiple_of(row, self.R), self.R), pl.ds(to, count)]
                    out.append(pltpu.make_async_copy(src, dst, sem.at[rt]))
        return out

    def start(self, info, refs, w, sem):
        for rt in range(self.T):
            for copy in self.copies(info, refs, w, sem, rt):
                copy.start()

    def wait(self, info, refs, w, sem, rt, first):
        for want in range(self.T):

            @pl.when((rt == want) & first)
            def _(want=want):
                for copy in self.copies(info, refs, w, sem, want):
                    copy.wait()


def part(info, rt, T):
    return lax.rem(info[0] - rt + T, T)


def call(kernel, name, grid, steps, info, operands, in_specs, outs, out_specs, scratch, estimate, mib=48):
    return pl.pallas_call(
        kernel,
        out_shape=outs,
        grid_spec=pltpu.PrefetchScalarGridSpec(
            num_scalar_prefetch=1, grid=steps, in_specs=in_specs, out_specs=out_specs, scratch_shapes=scratch
        ),
        cost_estimate=estimate,
        compiler_params=pltpu.CompilerParams(vmem_limit_bytes=mib << 20),
        name=name,
    )(info, *operands)


def shape(dims, dtype):
    return jax.ShapeDtypeStruct(dims, dtype)


def fixed(dims):
    return pl.BlockSpec(dims, lambda *_: (0,) * len(dims))


def project_qkv(grid, pieces, tokens, vec):
    T = grid.T
    S, D = tokens.shape
    tile = D // T
    ws = Weights(grid, D, [(pieces, 0, 3 * tile, 0)])

    def kernel(info, x, bias, *rest):
        refs, (q, k, v, w, sem) = rest[: len(ws.specs)], rest[len(ws.specs) :]
        rt = pl.program_id(0)

        @pl.when(rt == 0)
        def _():
            ws.start(info, refs, w, sem)

        ws.wait(info, refs, w, sem, rt, True)
        a, mine = x[...], w.at[rt]
        q[...] = (dot(a, mine[:, :tile]) + bias[6:7, :]).astype(BF16)
        k[...] = dot(a, mine[:, tile : 2 * tile]).astype(BF16)
        v[...] = (dot(a, mine[:, 2 * tile :]) + bias[7:8, :]).astype(BF16)

    cols = pl.BlockSpec((S, tile), lambda rt, info: (0, part(info, rt, T)))
    biases = pl.BlockSpec((vec.shape[0], tile), lambda rt, info: (0, part(info, rt, T)))
    out = shape((S, D), BF16)
    return call(
        kernel, "project_qkv", grid, (T,), grid.info, [tokens, vec] + ws.operands, [fixed((S, D)), biases] + ws.specs,
        (out, out, out), (cols, cols, cols), ws.scratch, cost(6 * S * D * D, 6 * D * D + 8 * S * D),
    )


def row_loop(S, rows, step, start):
    return lax.fori_loop(0, S // rows, lambda i, carry: step(pl.ds(pl.multiple_of(i * rows, rows), rows), carry), start)


def fold(a):
    return jnp.sum(a.reshape(a.shape[0] // 8, 8, a.shape[1]), axis=0)


def turn(src, dst):
    S = src.shape[0]

    def step(i, _):
        at = pl.ds(pl.multiple_of(i * 128, 128), 128)
        dst[:, at] = src[at, :].T
        return 0

    lax.fori_loop(0, S // 128, step, 0)


def normed(r):
    c = r - jnp.mean(r, axis=-1, keepdims=True)
    inv = lax.rsqrt(jnp.mean(c * c, axis=-1, keepdims=True) + EPS)
    return c * inv, inv


def normed_back(d, n, inv):
    return (d - jnp.mean(d, axis=-1, keepdims=True) - n * jnp.mean(d * n, axis=-1, keepdims=True)) * inv


ROWS = 32


def attend_out(grid, pieces, ctx, tokens, vec):
    T = grid.T
    S, D = tokens.shape
    tile = D // T
    ws = Weights(grid, D, [(pieces, 3 * tile, tile, 0)])

    def kernel(info, c, x, vecs, *rest):
        refs, (n1, inv1, low, low_t, w, sem, acc) = rest[: len(ws.specs)], rest[len(ws.specs) :]
        rt = pl.program_id(0)

        @pl.when(rt == 0)
        def _():
            ws.start(info, refs, w, sem)
            acc[...] = jnp.zeros_like(acc)

        ws.wait(info, refs, w, sem, rt, True)
        acc[...] += nt_dot(c[...], w[rt])

        @pl.when(rt == T - 1)
        def _():
            def step(at, carry):
                n, inv = normed(x[at, :].astype(F32) + (acc[at, :] + vecs[0:1, :]))
                n1[at, :] = n
                inv1[at, :] = jnp.broadcast_to(inv, (ROWS, 128))
                low[at, :] = (n * vecs[1:2, :] + vecs[2:3, :]).astype(BF16)
                return carry

            row_loop(S, ROWS, step, 0)
            turn(low, low_t)

    cols = pl.BlockSpec((S, tile), lambda rt, info: (0, part(info, rt, T)))
    return call(
        kernel, "attend_out", grid, (T,), grid.info, [ctx, tokens, vec] + ws.operands,
        [cols, fixed((S, D)), fixed(vec.shape)] + ws.specs,
        (shape((S, D), F32), shape((S, 128), F32), shape((S, D), BF16), shape((D, S), BF16)),
        (fixed((S, D)), fixed((S, 128)), fixed((S, D)), fixed((D, S))),
        ws.scratch + [pltpu.VMEM((S, D), F32)], cost(2 * S * D * D, 2 * D * D + 12 * S * D),
    )


def expand(grid, ws, low, up_b, FF):
    T = grid.T
    S, D = low.shape
    tile = D // T
    steps = FF // T // tile

    def kernel(info, x, b, *rest):
        refs, (act, slope, w, sem) = rest[: len(ws.specs)], rest[len(ws.specs) :]
        rt, j = pl.program_id(0), pl.program_id(1)

        @pl.when((rt == 0) & (j == 0))
        def _():
            ws.start(info, refs, w, sem)

        ws.wait(info, refs, w, sem, rt, j == 0)
        u = dot(x[...], w[rt, :, pl.ds(pl.multiple_of(j * tile, tile), tile)]) + b[...]
        cdf = 0.5 * (1.0 + lax.erf(u * (2.0**-0.5)))
        act[...] = (u * cdf).astype(BF16)
        slope[...] = (cdf + u * (jnp.exp(-0.5 * u * u) * 0.3989422804014327)).astype(BF16)

    def at(rt, j, info):
        return (0, part(info, rt, T) * steps + j)

    cols = pl.BlockSpec((S, tile), at)
    out = shape((S, FF), BF16)
    return call(
        kernel, "expand", grid, (T, steps), grid.info, [low, up_b] + ws.operands,
        [fixed((S, D)), pl.BlockSpec((1, tile), at)] + ws.specs, (out, out), (cols, cols), ws.scratch,
        cost(2 * S * D * FF, 2 * D * FF + 4 * S * FF, 2 * S * FF),
    )


def contract(grid, ws, act, n1, vec, teacher, keep, scales):
    T = grid.T
    S, D = n1.shape
    FF = act.shape[1]
    tile = D // T
    steps = FF // T // tile

    def kernel(info, scale, a, vecs, kept, n1_any, teacher_any, *rest):
        refs, rest = rest[: len(ws.specs)], rest[len(ws.specs) :]
        low, d_two, d_ffn, d_ffn_t, sums, w, sem, acc, n1_s, teacher_s, own_sem = rest
        rt, j = pl.program_id(0), pl.program_id(1)
        more = [
            pltpu.make_async_copy(n1_any, n1_s, own_sem.at[0]),
            pltpu.make_async_copy(teacher_any, teacher_s, own_sem.at[1]),
        ]

        @pl.when((rt == 0) & (j == 0))
        def _():
            ws.start(info, refs, w, sem)
            for copy in more:
                copy.start()
            acc[...] = jnp.zeros_like(acc)

        ws.wait(info, refs, w, sem, rt, j == 0)
        acc[...] += nt_dot(a[...], w[rt, :, pl.ds(pl.multiple_of(j * tile, tile), tile)])

        @pl.when((rt == T - 1) & (j == steps - 1))
        def _():
            for copy in more:
                copy.wait()

            def step(at, carry):
                s_bias, s_gain, s_shift, s_loss = carry
                first = n1_s[at, :] * vecs[1:2, :] + vecs[2:3, :]
                n, inv = normed(first + (acc[at, :] + vecs[3:4, :]))
                out = n * vecs[4:5, :] + vecs[5:6, :]
                low[at, :] = out.astype(BF16)
                error = out - teacher_s[at, :]
                weighed = kept[at, :] * error
                grad = scale[0] * weighed
                d = normed_back(grad * vecs[4:5, :], n, inv)
                d_two[at, :] = d
                d_ffn[at, :] = d.astype(BF16)
                return (
                    s_bias + fold(d), s_gain + fold(grad * n), s_shift + fold(grad), s_loss + fold(weighed * error),
                )

            zero = jnp.zeros((8, D), F32)
            found = row_loop(S, ROWS, step, (zero, zero, zero, zero))
            found = [jnp.sum(f, axis=0, keepdims=True) for f in found]
            sums[...] = jnp.concatenate(found + [jnp.zeros((4, D), F32)], axis=0)
            turn(d_ffn, d_ffn_t)

    cols = pl.BlockSpec((S, tile), lambda rt, j, info: (0, part(info, rt, T) * steps + j))
    rows = fixed((S, D))
    return call(
        kernel, "contract", grid, (T, steps), grid.info, [scales, act, vec, keep, n1, teacher] + ws.operands,
        [pl.BlockSpec(memory_space=pltpu.SMEM), cols, fixed(vec.shape), fixed((S, 1)), ANY, ANY] + ws.specs,
        (shape((S, D), BF16), shape((S, D), F32), shape((S, D), BF16), shape((D, S), BF16), shape((8, D), F32)),
        (rows, rows, rows, fixed((D, S)), fixed((8, D))),
        ws.scratch + [pltpu.VMEM((S, D), F32)] * 3 + [pltpu.SemaphoreType.DMA((2,))],
        cost(2 * S * D * FF, 2 * D * FF + 2 * S * FF + 20 * S * D),
    )


def contract_back(grid, ws, d_ffn, slope):
    T = grid.T
    S, D = d_ffn.shape
    FF = slope.shape[1]
    tile = D // T
    steps = FF // T // tile

    def kernel(info, x, s, *rest):
        refs, (out, sums, w, sem) = rest[: len(ws.specs)], rest[len(ws.specs) :]
        rt, j = pl.program_id(0), pl.program_id(1)

        @pl.when((rt == 0) & (j == 0))
        def _():
            ws.start(info, refs, w, sem)

        ws.wait(info, refs, w, sem, rt, j == 0)
        d = dot(x[...], w[rt, :, pl.ds(pl.multiple_of(j * tile, tile), tile)]) * s[...].astype(F32)
        d = d.astype(BF16)
        out[...] = d
        sums[...] = fold(d.astype(F32))

    def at(rt, j, info):
        return (0, part(info, rt, T) * steps + j)

    cols = pl.BlockSpec((S, tile), at)
    return call(
        kernel, "contract_back", grid, (T, steps), grid.info, [d_ffn, slope] + ws.operands,
        [fixed((S, D)), cols] + ws.specs, (shape((S, FF), BF16), shape((8, FF), F32)),
        (cols, pl.BlockSpec((8, tile), at)), ws.scratch, cost(2 * S * D * FF, 2 * D * FF + 4 * S * FF),
    )


def expand_back(grid, ws, d_hidden, d_two, n1, inv1, vec):
    T = grid.T
    S, D = n1.shape
    FF = d_hidden.shape[1]
    tile = D // T
    steps = FF // T // tile

    def kernel(info, a, vecs, inv, n1_any, d_two_any, *rest):
        refs, rest = rest[: len(ws.specs)], rest[len(ws.specs) :]
        d_one, d_attn, d_attn_t, sums, w, sem, acc, n1_s, d_two_s, own_sem = rest
        rt, j = pl.program_id(0), pl.program_id(1)
        more = [
            pltpu.make_async_copy(n1_any, n1_s, own_sem.at[0]),
            pltpu.make_async_copy(d_two_any, d_two_s, own_sem.at[1]),
        ]

        @pl.when((rt == 0) & (j == 0))
        def _():
            ws.start(info, refs, w, sem)
            for copy in more:
                copy.start()
            acc[...] = jnp.zeros_like(acc)

        ws.wait(info, refs, w, sem, rt, j == 0)
        acc[...] += nt_dot(a[...], w[rt, :, pl.ds(pl.multiple_of(j * tile, tile), tile)])

        @pl.when((rt == T - 1) & (j == steps - 1))
        def _():
            for copy in more:
                copy.wait()

            def step(at, carry):
                s_bias, s_gain, s_shift = carry
                n = n1_s[at, :]
                grad = d_two_s[at, :] + acc[at, :]
                d = normed_back(grad * vecs[1:2, :], n, inv[at, 0:1])
                d_one[at, :] = d
                d_attn[at, :] = d.astype(BF16)
                return s_bias + fold(d), s_gain + fold(grad * n), s_shift + fold(grad)

            zero = jnp.zeros((8, D), F32)
            found = row_loop(S, ROWS, step, (zero, zero, zero))
            found = [jnp.sum(f, axis=0, keepdims=True) for f in found]
            sums[...] = jnp.concatenate(found + [jnp.zeros((5, D), F32)], axis=0)
            turn(d_attn, d_attn_t)

    cols = pl.BlockSpec((S, tile), lambda rt, j, info: (0, part(info, rt, T) * steps + j))
    rows = fixed((S, D))
    return call(
        kernel, "expand_back", grid, (T, steps), grid.info, [d_hidden, vec, inv1, n1, d_two] + ws.operands,
        [cols, fixed(vec.shape), fixed((S, 128)), ANY, ANY] + ws.specs,
        (shape((S, D), F32), shape((S, D), BF16), shape((D, S), BF16), shape((8, D), F32)),
        (rows, rows, fixed((D, S)), fixed((8, D))),
        ws.scratch + [pltpu.VMEM((S, D), F32)] * 3 + [pltpu.SemaphoreType.DMA((2,))],
        cost(2 * S * D * FF, 2 * D * FF + 2 * S * FF + 20 * S * D),
    )


def attend_out_back(grid, pieces, d_attn):
    T = grid.T
    S, D = d_attn.shape
    tile = D // T
    ws = Weights(grid, D, [(pieces, 3 * tile, tile, 0)])

    def kernel(info, x, *rest):
        refs, (out, w, sem) = rest[: len(ws.specs)], rest[len(ws.specs) :]
        rt = pl.program_id(0)

        @pl.when(rt == 0)
        def _():
            ws.start(info, refs, w, sem)

        ws.wait(info, refs, w, sem, rt, True)
        out[...] = dot(x[...], w[rt]).astype(BF16)

    cols = pl.BlockSpec((S, tile), lambda rt, info: (0, part(info, rt, T)))
    return call(
        kernel, "attend_out_back", grid, (T,), grid.info, [d_attn] + ws.operands, [fixed((S, D))] + ws.specs,
        shape((S, D), BF16), cols, ws.scratch, cost(2 * S * D * D, 2 * D * D + 4 * S * D),
    )


def project_back(grid, pieces, dq, dk, dv, d_one):
    T = grid.T
    S, D = d_one.shape
    tile = D // T
    ws = Weights(grid, D, [(pieces, 0, 3 * tile, 0)])

    def kernel(info, q, k, v, one, *rest):
        refs, (out, w, sem) = rest[: len(ws.specs)], rest[len(ws.specs) :]
        rt = pl.program_id(0)

        @pl.when(rt == 0)
        def _():
            ws.start(info, refs, w, sem)
            out[...] = one[...]

        ws.wait(info, refs, w, sem, rt, True)
        g = nt_dot(q[...], w[rt, :, :tile]) + nt_dot(k[...], w[rt, :, tile : 2 * tile])
        out[...] += g + nt_dot(v[...], w[rt, :, 2 * tile :])

    cols = pl.BlockSpec((S, tile), lambda rt, info: (0, part(info, rt, T)))
    return call(
        kernel, "project_back", grid, (T,), grid.info, [dq, dk, dv, d_one] + ws.operands,
        [cols, cols, cols, fixed((S, D))] + ws.specs, shape((S, D), F32), fixed((S, D)), ws.scratch,
        cost(6 * S * D * D, 6 * D * D + 14 * S * D),
    )


def weight_grad(grid, lefts, rights, core, received=None, line_first=False):
    T, Z = grid.T, grid.Z
    D, S = lefts[0].shape
    R = D // grid.dp
    tile = D // T
    spans, steps = [], 0
    for which, b, lo, count in rights:
        spans.append((which, steps, lo // tile, count // tile, b.shape[1] // T // tile))
        steps += count // tile

    def kernel(info, *rest):
        left_refs = rest[: len(lefts)]
        right_refs = rest[len(lefts) : len(lefts) + len(rights)]
        rest = rest[len(lefts) + len(rights) :]
        got, out, rows = rest if received is not None else (None, *rest)
        rt, j = pl.program_id(0), pl.program_id(1)

        @pl.when((rt == 0) & (j == 0))
        def _():
            for a in range(len(lefts)):
                for rx in range(2):
                    for z in range(Z):
                        at = (z * 4 + (info[1] ^ rx) * 2 + (info[2] ^ core)) * R
                        to = (z * 2 + rx if line_first else rx * Z + z) * R
                        rows[a, pl.ds(to, R), :] = left_refs[a][pl.ds(pl.multiple_of(at, R), R), :]

        for (which, start, _, count, _), right in zip(spans, right_refs):

            @pl.when((j >= start) & (j < start + count))
            def _(which=which, right=right):
                g = dot(rows[which], right[...]).reshape(out.shape)
                if received is not None:
                    g = g + got[...].astype(F32)
                out[...] = g.astype(BF16)

    def right_map(start, lo, count, every):
        def index(rt, j, info):
            return (0, part(info, rt, T) * every + lo + jnp.clip(j - start, 0, count - 1))

        return index

    width = steps * tile
    if line_first:
        block = pl.BlockSpec((Z, 1, 2, R, tile), lambda rt, j, info: (0, rt, 0, 0, j))
        dims = (Z, T, 2, R, width)
    else:
        block = pl.BlockSpec((1, 2, Z, R, tile), lambda rt, j, info: (rt, 0, 0, 0, j))
        dims = (T, 2, Z, R, width)
    in_specs = [fixed((D, S)) for _ in lefts] + [pl.BlockSpec((S, tile), right_map(*s[1:])) for s in spans]
    operands = list(lefts) + [r[1] for r in rights]
    if received is not None:
        in_specs.append(block)
        operands.append(received)
    return call(
        kernel, "weight_grad", grid, (T, steps), grid.info, operands, in_specs, shape(dims, BF16), block,
        [pltpu.VMEM((len(lefts), D // 2, S), BF16)],
        cost(D * S * width * T, 2 * S * width * T + (1 if received is None else 2) * D * width * T), 32,
    )


def attention_forward(q, k, v, seg_col, seg_row):
    S, D = q.shape
    pairs = D // (2 * HD)

    def kernel(q, k, v, col, row, ctx, probs, bias):
        @pl.when(pl.program_id(0) == 0)
        def _():
            bias[...] = jnp.where(col[...] == row[...], 0.0, MASKED)

        lane = lax.broadcasted_iota(jnp.int32, (S, 2 * HD), 1) < HD
        query = q[...] * jnp.asarray(0.125, BF16)
        zero = jnp.zeros_like(query)
        outs = []
        for h in range(2):
            mine = jnp.where(lane == (h == 0), query, zero)
            s = nt_dot(mine, k[...]) + bias[...]
            e = jnp.exp(s - jnp.max(s, axis=-1, keepdims=True))
            p = (e * (1.0 / jnp.sum(e, axis=-1, keepdims=True))).astype(BF16)
            probs[h] = p
            outs.append(dot(p, v[...]))
        ctx[...] = jnp.where(lane, outs[0], outs[1]).astype(BF16)

    rows = pl.BlockSpec((S, 2 * HD), lambda i: (0, i))
    return pl.pallas_call(
        kernel,
        grid=(pairs,),
        out_shape=(shape((S, D), BF16), shape((2 * pairs, S, S), BF16)),
        in_specs=[rows, rows, rows, fixed((S, 1)), fixed((1, S))],
        out_specs=(rows, pl.BlockSpec((2, S, S), lambda i: (i, 0, 0))),
        scratch_shapes=[pltpu.VMEM((S, S), F32)],
        cost_estimate=cost(16 * S * S * D, 8 * S * D + 4 * pairs * S * S, 2 * pairs * S * S),
        compiler_params=pltpu.CompilerParams(vmem_limit_bytes=32 << 20),
        name="attention_forward",
    )(q, k, v, seg_col, seg_row)


def attention_backward(q, k, v, ctx, d_ctx, probs):
    S, D = q.shape
    pairs = D // (2 * HD)

    def kernel(q, k, v, ctx, d_ctx, probs, dq, dk, dv, sums):
        lane = lax.broadcasted_iota(jnp.int32, (S, 2 * HD), 1) < HD
        grad = d_ctx[...]
        both = grad.astype(F32) * ctx[...].astype(F32)
        dqs, dks, dvs = [], [], []
        for h in range(2):
            mask = lane == (h == 0)
            inner = jnp.sum(jnp.where(mask, both, 0.0), axis=-1, keepdims=True)
            mine = jnp.where(mask, grad, jnp.zeros_like(grad))
            d_prob = nt_dot(mine, v[...])
            p = probs[h]
            ds = (p.astype(F32) * (d_prob - inner)).astype(BF16)
            dvs.append(lax.dot_general(p, grad, TN, preferred_element_type=F32))
            dqs.append(dot(ds, k[...]))
            dks.append(lax.dot_general(ds, q[...], TN, preferred_element_type=F32))
        a = (jnp.where(lane, dqs[0], dqs[1]) * 0.125).astype(BF16)
        b = jnp.where(lane, dvs[0], dvs[1]).astype(BF16)
        dq[...] = a
        dk[...] = (jnp.where(lane, dks[0], dks[1]) * 0.125).astype(BF16)
        dv[...] = b
        total_a = jnp.sum(a.astype(F32), axis=0, keepdims=True)
        total_b = jnp.sum(b.astype(F32), axis=0, keepdims=True)
        sums[...] = jnp.concatenate([total_a, total_b, jnp.zeros((6, 2 * HD), F32)], axis=0)

    rows = pl.BlockSpec((S, 2 * HD), lambda i: (0, i))
    out = shape((S, D), BF16)
    return pl.pallas_call(
        kernel,
        grid=(pairs,),
        out_shape=(out, out, out, shape((8, D), F32)),
        in_specs=[rows] * 5 + [pl.BlockSpec((2, S, S), lambda i: (i, 0, 0))],
        out_specs=(rows, rows, rows, pl.BlockSpec((8, 2 * HD), lambda i: (0, i))),
        cost_estimate=cost(32 * S * S * D, 16 * S * D + 4 * pairs * S * S),
        compiler_params=pltpu.CompilerParams(vmem_limit_bytes=32 << 20),
        name="attention_backward",
    )(q, k, v, ctx, d_ctx, probs)


def after(x, *others):
    return lax.optimization_barrier((x, *others))[0]


def body(
    sizes,
    tokens,
    teacher,
    valid_mask,
    segments,
    loss_scale,
    qkv_weight,
    qv_bias,
    out_weight,
    out_bias,
    first_gain,
    first_shift,
    up_weight,
    up_bias,
    down_weight,
    down_bias,
    second_gain,
    second_shift,
):
    grid = Grid(*sizes)
    grid.here()
    T, dp = grid.T, grid.dp
    S, D = tokens.shape
    assert S == SEQ
    up_cols = up_weight.shape[1]
    FF = up_cols * T
    tile = D // T
    R = D // dp
    cut = up_cols - up_cols // 4
    keep = valid_mask.astype(F32)

    down_rows = down_weight.T
    first_own = jnp.concatenate([qkv_weight[0], qkv_weight[1], qkv_weight[2], out_weight.T], axis=1)
    middle_own = jnp.concatenate([up_weight, down_rows[:, cut:]], axis=1)
    first, middle, last = grid.gather(first_own, middle_own, down_rows[:, :cut])

    def placed(v):
        wide = lax.dynamic_update_slice_in_dim(jnp.zeros(v.shape[:-1] + (dp * v.shape[-1],), F32), v.astype(F32), grid.d * v.shape[-1], v.ndim - 1)
        out = jnp.zeros(v.shape[:-2] + (T,) + wide.shape[-2:], F32)
        return lax.dynamic_update_slice_in_dim(out, wide[..., None, :, :], grid.t, v.ndim - 2)

    eight = jnp.concatenate([jnp.stack([out_bias, first_gain, first_shift, down_bias, second_gain, second_shift]), qv_bias])
    packed = jnp.concatenate(
        [placed(eight).reshape(-1, 128), placed(up_bias).reshape(-1, 128), jnp.full((8, 128), jnp.sum(keep))]
    )
    packed = grid.total_small(packed)
    n8, nu = 8 * D // 128, FF // 128
    vec = packed[:n8].reshape(8, D)
    up_b = packed[n8 : n8 + nu].reshape(1, FF)
    count_all = packed[n8 + nu, 0]
    norm_scale = count_all * D

    mine = lax.dynamic_slice_in_dim(segments, grid.t * S, S)
    q, k, v = project_qkv(grid, first, tokens, vec)
    ctx, probs = attention_forward(q, k, v, mine[:, None], mine[None, :])
    n1, inv1, first_low, first_low_t = attend_out(grid, first, ctx, tokens, vec)
    up = Weights(grid, D, [(middle, 0, up_cols, 0)])
    down = Weights(grid, D, [(last, 0, cut, 0), (middle, up_cols, up_cols - cut, cut)])
    act, slope = expand(grid, up, first_low, up_b, FF)
    scales = (2.0 * loss_scale / norm_scale).reshape(1)
    out_low, d_two, d_ffn, d_ffn_t, sums_two = contract(grid, down, act, n1, vec, teacher, keep[:, None], scales)

    theirs = weight_grad(grid, [d_ffn_t], [(0, act, 0, cut)], 1, line_first=True)
    theirs = grid.cs(theirs)
    d_hidden, sums_up = contract_back(grid, down, d_ffn, slope)
    ours = weight_grad(grid, [d_ffn_t], [(0, act, 0, cut)], 0, theirs, line_first=True)
    g_last = grid.scatter_line_first(ours)

    d_one, d_attn, d_attn_t, sums_one = expand_back(grid, up, d_hidden, d_two, n1, inv1, vec)
    lefts = [first_low_t, d_attn_t, d_ffn_t]
    rights = [(0, d_hidden, 0, up_cols), (1, ctx, 0, tile), (2, act, cut, up_cols - cut)]
    theirs = grid.cs(weight_grad(grid, lefts, rights, 1))
    d_ctx = attend_out_back(grid, first, d_attn)
    g_middle = grid.scatter(weight_grad(grid, lefts, rights, 0, theirs))

    dq, dk, dv, sums_qv = attention_backward(q, k, v, ctx, d_ctx, probs)
    tokens_t = tokens.T
    rights = [(0, dq, 0, tile), (0, dk, 0, tile), (0, dv, 0, tile)]
    theirs = grid.cs(weight_grad(grid, [tokens_t], rights, 1))
    grad_tokens = project_back(grid, first, dq, dk, dv, d_one)
    g_first = grid.scatter(weight_grad(grid, [tokens_t], rights, 0, theirs))

    found = jnp.concatenate(
        [
            jnp.concatenate([sums_one[0:3], sums_two[0:3], sums_qv[0:2]]).reshape(-1, 128),
            jnp.sum(sums_up, axis=0).reshape(-1, 128),
            jnp.full((8, 128), jnp.sum(sums_two[3])),
        ]
    )
    found = grid.total_small(found)

    def own(v, rows):
        v = lax.dynamic_slice_in_dim(v, grid.t * rows, rows, v.ndim - 2)
        return lax.dynamic_slice_in_dim(v, grid.d * (HD // dp), HD // dp, v.ndim - 1)

    g8 = own(found[:n8].reshape(8, D // HD, HD), D // HD // T)
    g_up_b = own(found[n8 : n8 + nu].reshape(FF // HD, HD), FF // HD // T)
    loss_value = found[n8 + nu, 0] / norm_scale
    g_down = jnp.concatenate([g_last, g_middle[:, up_cols + tile :]], axis=1)
    return (
        out_low,
        loss_value,
        grad_tokens,
        g_first.reshape(R, 3, tile).transpose(1, 0, 2),
        g8[6:8],
        g_middle[:, up_cols : up_cols + tile].T,
        g8[0],
        g8[1],
        g8[2],
        g_middle[:, :up_cols],
        g_up_b,
        g_down.T,
        g8[3],
        g8[4],
        g8[5],
    )


def solution(mesh):
    vector = P("tensor", "dp")
    rows = P(("dp", "tensor"), None)
    qkv, qv, cols = P(None, "dp", "tensor"), P(None, "tensor", "dp"), P("dp", "tensor")
    return jax.shard_map(
        functools.partial(body, (mesh.shape["dp"], mesh.shape["tensor"])),
        mesh=mesh,
        in_specs=(
            rows, rows, P(("dp", "tensor")), P("dp"), P(), qkv, qv, vector, vector, vector, vector, cols,
            vector, vector, vector, vector, vector,
        ),
        out_specs=(
            rows, P(), rows, qkv, qv, vector, vector, vector, vector, cols, vector, vector, vector, vector, vector,
        ),
        check_vma=False,
    )
```

```python
import functools

import jax
import jax.numpy as jnp
from jax import lax
from jax.experimental import pallas as pl
from jax.experimental.pallas import tpu as pltpu
from jax.sharding import PartitionSpec as P

HD = 64
SEQ = 512
EPS = 1e-06
MASKED = -1e30
F32 = jnp.float32
BF16 = jnp.bfloat16
ANY = pl.BlockSpec(memory_space=pltpu.HBM)
NT = (((1,), (1,)), ((), ()))
TN = (((0,), (0,)), ((), ()))


def cost(flops, nbytes, trans=0):
    return pl.CostEstimate(flops=int(flops), bytes_accessed=int(nbytes), transcendentals=int(trans))


def nt_dot(a, b):
    return lax.dot_general(a, b, NT, preferred_element_type=F32)


def dot(a, b):
    return jnp.dot(a, b, preferred_element_type=F32)


def after(x, *others):
    return lax.optimization_barrier((x, *others))[0] if others else x


def add(a, b):
    return (a.astype(F32) + b.astype(F32)).astype(BF16)


class Pieces:
    def __init__(self, parts):
        self.arrays = [a for a, _ in parts]
        self.places = [p for _, p in parts]


class Grid:
    def __init__(self, dp, tensor):
        self.dp, self.T, self.Z = dp, tensor, dp // 4
        assert dp == self.Z * 4
        Z = self.Z
        self.cycle = [0] + list(range(1, Z, 2)) + list(range(2, Z, 2))[::-1]
        self.place = [self.cycle.index(z) for z in range(Z)]
        after = {self.cycle[i]: self.cycle[(i + 1) % Z] for i in range(Z)}
        cells = [(z, x, c) for z in range(Z) for x in range(2) for c in range(2)]
        self.to_z = [(self.rank(z, x, c), self.rank(after[z], x, c)) for z, x, c in cells]
        self.to_x = [(self.rank(z, x, c), self.rank(z, 1 - x, c)) for z, x, c in cells]
        self.to_c = [(self.rank(z, x, c), self.rank(z, x, 1 - c)) for z, x, c in cells]
        self.to_t = [(t, (t + 1) % tensor) for t in range(tensor)]
        self.square = tensor == 2 and Z == 4

    @staticmethod
    def rank(z, x, c):
        return z * 4 + x * 2 + c

    def here(self):
        d = lax.axis_index("dp")
        self.d, self.z, self.x, self.c, self.t = d, d // 4, (d // 2) % 2, d % 2, lax.axis_index("tensor")
        back = []
        for k in range(self.Z):
            options = [self.cycle[(p - k) % self.Z] for p in self.place]
            back.append(sum(jnp.where(self.z == z, o, 0) for z, o in enumerate(options)))
        self.back = back
        self.info = jnp.stack([v.astype(jnp.int32) for v in [self.t, self.x, self.c, self.z] + back])

    def zs(self, a):
        return lax.ppermute(a, "dp", self.to_z)

    def xs(self, a):
        return lax.ppermute(a, "dp", self.to_x)

    def cs(self, a):
        return lax.ppermute(a, "dp", self.to_c)

    def ts(self, a):
        return lax.ppermute(a, "tensor", self.to_t)

    def both_cores(self, parts):
        twins = [(self.cs(a), [(t, x, 1, k) for t, x, _, k in places]) for a, places in parts]
        return Pieces(parts + twins)

    def gather_general(self, own):
        ring = [own]
        for _ in range(self.Z - 1):
            ring.append(self.zs(ring[-1]))
        line, slots = jnp.stack(ring), range(self.Z)
        parts = [(line, [(0, 0, 0, k) for k in slots]), (self.xs(line), [(0, 1, 0, k) for k in slots])]
        rows = line
        for rt in range(1, self.T):
            rows = self.ts(rows)
            parts.append((rows, [(rt, 0, 0, k) for k in slots]))
            parts.append((self.xs(rows), [(rt, 1, 0, k) for k in slots]))
        return self.both_cores(parts)

    def gather(self, first, middle, last, hold):
        if not self.square:
            whole = [self.gather_general(a) for a in (first, middle, last)]
            return whole[0], lambda *_: whole[1:]
        half = last.shape[0] // 2
        a0, b0, d = first[None], middle, last
        a1 = self.zs(a0)
        d_x, d_t = self.xs(d), self.ts(d)
        a0_x, a0_t = self.xs(a0), self.ts(a0)
        a2 = self.zs(a1)
        d_far = [self.xs(d_t[:half]), self.ts(d_x[half:])]
        a1_x, a1_t = self.xs(a1), self.ts(a1)
        plane = jnp.stack([d, d_x, d_t, jnp.concatenate(d_far)])
        a3 = self.zs(a2)
        b1 = self.zs(b0)
        a23 = jnp.concatenate([a2, a3])
        a23_x, a23_t = self.xs(a23), self.ts(a23)
        b2 = self.zs(b1)
        a_far = [self.xs(a0_t), self.xs(a1_t), self.ts(a23_x)]
        b3 = self.zs(b2)
        line = jnp.stack([b0, b1, b2, b3])
        p1 = self.zs(plane)

        def at(t, x, *slots):
            return [(t, x, 0, k) for k in slots]

        a_parts = [
            (a0, at(0, 0, 0)), (a1, at(0, 0, 1)), (a23, at(0, 0, 2, 3)),
            (a0_x, at(0, 1, 0)), (a1_x, at(0, 1, 1)), (a23_x, at(0, 1, 2, 3)),
            (a0_t, at(1, 0, 0)), (a1_t, at(1, 0, 1)), (a23_t, at(1, 0, 2, 3)),
            (a_far[0], at(1, 1, 0)), (a_far[1], at(1, 1, 1)), (a_far[2], at(1, 1, 2, 3)),
        ]

        def others(q, ctx, low):
            b_x, b_t = self.xs(after(line, a_far[1])), self.ts(after(line, a_far[2]))
            p2 = self.zs(p1)
            b_far = [self.xs(after(b_t[:2], ctx)), self.ts(after(b_x[2:], ctx))]
            p3 = self.zs(after(p2, q))
            b_parts = [
                (line, at(0, 0, 0, 1, 2, 3)), (b_x, at(0, 1, 0, 1, 2, 3)), (b_t, at(1, 0, 0, 1, 2, 3)),
                (b_far[0], at(1, 1, 0, 1)), (b_far[1], at(1, 1, 2, 3)),
            ]
            d_parts = [
                (p, [(0, 0, 0, k), (0, 1, 0, k), (1, 0, 0, k), (1, 1, 0, k)]) for k, p in enumerate([plane, p1, p2, p3])
            ]
            return self.both_cores(b_parts), self.both_cores(d_parts)

        return self.both_cores(a_parts), others

    def total_small(self, v):
        v = v + self.cs(v)
        v = v + self.xs(v)
        held = v
        for _ in range(1, self.T):
            held = self.ts(held)
            v = v + held
        held = v
        for _ in range(1, self.Z):
            held = self.zs(held)
            v = v + held
        return v

    def line_hop(self, own, step, held=None):
        block = lax.dynamic_index_in_dim(own, self.back[step], 0, keepdims=False)
        if held is not None:
            block = block.astype(F32) + held.astype(F32)
        return self.zs(block.astype(BF16))

    def line_end(self, own, held):
        return lax.dynamic_index_in_dim(own, self.z, 0, keepdims=False).astype(F32) + held.astype(F32)

    def line(self, own, held=None, first=1):
        for step in range(first, self.Z):
            held = self.line_hop(own, step, held)
        return self.line_end(own, held)

    def plane_start(self, parts):
        own, x_lo, x_hi, t_lo, t_hi, far_lo, far_hi = parts
        return self.xs(far_lo), self.ts(far_hi), self.xs(x_lo), self.ts(t_hi)

    def plane_middle(self, parts, found):
        return self.xs(add(parts[2], found[1])), self.ts(add(parts[3], found[0]))

    def plane_end(self, parts, found, last):
        own, half = parts[0].astype(F32), parts[0].shape[0] // 2
        low = own[:half] + found[2].astype(F32) + last[1].astype(F32)
        high = own[half:] + last[0].astype(F32) + found[3].astype(F32)
        return jnp.concatenate([low, high])

    def plane(self, parts):
        found = self.plane_start(parts)
        return self.plane_end(parts, found, self.plane_middle(parts, found))

    def quarters(self, g):
        half = g.shape[2] // 2
        x, t, far = g[0, 1], g[1, 0], g[1, 1]
        return g[0, 0], x[:half], x[half:], t[:half], t[half:], far[:half], far[half:]

    def general(self, g):
        rows = g[:, 0].astype(F32) + self.xs(g[:, 1]).astype(F32)
        held = None
        for step in range(1, self.T):
            block = rows[(self.T - step) % self.T]
            if held is not None:
                block = block + held.astype(F32)
            held = self.ts(block.astype(BF16))
        return rows[0] + held.astype(F32)


class Weights:
    def __init__(self, grid, D, sources):
        self.T, self.D, self.R = grid.T, D, D // grid.dp
        self.sources = sources
        self.width = sum(s[2] for s in sources)
        seen = []
        for pieces, *_ in sources:
            if pieces not in seen:
                seen.append(pieces)
        self.operands = [pltpu.with_memory_space_constraint(a, pltpu.HBM) for pieces in seen for a in pieces.arrays]
        self.first = {id(p): sum(len(q.arrays) for q in seen[:i]) for i, p in enumerate(seen)}
        self.specs = [ANY] * len(self.operands)
        self.scratch = [pltpu.VMEM((self.T, D, self.width), BF16), pltpu.SemaphoreType.DMA((self.T,))]

    def copies(self, info, refs, w, sem, want):
        out = []
        for pieces, lo, count, to in self.sources:
            base = self.first[id(pieces)]
            for i, places in enumerate(pieces.places):
                for entry, (rt, rx, rc, k) in enumerate(places):
                    if rt != want:
                        continue
                    row = (info[4 + k] * 4 + (info[1] ^ rx) * 2 + (info[2] ^ rc)) * self.R
                    src = refs[base + i].at[entry, :, pl.ds(lo, count)]
                    dst = w.at[rt, pl.ds(pl.multiple_of(row, self.R), self.R), pl.ds(to, count)]
                    out.append(pltpu.make_async_copy(src, dst, sem.at[rt]))
        return out

    def start(self, info, refs, w, sem):
        for rt in range(self.T):
            for copy in self.copies(info, refs, w, sem, rt):
                copy.start()

    def wait(self, info, refs, w, sem, rt, first):
        for want in range(self.T):

            @pl.when((rt == want) & first)
            def _(want=want):
                for copy in self.copies(info, refs, w, sem, want):
                    copy.wait()


def part(info, rt, T):
    return lax.rem(info[0] - rt + T, T)


def call(kernel, name, grid, steps, info, operands, in_specs, outs, out_specs, scratch, estimate, mib=36):
    return pl.pallas_call(
        kernel,
        out_shape=outs,
        grid_spec=pltpu.PrefetchScalarGridSpec(
            num_scalar_prefetch=1, grid=steps, in_specs=in_specs, out_specs=out_specs, scratch_shapes=scratch
        ),
        cost_estimate=estimate,
        compiler_params=pltpu.CompilerParams(vmem_limit_bytes=mib << 20),
        name=name,
    )(info, *operands)


def shape(dims, dtype):
    return jax.ShapeDtypeStruct(dims, dtype)


def fixed(dims):
    return pl.BlockSpec(dims, lambda *_: (0,) * len(dims))


def project_qkv(grid, pieces, tokens, vec):
    T = grid.T
    S, D = tokens.shape
    tile = D // T
    ws = Weights(grid, D, [(pieces, 0, 3 * tile, 0)])

    def kernel(info, x, bias, *rest):
        refs, (q, k, v, w, sem) = rest[: len(ws.specs)], rest[len(ws.specs) :]
        rt = pl.program_id(0)

        @pl.when(rt == 0)
        def _():
            ws.start(info, refs, w, sem)

        ws.wait(info, refs, w, sem, rt, True)
        a, mine = x[...], w.at[rt]
        q[...] = (dot(a, mine[:, :tile]) + bias[6:7, :]).astype(BF16)
        k[...] = dot(a, mine[:, tile : 2 * tile]).astype(BF16)
        v[...] = (dot(a, mine[:, 2 * tile :]) + bias[7:8, :]).astype(BF16)

    cols = pl.BlockSpec((S, tile), lambda rt, info: (0, part(info, rt, T)))
    biases = pl.BlockSpec((vec.shape[0], tile), lambda rt, info: (0, part(info, rt, T)))
    out = shape((S, D), BF16)
    return call(
        kernel, "project_qkv", grid, (T,), grid.info, [tokens, vec] + ws.operands, [fixed((S, D)), biases] + ws.specs,
        (out, out, out), (cols, cols, cols), ws.scratch, cost(6 * S * D * D, 6 * D * D + 8 * S * D),
    )


def row_loop(S, rows, step, start):
    return lax.fori_loop(0, S // rows, lambda i, carry: step(pl.ds(pl.multiple_of(i * rows, rows), rows), carry), start)


def fold(a):
    return jnp.sum(a.reshape(a.shape[0] // 8, 8, a.shape[1]), axis=0)


def turn(src, dst):
    S = src.shape[0]

    def step(i, _):
        at = pl.ds(pl.multiple_of(i * 128, 128), 128)
        dst[:, at] = src[at, :].T
        return 0

    lax.fori_loop(0, S // 128, step, 0)


def normed(r):
    c = r - jnp.mean(r, axis=-1, keepdims=True)
    inv = lax.rsqrt(jnp.mean(c * c, axis=-1, keepdims=True) + EPS)
    return c * inv, inv


def normed_back(d, n, inv):
    return (d - jnp.mean(d, axis=-1, keepdims=True) - n * jnp.mean(d * n, axis=-1, keepdims=True)) * inv


ROWS = 128


def attend_out(grid, pieces, ctx, tokens, vec):
    T = grid.T
    S, D = tokens.shape
    tile = D // T
    ws = Weights(grid, D, [(pieces, 3 * tile, tile, 0)])

    def kernel(info, c, x, vecs, *rest):
        refs, (n1, inv1, low, low_t, w, sem, acc) = rest[: len(ws.specs)], rest[len(ws.specs) :]
        rt = pl.program_id(0)

        @pl.when(rt == 0)
        def _():
            ws.start(info, refs, w, sem)
            acc[...] = jnp.zeros_like(acc)

        ws.wait(info, refs, w, sem, rt, True)
        acc[...] += nt_dot(c[...], w[rt])

        @pl.when(rt == T - 1)
        def _():
            def step(at, carry):
                n, inv = normed(x[at, :].astype(F32) + (acc[at, :] + vecs[0:1, :]))
                n1[at, :] = n
                inv1[at, :] = jnp.broadcast_to(inv, (ROWS, 128))
                low[at, :] = (n * vecs[1:2, :] + vecs[2:3, :]).astype(BF16)
                return carry

            row_loop(S, ROWS, step, 0)
            turn(low, low_t)

    cols = pl.BlockSpec((S, tile), lambda rt, info: (0, part(info, rt, T)))
    return call(
        kernel, "attend_out", grid, (T,), grid.info, [ctx, tokens, vec] + ws.operands,
        [cols, fixed((S, D)), fixed(vec.shape)] + ws.specs,
        (shape((S, D), F32), shape((S, 128), F32), shape((S, D), BF16), shape((D, S), BF16)),
        (fixed((S, D)), fixed((S, 128)), fixed((S, D)), fixed((D, S))),
        ws.scratch + [pltpu.VMEM((S, D), F32)], cost(2 * S * D * D, 2 * D * D + 12 * S * D),
    )


def chunks(width, size):
    return [(lo, min(size, width - lo)) for lo in range(0, width, size)]


WIDE = 1024


def expand(grid, ws, low, up_b, FF):
    T = grid.T
    S, D = low.shape
    cols = FF // T

    def kernel(info, x, b, *rest):
        refs, (act, slope, w, sem) = rest[: len(ws.specs)], rest[len(ws.specs) :]
        rt = pl.program_id(0)

        @pl.when(rt == 0)
        def _():
            ws.start(info, refs, w, sem)

        ws.wait(info, refs, w, sem, rt, True)
        for lo, n in chunks(cols, WIDE // 2):
            u = dot(x[...], w[rt, :, lo : lo + n]) + b[:, lo : lo + n]
            cdf = 0.5 * (1.0 + lax.erf(u * (2.0**-0.5)))
            act[:, lo : lo + n] = (u * cdf).astype(BF16)
            slope[:, lo : lo + n] = (cdf + u * (jnp.exp(-0.5 * u * u) * 0.3989422804014327)).astype(BF16)

    def at(rt, info):
        return (0, part(info, rt, T))

    block = pl.BlockSpec((S, cols), at)
    out = shape((S, FF), BF16)
    return call(
        kernel, "expand", grid, (T,), grid.info, [low, up_b] + ws.operands,
        [fixed((S, D)), pl.BlockSpec((1, cols), at)] + ws.specs, (out, out), (block, block), ws.scratch,
        cost(2 * S * D * FF, 2 * D * FF + 4 * S * FF, 2 * S * FF),
    )


def contract(grid, ws, act, n1, vec, teacher, keep, scales):
    T = grid.T
    S, D = n1.shape
    FF = act.shape[1]
    cols = FF // T

    def kernel(info, scale, a, vecs, kept, n1_any, teacher_any, *rest):
        refs, rest = rest[: len(ws.specs)], rest[len(ws.specs) :]
        low, d_two, d_ffn, d_ffn_t, sums, w, sem, acc, n1_s, teacher_s, own_sem = rest
        rt = pl.program_id(0)
        more = [
            pltpu.make_async_copy(n1_any, n1_s, own_sem.at[0]),
            pltpu.make_async_copy(teacher_any, teacher_s, own_sem.at[1]),
        ]

        @pl.when(rt == 0)
        def _():
            ws.start(info, refs, w, sem)
            for copy in more:
                copy.start()

        ws.wait(info, refs, w, sem, rt, True)

        def product(add):
            for lo, n in chunks(D, WIDE // 2):
                got = nt_dot(a[...], w[rt, lo : lo + n, :])
                acc[:, lo : lo + n] = acc[:, lo : lo + n] + got if add else got

        pl.when(rt == 0)(lambda: product(False))
        pl.when(rt > 0)(lambda: product(True))

        @pl.when(rt == T - 1)
        def _():
            for copy in more:
                copy.wait()

            def step(at, carry):
                s_bias, s_gain, s_shift, s_loss = carry
                first = n1_s[at, :] * vecs[1:2, :] + vecs[2:3, :]
                n, inv = normed(first + (acc[at, :] + vecs[3:4, :]))
                out = n * vecs[4:5, :] + vecs[5:6, :]
                low[at, :] = out.astype(BF16)
                error = out - teacher_s[at, :]
                weighed = kept[at, :] * error
                grad = scale[0] * weighed
                d = normed_back(grad * vecs[4:5, :], n, inv)
                d_two[at, :] = d
                d_ffn[at, :] = d.astype(BF16)
                return (
                    s_bias + fold(d), s_gain + fold(grad * n), s_shift + fold(grad), s_loss + fold(weighed * error),
                )

            zero = jnp.zeros((8, D), F32)
            found = row_loop(S, ROWS, step, (zero, zero, zero, zero))
            found = [jnp.sum(f, axis=0, keepdims=True) for f in found]
            sums[...] = jnp.concatenate(found + [jnp.zeros((4, D), F32)], axis=0)
            turn(d_ffn, d_ffn_t)

    block = pl.BlockSpec((S, cols), lambda rt, info: (0, part(info, rt, T)))
    rows = fixed((S, D))
    return call(
        kernel, "contract", grid, (T,), grid.info, [scales, act, vec, keep, n1, teacher] + ws.operands,
        [pl.BlockSpec(memory_space=pltpu.SMEM), block, fixed(vec.shape), fixed((S, 1)), ANY, ANY] + ws.specs,
        (shape((S, D), BF16), shape((S, D), F32), shape((S, D), BF16), shape((D, S), BF16), shape((8, D), F32)),
        (rows, rows, rows, fixed((D, S)), fixed((8, D))),
        ws.scratch + [pltpu.VMEM((S, D), F32)] * 3 + [pltpu.SemaphoreType.DMA((2,))],
        cost(2 * S * D * FF, 2 * D * FF + 2 * S * FF + 20 * S * D),
    )


def contract_back(grid, ws, d_ffn, slope):
    T = grid.T
    S, D = d_ffn.shape
    FF = slope.shape[1]
    cols = FF // T

    def kernel(info, x, s, *rest):
        refs, (out, sums, w, sem) = rest[: len(ws.specs)], rest[len(ws.specs) :]
        rt = pl.program_id(0)

        @pl.when(rt == 0)
        def _():
            ws.start(info, refs, w, sem)

        ws.wait(info, refs, w, sem, rt, True)
        for lo, n in chunks(cols, WIDE):
            d = dot(x[...], w[rt, :, lo : lo + n]) * s[:, lo : lo + n].astype(F32)
            d = d.astype(BF16)
            out[:, lo : lo + n] = d
            sums[:, lo : lo + n] = fold(d.astype(F32))

    def at(rt, info):
        return (0, part(info, rt, T))

    block = pl.BlockSpec((S, cols), at)
    return call(
        kernel, "contract_back", grid, (T,), grid.info, [d_ffn, slope] + ws.operands,
        [fixed((S, D)), block] + ws.specs, (shape((S, FF), BF16), shape((8, FF), F32)),
        (block, pl.BlockSpec((8, cols), at)), ws.scratch, cost(2 * S * D * FF, 2 * D * FF + 4 * S * FF),
    )


def expand_back(grid, ws, d_hidden, d_two, n1, inv1, vec):
    T = grid.T
    S, D = n1.shape
    FF = d_hidden.shape[1]
    cols = FF // T

    def kernel(info, a, vecs, inv, n1_any, d_two_any, *rest):
        refs, rest = rest[: len(ws.specs)], rest[len(ws.specs) :]
        d_one, d_attn, d_attn_t, sums, w, sem, acc, n1_s, d_two_s, own_sem = rest
        rt = pl.program_id(0)
        more = [
            pltpu.make_async_copy(n1_any, n1_s, own_sem.at[0]),
            pltpu.make_async_copy(d_two_any, d_two_s, own_sem.at[1]),
        ]

        @pl.when(rt == 0)
        def _():
            ws.start(info, refs, w, sem)
            for copy in more:
                copy.start()

        ws.wait(info, refs, w, sem, rt, True)

        def product(add):
            for lo, n in chunks(D, WIDE // 2):
                got = nt_dot(a[...], w[rt, lo : lo + n, :])
                acc[:, lo : lo + n] = acc[:, lo : lo + n] + got if add else got

        pl.when(rt == 0)(lambda: product(False))
        pl.when(rt > 0)(lambda: product(True))

        @pl.when(rt == T - 1)
        def _():
            for copy in more:
                copy.wait()

            def step(at, carry):
                s_bias, s_gain, s_shift = carry
                n = n1_s[at, :]
                grad = d_two_s[at, :] + acc[at, :]
                d = normed_back(grad * vecs[1:2, :], n, inv[at, 0:1])
                d_one[at, :] = d
                d_attn[at, :] = d.astype(BF16)
                return s_bias + fold(d), s_gain + fold(grad * n), s_shift + fold(grad)

            zero = jnp.zeros((8, D), F32)
            found = row_loop(S, ROWS, step, (zero, zero, zero))
            found = [jnp.sum(f, axis=0, keepdims=True) for f in found]
            sums[...] = jnp.concatenate(found + [jnp.zeros((5, D), F32)], axis=0)
            turn(d_attn, d_attn_t)

    block = pl.BlockSpec((S, cols), lambda rt, info: (0, part(info, rt, T)))
    rows = fixed((S, D))
    return call(
        kernel, "expand_back", grid, (T,), grid.info, [d_hidden, vec, inv1, n1, d_two] + ws.operands,
        [block, fixed(vec.shape), fixed((S, 128)), ANY, ANY] + ws.specs,
        (shape((S, D), F32), shape((S, D), BF16), shape((D, S), BF16), shape((8, D), F32)),
        (rows, rows, fixed((D, S)), fixed((8, D))),
        ws.scratch + [pltpu.VMEM((S, D), F32)] * 3 + [pltpu.SemaphoreType.DMA((2,))],
        cost(2 * S * D * FF, 2 * D * FF + 2 * S * FF + 20 * S * D),
    )


def attend_out_back(grid, pieces, d_attn):
    T = grid.T
    S, D = d_attn.shape
    tile = D // T
    ws = Weights(grid, D, [(pieces, 3 * tile, tile, 0)])

    def kernel(info, x, *rest):
        refs, (out, w, sem) = rest[: len(ws.specs)], rest[len(ws.specs) :]
        rt = pl.program_id(0)

        @pl.when(rt == 0)
        def _():
            ws.start(info, refs, w, sem)

        ws.wait(info, refs, w, sem, rt, True)
        out[...] = dot(x[...], w[rt]).astype(BF16)

    cols = pl.BlockSpec((S, tile), lambda rt, info: (0, part(info, rt, T)))
    return call(
        kernel, "attend_out_back", grid, (T,), grid.info, [d_attn] + ws.operands, [fixed((S, D))] + ws.specs,
        shape((S, D), BF16), cols, ws.scratch, cost(2 * S * D * D, 2 * D * D + 4 * S * D),
    )


def project_back(grid, pieces, dq, dk, dv, d_one):
    T = grid.T
    S, D = d_one.shape
    tile = D // T
    ws = Weights(grid, D, [(pieces, 0, 3 * tile, 0)])

    def kernel(info, q, k, v, one, *rest):
        refs, (out, w, sem) = rest[: len(ws.specs)], rest[len(ws.specs) :]
        rt = pl.program_id(0)

        @pl.when(rt == 0)
        def _():
            ws.start(info, refs, w, sem)
            out[...] = one[...]

        ws.wait(info, refs, w, sem, rt, True)
        g = nt_dot(q[...], w[rt, :, :tile]) + nt_dot(k[...], w[rt, :, tile : 2 * tile])
        out[...] += g + nt_dot(v[...], w[rt, :, 2 * tile :])

    cols = pl.BlockSpec((S, tile), lambda rt, info: (0, part(info, rt, T)))
    return call(
        kernel, "project_back", grid, (T,), grid.info, [dq, dk, dv, d_one] + ws.operands,
        [cols, cols, cols, fixed((S, D))] + ws.specs, shape((S, D), F32), fixed((S, D)), ws.scratch,
        cost(6 * S * D * D, 6 * D * D + 14 * S * D),
    )


def weight_grad(grid, lefts, rights, core, received=None, line_first=False, parts=False):
    T, Z = grid.T, grid.Z
    D, S = lefts[0].shape
    R = D // grid.dp
    spans, width = [], 0
    for which, b, lo, count in rights:
        assert b.shape[1] // T % count == 0 and lo % count == 0
        spans.append((which, width, lo // count, count, b.shape[1] // T // count))
        width += count

    def kernel(info, *rest):
        left_refs = rest[: len(lefts)]
        right_refs = rest[len(lefts) : len(lefts) + len(rights)]
        rest = rest[len(lefts) + len(rights) :]
        got, rest = (rest[0], rest[1:]) if received is not None else (None, rest)
        *outs, rows = rest
        out, rt = outs[0], pl.program_id(0)

        @pl.when(pl.program_id(0) == 0)
        def _():
            for a in range(len(lefts)):
                for rx in range(2):
                    for z in range(Z):
                        at = (z * 4 + (info[1] ^ rx) * 2 + (info[2] ^ core)) * R
                        to = (z * 2 + rx if line_first else rx * Z + z) * R
                        rows[a, pl.ds(to, R), :] = left_refs[a][pl.ds(pl.multiple_of(at, R), R), :]

        for (which, start, _, count, _), right in zip(spans, right_refs):
            for lo, n in chunks(count, WIDE):
                to = pl.ds(start + lo, n)
                g = dot(rows[which], right[:, lo : lo + n])
                if not parts:
                    g = g.reshape(out.shape[:-1] + (n,))
                    if received is not None:
                        g = g + got[:, :, :, :, to].astype(F32)
                    out[:, :, :, :, to] = g.astype(BF16)
                    continue
                g = (g.reshape(got.shape[1:-1] + (n,)) + got[0, :, :, :, to].astype(F32)).astype(BF16)
                half = Z // 2

                @pl.when(rt == 0)
                def _(g=g, to=to):
                    outs[0][:, :, to] = g[0]
                    outs[1][:, :, to] = g[1, :half]
                    outs[2][:, :, to] = g[1, half:]

                @pl.when(rt == 1)
                def _(g=g, to=to):
                    outs[3][:, :, to] = g[0, :half]
                    outs[4][:, :, to] = g[0, half:]
                    outs[5][:, :, to] = g[1, :half]
                    outs[6][:, :, to] = g[1, half:]

    def right_map(which, start, first, count, every):
        return lambda rt, info: (0, part(info, rt, T) * every + first)

    if line_first:
        block = pl.BlockSpec((Z, 1, 2, R, width), lambda rt, info: (0, rt, 0, 0, 0))
        dims = (Z, T, 2, R, width)
    else:
        block = pl.BlockSpec((1, 2, Z, R, width), lambda rt, info: (rt, 0, 0, 0, 0))
        dims = (T, 2, Z, R, width)
    in_specs = [fixed((D, S)) for _ in lefts] + [pl.BlockSpec((S, s[3]), right_map(*s)) for s in spans]
    operands = list(lefts) + [r[1] for r in rights]
    if received is not None:
        in_specs.append(block)
        operands.append(received)
    out_shapes, out_specs = shape(dims, BF16), block
    if parts:
        sizes = [(Z, R, width)] + [(Z // 2, R, width)] * 6
        out_shapes, out_specs = tuple(shape(s, BF16) for s in sizes), tuple(fixed(s) for s in sizes)
    return call(
        kernel, "weight_grad", grid, (T,), grid.info, operands, in_specs, out_shapes, out_specs,
        [pltpu.VMEM((len(lefts), D // 2, S), BF16)],
        cost(D * S * width * T, 2 * S * width * T + (1 if received is None else 2) * D * width * T), 32,
    )


def attention_forward(q, k, v, seg_col, seg_row):
    S, D = q.shape
    pairs = D // (2 * HD)

    def kernel(q, k, v, col, row, ctx, probs, bias):
        @pl.when(pl.program_id(0) == 0)
        def _():
            bias[...] = jnp.where(col[...] == row[...], 0.0, MASKED)

        lane = lax.broadcasted_iota(jnp.int32, (S, 2 * HD), 1) < HD
        query = q[...] * jnp.asarray(0.125, BF16)
        zero = jnp.zeros_like(query)
        outs = []
        for h in range(2):
            mine = jnp.where(lane == (h == 0), query, zero)
            s = nt_dot(mine, k[...]) + bias[...]
            e = jnp.exp(s - jnp.max(s, axis=-1, keepdims=True))
            p = (e * (1.0 / jnp.sum(e, axis=-1, keepdims=True))).astype(BF16)
            probs[h] = p
            outs.append(dot(p, v[...]))
        ctx[...] = jnp.where(lane, outs[0], outs[1]).astype(BF16)

    rows = pl.BlockSpec((S, 2 * HD), lambda i: (0, i))
    return pl.pallas_call(
        kernel,
        grid=(pairs,),
        out_shape=(shape((S, D), BF16), shape((2 * pairs, S, S), BF16)),
        in_specs=[rows, rows, rows, fixed((S, 1)), fixed((1, S))],
        out_specs=(rows, pl.BlockSpec((2, S, S), lambda i: (i, 0, 0))),
        scratch_shapes=[pltpu.VMEM((S, S), F32)],
        cost_estimate=cost(16 * S * S * D, 8 * S * D + 4 * pairs * S * S, 2 * pairs * S * S),
        compiler_params=pltpu.CompilerParams(vmem_limit_bytes=24 << 20),
        name="attention_forward",
    )(q, k, v, seg_col, seg_row)


def attention_backward(q, k, v, ctx, d_ctx, probs):
    S, D = q.shape
    pairs = D // (2 * HD)

    def kernel(q, k, v, ctx, d_ctx, probs, dq, dk, dv, sums):
        lane = lax.broadcasted_iota(jnp.int32, (S, 2 * HD), 1) < HD
        grad = d_ctx[...]
        both = grad.astype(F32) * ctx[...].astype(F32)
        dqs, dks, dvs = [], [], []
        for h in range(2):
            mask = lane == (h == 0)
            inner = jnp.sum(jnp.where(mask, both, 0.0), axis=-1, keepdims=True)
            mine = jnp.where(mask, grad, jnp.zeros_like(grad))
            d_prob = nt_dot(mine, v[...])
            p = probs[h]
            ds = (p.astype(F32) * (d_prob - inner)).astype(BF16)
            dvs.append(lax.dot_general(p, grad, TN, preferred_element_type=F32))
            dqs.append(dot(ds, k[...]))
            dks.append(lax.dot_general(ds, q[...], TN, preferred_element_type=F32))
        a = (jnp.where(lane, dqs[0], dqs[1]) * 0.125).astype(BF16)
        b = jnp.where(lane, dvs[0], dvs[1]).astype(BF16)
        dq[...] = a
        dk[...] = (jnp.where(lane, dks[0], dks[1]) * 0.125).astype(BF16)
        dv[...] = b
        total_a = jnp.sum(a.astype(F32), axis=0, keepdims=True)
        total_b = jnp.sum(b.astype(F32), axis=0, keepdims=True)
        sums[...] = jnp.concatenate([total_a, total_b, jnp.zeros((6, 2 * HD), F32)], axis=0)

    rows = pl.BlockSpec((S, 2 * HD), lambda i: (0, i))
    out = shape((S, D), BF16)
    return pl.pallas_call(
        kernel,
        grid=(pairs,),
        out_shape=(out, out, out, shape((8, D), F32)),
        in_specs=[rows] * 5 + [pl.BlockSpec((2, S, S), lambda i: (i, 0, 0))],
        out_specs=(rows, rows, rows, pl.BlockSpec((8, 2 * HD), lambda i: (0, i))),
        cost_estimate=cost(32 * S * S * D, 16 * S * D + 4 * pairs * S * S),
        compiler_params=pltpu.CompilerParams(vmem_limit_bytes=24 << 20),
        name="attention_backward",
    )(q, k, v, ctx, d_ctx, probs)


def body(
    sizes,
    tokens,
    teacher,
    valid_mask,
    segments,
    loss_scale,
    qkv_weight,
    qv_bias,
    out_weight,
    out_bias,
    first_gain,
    first_shift,
    up_weight,
    up_bias,
    down_weight,
    down_bias,
    second_gain,
    second_shift,
):
    grid = Grid(*sizes)
    grid.here()
    T, dp = grid.T, grid.dp
    S, D = tokens.shape
    assert S == SEQ
    up_cols = up_weight.shape[1]
    FF = up_cols * T
    tile = D // T
    R = D // dp
    cut = up_cols // 2
    keep = valid_mask.astype(F32)

    down_rows = down_weight.T
    first_own = jnp.concatenate([qkv_weight[0], qkv_weight[1], qkv_weight[2], out_weight.T], axis=1)
    first_own = after(first_own)
    first, others = grid.gather(first_own, up_weight, down_weight.T, None)

    def placed(v):
        wide = lax.dynamic_update_slice_in_dim(jnp.zeros(v.shape[:-1] + (dp * v.shape[-1],), F32), v.astype(F32), grid.d * v.shape[-1], v.ndim - 1)
        out = jnp.zeros(v.shape[:-2] + (T,) + wide.shape[-2:], F32)
        return lax.dynamic_update_slice_in_dim(out, wide[..., None, :, :], grid.t, v.ndim - 2)

    eight = jnp.concatenate([jnp.stack([out_bias, first_gain, first_shift, down_bias, second_gain, second_shift]), qv_bias])
    packed = jnp.concatenate(
        [placed(after(eight, first_own)).reshape(-1, 128), placed(up_bias).reshape(-1, 128), jnp.full((8, 128), jnp.sum(keep))]
    )
    packed = grid.total_small(packed)
    n8, nu = 8 * D // 128, FF // 128
    vec = packed[:n8].reshape(8, D)
    up_b = packed[n8 : n8 + nu].reshape(1, FF)
    count_all = packed[n8 + nu, 0]
    norm_scale = count_all * D

    mine = lax.dynamic_slice_in_dim(segments, grid.t * S, S)
    q, k, v = project_qkv(grid, first, tokens, vec)
    ctx, probs = attention_forward(q, k, v, mine[:, None], mine[None, :])
    n1, inv1, first_low, first_low_t = attend_out(grid, first, ctx, tokens, vec)
    middle, last = others(q, ctx, first_low)
    up = Weights(grid, D, [(middle, 0, up_cols, 0)])
    down = Weights(grid, D, [(last, 0, up_cols, 0)])
    act, slope = expand(grid, up, first_low, up_b, FF)
    scales = (2.0 * loss_scale / norm_scale).reshape(1)
    out_low, d_two, d_ffn, d_ffn_t, sums_two = contract(grid, down, act, n1, vec, teacher, keep[:, None], scales)

    square = grid.square

    def grads(lefts, rights, line_first=False):
        theirs = weight_grad(grid, lefts, rights, 1, line_first=line_first)

        def ours(*wait):
            got = after(arriving, *wait)
            return weight_grad(grid, lefts, rights, 0, got, line_first, square and not line_first)

        arriving = grid.cs(theirs)
        return theirs, arriving, ours

    if square:
        start, middle_of, end = grid.plane_start, grid.plane_middle, grid.plane_end
    else:
        start, middle_of, end = lambda g: (g,), lambda g, found: (g,), lambda g, found, last: grid.general(g)

    sib_a, _, ours_a = grads([d_ffn_t], [(0, act, 0, cut)])
    sib_b, _, ours_b = grads([after(d_ffn_t, sib_a)], [(0, act, cut, cut)], True)
    a = ours_a(sib_b)
    a_found = start(a)
    b = ours_b(a[0])
    b_held = grid.line_hop(b, 1)
    d_hidden, sums_up = contract_back(grid, down, after(d_ffn, b), slope)
    sib_u, got_u, ours_u = grads([first_low_t], [(0, d_hidden, 0, up_cols)])
    a_last = middle_of(a, a_found)
    hidden = after(d_hidden, sib_u, *a_found)
    d_one, d_attn, d_attn_t, sums_one = expand_back(grid, up, hidden, d_two, n1, inv1, vec)
    a_own = end(a, a_found, a_last).astype(BF16)
    b_held = grid.line_hop(b, 2, b_held)
    u = ours_u(d_attn, *a_last)
    u_found = start(u)
    a_held = grid.line_hop(a_own, 1)
    d_ctx = attend_out_back(grid, first, after(d_attn, u[0]))
    dq, dk, dv, sums_qv = attention_backward(q, k, v, ctx, d_ctx, probs)
    u_last = middle_of(u, u_found)
    b_held = grid.line_hop(b, 3, b_held)
    sib_l, got_l, ours_l = grads(
        [tokens.T, after(d_attn_t, *u_found)], [(0, dq, 0, tile), (0, dk, 0, tile), (0, dv, 0, tile), (1, ctx, 0, tile)]
    )
    grad_tokens = project_back(grid, first, after(dq, sib_l), dk, dv, d_one)
    b_own = grid.line_end(b, b_held).astype(BF16)
    g_down_a = grid.line(a_own, a_held, 2)
    l = ours_l(grad_tokens, *u_last)
    l_found = start(l)
    g_up = grid.line(end(u, u_found, u_last).astype(BF16))
    g_first = grid.line(end(l, l_found, middle_of(l, l_found)).astype(BF16))
    g_down_b = grid.plane(grid.quarters(b_own)) if square else grid.general(b_own)

    found = jnp.concatenate(
        [
            jnp.concatenate([sums_one[0:3], sums_two[0:3], sums_qv[0:2]]).reshape(-1, 128),
            jnp.sum(sums_up, axis=0).reshape(-1, 128),
            jnp.full((8, 128), jnp.sum(sums_two[3])),
        ]
    )
    found = grid.total_small(found)

    def own(v, rows):
        v = lax.dynamic_slice_in_dim(v, grid.t * rows, rows, v.ndim - 2)
        return lax.dynamic_slice_in_dim(v, grid.d * (HD // dp), HD // dp, v.ndim - 1)

    g8 = own(found[:n8].reshape(8, D // HD, HD), D // HD // T)
    g_up_b = own(found[n8 : n8 + nu].reshape(FF // HD, HD), FF // HD // T)
    loss_value = found[n8 + nu, 0] / norm_scale
    g_down = jnp.concatenate([g_down_a, g_down_b], axis=1)
    return (
        out_low,
        loss_value,
        grad_tokens,
        g_first[:, : 3 * tile].reshape(R, 3, tile).transpose(1, 0, 2),
        g8[6:8],
        g_first[:, 3 * tile :].T,
        g8[0],
        g8[1],
        g8[2],
        g_up,
        g_up_b,
        g_down.T,
        g8[3],
        g8[4],
        g8[5],
    )


def solution(mesh):
    vector = P("tensor", "dp")
    rows = P(("dp", "tensor"), None)
    qkv, qv, cols = P(None, "dp", "tensor"), P(None, "tensor", "dp"), P("dp", "tensor")
    return jax.shard_map(
        functools.partial(body, (mesh.shape["dp"], mesh.shape["tensor"])),
        mesh=mesh,
        in_specs=(
            rows, rows, P(("dp", "tensor")), P("dp"), P(), qkv, qv, vector, vector, vector, vector, cols,
            vector, vector, vector, vector, vector,
        ),
        out_specs=(
            rows, P(), rows, qkv, qv, vector, vector, vector, vector, cols, vector, vector, vector, vector, vector,
        ),
        check_vma=False,
    )
```

```python
import functools
import math

import jax
import jax.numpy as jnp
from jax import lax
from jax.experimental import pallas as pl
from jax.experimental.pallas import tpu as pltpu
from jax.sharding import PartitionSpec as P

HD = 64
SEQ = 512
EPS = 1e-06
MASKED = -1e30
F32 = jnp.float32
BF16 = jnp.bfloat16
ANY = pl.BlockSpec(memory_space=pltpu.HBM)
NT = (((1,), (1,)), ((), ()))
TN = (((0,), (0,)), ((), ()))


def cost(flops, nbytes, trans=0):
    return pl.CostEstimate(flops=int(flops), bytes_accessed=int(nbytes), transcendentals=int(trans))


def nt_dot(a, b):
    return lax.dot_general(a, b, NT, preferred_element_type=F32)


def dot(a, b):
    return jnp.dot(a, b, preferred_element_type=F32)


def after(x, *others):
    return lax.optimization_barrier((x, *others))[0] if others else x


def add(a, b):
    return (a.astype(F32) + b.astype(F32)).astype(BF16)


def in_hbm(*arrays):
    kept = tuple(pltpu.with_memory_space_constraint(a, pltpu.HBM) for a in arrays)
    return kept if len(kept) > 1 else kept[0]


class Pieces:
    def __init__(self, parts):
        self.arrays = [a for a, _ in parts]
        self.places = [p for _, p in parts]


class Grid:
    def __init__(self, dp, tensor):
        self.dp, self.T, self.Z = dp, tensor, dp // 4
        assert dp == self.Z * 4
        Z = self.Z
        self.cycle = [0] + list(range(1, Z, 2)) + list(range(2, Z, 2))[::-1]
        self.place = [self.cycle.index(z) for z in range(Z)]
        after = {self.cycle[i]: self.cycle[(i + 1) % Z] for i in range(Z)}
        cells = [(z, x, c) for z in range(Z) for x in range(2) for c in range(2)]
        self.to_z = [(self.rank(z, x, c), self.rank(after[z], x, c)) for z, x, c in cells]
        self.to_x = [(self.rank(z, x, c), self.rank(z, 1 - x, c)) for z, x, c in cells]
        self.to_c = [(self.rank(z, x, c), self.rank(z, x, 1 - c)) for z, x, c in cells]
        self.to_t = [(t, (t + 1) % tensor) for t in range(tensor)]
        self.square = tensor == 2 and Z == 4

    @staticmethod
    def rank(z, x, c):
        return z * 4 + x * 2 + c

    def here(self):
        d = lax.axis_index("dp")
        self.d, self.z, self.x, self.c, self.t = d, d // 4, (d // 2) % 2, d % 2, lax.axis_index("tensor")
        back = []
        for k in range(self.Z):
            options = [self.cycle[(p - k) % self.Z] for p in self.place]
            back.append(sum(jnp.where(self.z == z, o, 0) for z, o in enumerate(options)))
        self.back = back
        self.info = jnp.stack([v.astype(jnp.int32) for v in [self.t, self.x, self.c, self.z] + back])

    def zs(self, a):
        return lax.ppermute(a, "dp", self.to_z)

    def xs(self, a):
        return lax.ppermute(a, "dp", self.to_x)

    def cs(self, a):
        return lax.ppermute(a, "dp", self.to_c)

    def ts(self, a):
        return lax.ppermute(a, "tensor", self.to_t)

    def both_cores(self, parts, late=(), *hold):
        twins = [(self.cs(a), [(t, x, 1, k) for t, x, _, k in places]) for a, places in parts]
        twins += [(self.cs(after(a, *hold)), [(t, x, 1, k) for t, x, _, k in places]) for a, places in late]
        return Pieces(parts + list(late) + twins)

    def gather_general(self, own):
        ring = [own]
        for _ in range(self.Z - 1):
            ring.append(self.zs(ring[-1]))
        line, slots = jnp.stack(ring), range(self.Z)
        parts = [(line, [(0, 0, 0, k) for k in slots]), (self.xs(line), [(0, 1, 0, k) for k in slots])]
        rows = line
        for rt in range(1, self.T):
            rows = self.ts(rows)
            parts.append((rows, [(rt, 0, 0, k) for k in slots]))
            parts.append((self.xs(rows), [(rt, 1, 0, k) for k in slots]))
        return self.both_cores(parts)

    def gather(self, first, middle, last, hold):
        if not self.square:
            whole = [self.gather_general(a) for a in (first, middle, last)]
            return whole[0], lambda *_: (whole[2].arrays[0], whole[2].arrays[0], lambda *_: (whole[1], lambda *_: whole[2]))
        half = last.shape[0] // 2
        a0, b0, d = first[None], middle, last
        d_x, d_t = self.xs(d), self.ts(d)
        a1 = self.zs(a0)
        a0_x, a0_t = self.xs(after(a0, d_x)), self.ts(after(a0, d_t))
        a2 = self.zs(after(a1, d_x, d_t))
        d_far = [self.xs(after(d_t[:half], a0_x)), self.ts(after(d_x[half:], a0_t))]
        a1_x, a1_t = self.xs(a1), self.ts(a1)
        a3 = self.zs(after(a2, a0_x, a0_t))
        b1 = self.zs(after(b0, a3, a1_x, a1_t, *d_far))
        a23 = jnp.concatenate([a2, a3])
        a23_x, a23_t = self.xs(a23), self.ts(a23)
        b2 = self.zs(b1)
        a_far = [self.xs(a0_t), self.xs(a1_t), self.ts(a23_x)]
        plane = jnp.stack([d, d_x, d_t, jnp.concatenate(d_far)])
        b3 = self.zs(after(b2, a23_x, a23_t))
        line = jnp.stack([b0, b1, b2, b3])
        p1 = self.zs(after(plane, b3))

        def at(t, x, *slots):
            return [(t, x, 0, k) for k in slots]

        a_parts = [
            (a0, at(0, 0, 0)), (a1, at(0, 0, 1)), (a23, at(0, 0, 2, 3)),
            (a0_x, at(0, 1, 0)), (a1_x, at(0, 1, 1)), (a23_x, at(0, 1, 2, 3)),
            (a0_t, at(1, 0, 0)), (a1_t, at(1, 0, 1)), (a23_t, at(1, 0, 2, 3)),
            (a_far[0], at(1, 1, 0)), (a_far[1], at(1, 1, 1)), (a_far[2], at(1, 1, 2, 3)),
        ]

        def others(ctx):
            b_x, b_t = self.xs(after(line, a_far[1])), self.ts(after(line, a_far[2]))
            p2 = self.zs(p1)
            b_far = [self.xs(after(b_t[:2], ctx)), self.ts(after(b_x[2:], ctx))]
            p3 = self.zs(p2)
            b_parts = [
                (line, at(0, 0, 0, 1, 2, 3)), (b_x, at(0, 1, 0, 1, 2, 3)), (b_t, at(1, 0, 0, 1, 2, 3)),
                (b_far[0], at(1, 1, 0, 1)), (b_far[1], at(1, 1, 2, 3)),
            ]
            d_parts = [
                (p, [(0, 0, 0, k), (0, 1, 0, k), (1, 0, 0, k), (1, 1, 0, k)]) for k, p in enumerate([plane, p1, p2, p3])
            ]

            def last_of(low):
                return self.both_cores(b_parts[:3], b_parts[3:], low), lambda act: self.both_cores(d_parts[:3], d_parts[3:], act)

            return p1, p2, last_of

        return self.both_cores(a_parts), others

    def total_small(self, v):
        v = v + self.cs(v)
        held = v
        for _ in range(1, self.Z):
            held = self.zs(held)
            v = v + held
        v = v + self.xs(v)
        held = v
        for _ in range(1, self.T):
            held = self.ts(held)
            v = v + held
        return v

    def line_block(self, own, step, held=None):
        block = lax.dynamic_index_in_dim(own, self.back[step], 0, keepdims=False)
        if held is not None:
            block = block.astype(F32) + held.astype(F32)
        return block.astype(BF16)

    def line_hop(self, own, step, held=None):
        return self.zs(self.line_block(own, step, held))

    def line_end(self, own, held):
        return lax.dynamic_index_in_dim(own, self.z, 0, keepdims=False).astype(F32) + held.astype(F32)

    def line(self, own, held=None, first=1):
        for step in range(first, self.Z):
            held = self.line_hop(own, step, held)
        return self.line_end(own, held)

    def plane_start(self, parts):
        return self.xs(parts[1]), self.ts(parts[3])

    def plane_middle(self, parts, found):
        half = parts[2].shape[0]
        return self.xs(add(parts[2], found[1][:half])), self.ts(add(parts[4], found[0][:half]))

    def plane_end(self, parts, found, last):
        half = parts[2].shape[0]
        own = after(parts[0], *last).astype(F32)
        low = own[:half] + found[0][half:].astype(F32) + last[1].astype(F32)
        high = own[half:] + last[0].astype(F32) + found[1][half:].astype(F32)
        return jnp.concatenate([low, high])

    def general(self, g):
        rows = g[:, 0].astype(F32) + self.xs(g[:, 1]).astype(F32)
        held = None
        for step in range(1, self.T):
            block = rows[(self.T - step) % self.T]
            if held is not None:
                block = block + held.astype(F32)
            held = self.ts(block.astype(BF16))
        return rows[0] + held.astype(F32)


class Weights:
    def __init__(self, grid, D, sources):
        self.T, self.D, self.R = grid.T, D, D // grid.dp
        self.sources = sources
        self.width = sum(s[2] for s in sources)
        seen = []
        for pieces, *_ in sources:
            if pieces not in seen:
                seen.append(pieces)
        self.operands = [pltpu.with_memory_space_constraint(a, pltpu.HBM) for pieces in seen for a in pieces.arrays]
        self.first = {id(p): sum(len(q.arrays) for q in seen[:i]) for i, p in enumerate(seen)}
        self.specs = [ANY] * len(self.operands)
        self.scratch = [pltpu.VMEM((self.T, D, self.width), BF16), pltpu.SemaphoreType.DMA((self.T,))]

    def copies(self, info, refs, w, sem, want):
        out = []
        for pieces, lo, count, to in self.sources:
            base = self.first[id(pieces)]
            for i, places in enumerate(pieces.places):
                for entry, (rt, rx, rc, k) in enumerate(places):
                    if rt != want:
                        continue
                    row = (info[4 + k] * 4 + (info[1] ^ rx) * 2 + (info[2] ^ rc)) * self.R
                    src = refs[base + i].at[entry, :, pl.ds(lo, count)]
                    dst = w.at[rt, pl.ds(pl.multiple_of(row, self.R), self.R), pl.ds(to, count)]
                    out.append(pltpu.make_async_copy(src, dst, sem.at[rt]))
        return out

    def start(self, info, refs, w, sem):
        for rt in range(self.T):
            for copy in self.copies(info, refs, w, sem, rt):
                copy.start()

    def wait(self, info, refs, w, sem, rt, first):
        for want in range(self.T):

            @pl.when((rt == want) & first)
            def _(want=want):
                for copy in self.copies(info, refs, w, sem, want):
                    copy.wait()


def pack(grid, qkv_weight, out_rows, vectors, qv_bias, up_bias, valid_mask):
    R, tile = out_rows.shape
    w, h = vectors[0].shape
    S = valid_mask.shape[0]

    def kernel(info, qkv, out_w, mask, *rest):
        *items, qv, up, out, held = rest
        for i in range(3):
            out[:, i * tile : (i + 1) * tile] = qkv[i]
        out[:, 3 * tile : 4 * tile] = out_w[...]
        held[...] = jnp.zeros_like(held)
        d = info[3] * 4 + info[1] * 2 + info[2]
        lane = lax.broadcasted_iota(jnp.int32, (w, 128), 1) - lax.broadcasted_iota(jnp.int32, (w, 128), 0)
        low, high = (jnp.where(lane == d * w + add, 1.0, 0.0).astype(BF16) for add in (0, HD))
        at = 0
        for item in [v[...] for v in items] + [qv[0], qv[1], up[...]]:
            rows = item.shape[1]
            pick = lax.broadcasted_iota(jnp.int32, (rows // 2, rows), 1) - 2 * lax.broadcasted_iota(jnp.int32, (rows // 2, rows), 0)
            even, odd = (jnp.where(pick == k, 1.0, 0.0).astype(BF16) for k in (0, 1))
            wide = [lax.dot_general(item, e, TN, preferred_element_type=F32).astype(BF16) for e in (low, high)]
            held[at : at + rows // 2, :] = dot(even, wide[0]) + dot(odd, wide[1])
            at += rows // 2
        count = jnp.sum(mask[...].astype(F32), axis=1, keepdims=True).astype(jnp.int32)
        rest_of = jnp.bitwise_and(count, 15)
        held[at : at + 1, :] = jnp.broadcast_to((count - rest_of).astype(F32), (1, 128))
        held[at + 1 : at + 2, :] = jnp.broadcast_to(rest_of.astype(F32), (1, 128))
        out[:, 4 * tile :] = held[...].astype(BF16)

    operands = list(in_hbm(qkv_weight, out_rows, valid_mask.reshape(1, S), *vectors, qv_bias, up_bias))
    return call(
        kernel, "pack", grid, (1,), grid.info, operands, [fixed(a.shape) for a in operands],
        shape((R, 4 * tile + 128), BF16), fixed((R, 4 * tile + 128)), [pltpu.VMEM((R, 128), F32)],
        cost(0, 4 * R * 4 * tile), 16,
    )


def unpack(grid, pieces, first, rows):
    T, Z = grid.T, grid.Z
    arrays = [pltpu.with_memory_space_constraint(a, pltpu.HBM) for a in pieces.arrays]
    places = [(i, j, p) for i, ps in enumerate(pieces.places) for j, p in enumerate(ps)]

    def kernel(info, *rest):
        refs, (out, held, sem) = rest[: len(arrays)], rest[len(arrays) :]
        copies = [
            pltpu.make_async_copy(refs[i].at[j, :rows, pl.ds(first, 128)], held.at[n], sem)
            for n, (i, j, _) in enumerate(places)
        ]
        for copy in copies:
            copy.start()
        for copy in copies:
            copy.wait()
        for rt in range(T):
            mine = [n for n, (_, _, p) in enumerate(places) if p[0] == rt]
            total = held[mine[0]].astype(F32)
            for n in mine[1:]:
                total = total + held[n].astype(F32)
            out[pl.ds(part(info, rt, T), 1)] = total[None]

    return call(
        kernel, "unpack", grid, (1,), grid.info, arrays, [ANY] * len(arrays), shape((T, rows, 128), F32),
        fixed((T, rows, 128)), [pltpu.VMEM((len(places), rows, 128), BF16), pltpu.SemaphoreType.DMA],
        cost(0, 4 * len(places) * rows * 128), 16,
    )


def part(info, rt, T):
    return lax.rem(info[0] - rt + T, T)


def call(kernel, name, grid, steps, info, operands, in_specs, outs, out_specs, scratch, estimate, mib=36):
    return pl.pallas_call(
        kernel,
        out_shape=outs,
        grid_spec=pltpu.PrefetchScalarGridSpec(
            num_scalar_prefetch=1, grid=steps, in_specs=in_specs, out_specs=out_specs, scratch_shapes=scratch
        ),
        cost_estimate=estimate,
        compiler_params=pltpu.CompilerParams(vmem_limit_bytes=mib << 20),
        name=name,
    )(info, *operands)


def shape(dims, dtype):
    return jax.ShapeDtypeStruct(dims, dtype)


def shape_hbm(dims, dtype):
    return pltpu.HBM(dims, dtype)


def fixed(dims):
    return pl.BlockSpec(dims, lambda *_: (0,) * len(dims))


def project_qkv(grid, pieces, tokens, vec):
    T = grid.T
    S, D = tokens.shape
    tile = D // T
    ws = Weights(grid, D, [(pieces, 0, 3 * tile, 0)])

    def kernel(info, x, bias, *rest):
        refs, (q, k, v, w, sem) = rest[: len(ws.specs)], rest[len(ws.specs) :]
        rt = pl.program_id(0)

        @pl.when(rt == 0)
        def _():
            ws.start(info, refs, w, sem)

        ws.wait(info, refs, w, sem, rt, True)
        a, mine = x[...], w.at[rt]
        q[...] = (dot(a, mine[:, :tile]) + bias[6:7, :]).astype(BF16)
        k[...] = dot(a, mine[:, tile : 2 * tile]).astype(BF16)
        v[...] = (dot(a, mine[:, 2 * tile :]) + bias[7:8, :]).astype(BF16)

    cols = pl.BlockSpec((S, tile), lambda rt, info: (0, part(info, rt, T)))
    biases = pl.BlockSpec((vec.shape[0], tile), lambda rt, info: (0, part(info, rt, T)))
    out = shape((S, D), BF16)
    return call(
        kernel, "project_qkv", grid, (T,), grid.info, [tokens, vec] + ws.operands, [fixed((S, D)), biases] + ws.specs,
        (out, out, out), (cols, cols, cols), ws.scratch, cost(6 * S * D * D, 6 * D * D + 8 * S * D),
    )


def row_loop(S, rows, step, start):
    return lax.fori_loop(0, S // rows, lambda i, carry: step(pl.ds(pl.multiple_of(i * rows, rows), rows), carry), start)


def fold(a):
    return jnp.sum(a.reshape(a.shape[0] // 8, 8, a.shape[1]), axis=0)


def turn(src, dst):
    S = src.shape[0]

    def step(i, _):
        at = pl.ds(pl.multiple_of(i * 128, 128), 128)
        dst[:, at] = src[at, :].T
        return 0

    lax.fori_loop(0, S // 128, step, 0)


def normed(r):
    c = r - jnp.mean(r, axis=-1, keepdims=True)
    inv = lax.rsqrt(jnp.mean(c * c, axis=-1, keepdims=True) + EPS)
    return c * inv, inv


def normed_back(d, n, inv):
    return (d - jnp.mean(d, axis=-1, keepdims=True) - n * jnp.mean(d * n, axis=-1, keepdims=True)) * inv


ROWS = 128


def attend_out(grid, pieces, ctx, tokens, vec):
    T = grid.T
    S, D = tokens.shape
    tile = D // T
    ws = Weights(grid, D, [(pieces, 3 * tile, tile, 0)])

    def kernel(info, c, x, vecs, *rest):
        refs, (n1, inv1, low, low_t, w, sem, acc) = rest[: len(ws.specs)], rest[len(ws.specs) :]
        rt = pl.program_id(0)

        @pl.when(rt == 0)
        def _():
            ws.start(info, refs, w, sem)
            acc[...] = jnp.zeros_like(acc)

        ws.wait(info, refs, w, sem, rt, True)
        acc[...] += nt_dot(c[...], w[rt])

        @pl.when(rt == T - 1)
        def _():
            def step(at, carry):
                n, inv = normed(x[at, :].astype(F32) + (acc[at, :] + vecs[0:1, :]))
                n1[at, :] = n
                inv1[at, :] = jnp.broadcast_to(inv, (ROWS, 128))
                low[at, :] = (n * vecs[1:2, :] + vecs[2:3, :]).astype(BF16)
                return carry

            row_loop(S, ROWS, step, 0)
            turn(low, low_t)

    cols = pl.BlockSpec((S, tile), lambda rt, info: (0, part(info, rt, T)))
    return call(
        kernel, "attend_out", grid, (T,), grid.info, [ctx, tokens, vec] + ws.operands,
        [cols, fixed((S, D)), fixed(vec.shape)] + ws.specs,
        (shape_hbm((S, D), F32), shape((S, 128), F32), shape((S, D), BF16), shape((D, S), BF16)),
        (fixed((S, D)), fixed((S, 128)), fixed((S, D)), fixed((D, S))),
        ws.scratch + [pltpu.VMEM((S, D), F32)], cost(2 * S * D * D, 2 * D * D + 12 * S * D),
    )


def chunks(width, size):
    return [(lo, min(size, width - lo)) for lo in range(0, width, size)]


WIDE = 1024


def expand(grid, ws, low, up_b, FF):
    T = grid.T
    S, D = low.shape
    cols = FF // T

    def kernel(info, x, b, *rest):
        refs, (act, slope, w, sem) = rest[: len(ws.specs)], rest[len(ws.specs) :]
        rt = pl.program_id(0)

        @pl.when(rt == 0)
        def _():
            ws.start(info, refs, w, sem)

        ws.wait(info, refs, w, sem, rt, True)
        for lo, n in chunks(cols, WIDE // 2):
            u = dot(x[...], w[rt, :, lo : lo + n]) + b[:, lo : lo + n]
            cdf = 0.5 * (1.0 + lax.erf(u * (2.0**-0.5)))
            act[:, lo : lo + n] = (u * cdf).astype(BF16)
            slope[:, lo : lo + n] = (cdf + u * (jnp.exp(-0.5 * u * u) * 0.3989422804014327)).astype(BF16)

    def at(rt, info):
        return (0, part(info, rt, T))

    block = pl.BlockSpec((S, cols), at)
    out = shape((S, FF), BF16)
    return call(
        kernel, "expand", grid, (T,), grid.info, [low, up_b] + ws.operands,
        [fixed((S, D)), pl.BlockSpec((1, cols), at)] + ws.specs, (out, shape_hbm((S, FF), BF16)), (block, block), ws.scratch,
        cost(2 * S * D * FF, 2 * D * FF + 4 * S * FF, 2 * S * FF),
    )


def contract(grid, ws, act, n1, vec, teacher, keep, scales):
    T = grid.T
    S, D = n1.shape
    FF = act.shape[1]
    cols = FF // T

    def kernel(info, scale, a, vecs, kept, n1_any, teacher_any, *rest):
        refs, rest = rest[: len(ws.specs)], rest[len(ws.specs) :]
        low, d_two, d_ffn, d_ffn_t, sums, w, sem, acc, n1_s, teacher_s, own_sem = rest
        rt = pl.program_id(0)
        more = [
            pltpu.make_async_copy(n1_any, n1_s, own_sem.at[0]),
            pltpu.make_async_copy(teacher_any, teacher_s, own_sem.at[1]),
        ]

        @pl.when(rt == 0)
        def _():
            ws.start(info, refs, w, sem)
            for copy in more:
                copy.start()

        ws.wait(info, refs, w, sem, rt, True)

        def product(add):
            for lo, n in chunks(D, WIDE // 2):
                got = nt_dot(a[...], w[rt, lo : lo + n, :])
                acc[:, lo : lo + n] = acc[:, lo : lo + n] + got if add else got

        pl.when(rt == 0)(lambda: product(False))
        pl.when(rt > 0)(lambda: product(True))

        @pl.when(rt == T - 1)
        def _():
            for copy in more:
                copy.wait()

            def step(at, carry):
                s_bias, s_gain, s_shift, s_loss = carry
                first = n1_s[at, :] * vecs[1:2, :] + vecs[2:3, :]
                n, inv = normed(first + (acc[at, :] + vecs[3:4, :]))
                out = n * vecs[4:5, :] + vecs[5:6, :]
                low[at, :] = out.astype(BF16)
                error = out - teacher_s[at, :]
                weighed = kept[at, :] * error
                grad = scale[0] * weighed
                d = normed_back(grad * vecs[4:5, :], n, inv)
                d_two[at, :] = d
                d_ffn[at, :] = d.astype(BF16)
                return (
                    s_bias + fold(d), s_gain + fold(grad * n), s_shift + fold(grad), s_loss + fold(weighed * error),
                )

            zero = jnp.zeros((8, D), F32)
            found = row_loop(S, ROWS, step, (zero, zero, zero, zero))
            found = [jnp.sum(f, axis=0, keepdims=True) for f in found]
            sums[...] = jnp.concatenate(found + [jnp.zeros((4, D), F32)], axis=0)
            turn(d_ffn, d_ffn_t)

    block = pl.BlockSpec((S, cols), lambda rt, info: (0, part(info, rt, T)))
    rows = fixed((S, D))
    return call(
        kernel, "contract", grid, (T,), grid.info, [scales, act, vec, keep, *in_hbm(n1, teacher)] + ws.operands,
        [pl.BlockSpec(memory_space=pltpu.SMEM), block, fixed(vec.shape), fixed((S, 1)), ANY, ANY] + ws.specs,
        (shape_hbm((S, D), BF16), shape_hbm((S, D), F32), shape((S, D), BF16), shape((D, S), BF16), shape((8, D), F32)),
        (rows, rows, rows, fixed((D, S)), fixed((8, D))),
        ws.scratch + [pltpu.VMEM((S, D), F32)] * 3 + [pltpu.SemaphoreType.DMA((2,))],
        cost(2 * S * D * FF, 2 * D * FF + 2 * S * FF + 20 * S * D),
    )


def contract_back(grid, ws, d_ffn, slope):
    T = grid.T
    S, D = d_ffn.shape
    FF = slope.shape[1]
    cols = FF // T

    def kernel(info, x, s, *rest):
        refs, (out, sums, w, sem) = rest[: len(ws.specs)], rest[len(ws.specs) :]
        rt = pl.program_id(0)

        @pl.when(rt == 0)
        def _():
            ws.start(info, refs, w, sem)

        ws.wait(info, refs, w, sem, rt, True)
        for lo, n in chunks(cols, WIDE):
            d = dot(x[...], w[rt, :, lo : lo + n]) * s[:, lo : lo + n].astype(F32)
            d = d.astype(BF16)
            out[:, lo : lo + n] = d
            sums[:, lo : lo + n] = fold(d.astype(F32))

    def at(rt, info):
        return (0, part(info, rt, T))

    block = pl.BlockSpec((S, cols), at)
    return call(
        kernel, "contract_back", grid, (T,), grid.info, [d_ffn, in_hbm(slope)] + ws.operands,
        [fixed((S, D)), block] + ws.specs, (shape((S, FF), BF16), shape((8, FF), F32)),
        (block, pl.BlockSpec((8, cols), at)), ws.scratch, cost(2 * S * D * FF, 2 * D * FF + 4 * S * FF),
    )


def expand_back(grid, ws, d_hidden, d_two, n1, inv1, vec):
    T = grid.T
    S, D = n1.shape
    FF = d_hidden.shape[1]
    cols = FF // T

    def kernel(info, a, vecs, inv, n1_any, d_two_any, *rest):
        refs, rest = rest[: len(ws.specs)], rest[len(ws.specs) :]
        d_one, d_attn, d_attn_t, sums, w, sem, acc, n1_s, d_two_s, own_sem = rest
        rt = pl.program_id(0)
        more = [
            pltpu.make_async_copy(n1_any, n1_s, own_sem.at[0]),
            pltpu.make_async_copy(d_two_any, d_two_s, own_sem.at[1]),
        ]

        @pl.when(rt == 0)
        def _():
            ws.start(info, refs, w, sem)
            for copy in more:
                copy.start()

        ws.wait(info, refs, w, sem, rt, True)

        def product(add):
            for lo, n in chunks(D, WIDE // 2):
                got = nt_dot(a[...], w[rt, lo : lo + n, :])
                acc[:, lo : lo + n] = acc[:, lo : lo + n] + got if add else got

        pl.when(rt == 0)(lambda: product(False))
        pl.when(rt > 0)(lambda: product(True))

        @pl.when(rt == T - 1)
        def _():
            for copy in more:
                copy.wait()

            def step(at, carry):
                s_bias, s_gain, s_shift = carry
                n = n1_s[at, :]
                grad = d_two_s[at, :] + acc[at, :]
                d = normed_back(grad * vecs[1:2, :], n, inv[at, 0:1])
                d_one[at, :] = d
                d_attn[at, :] = d.astype(BF16)
                return s_bias + fold(d), s_gain + fold(grad * n), s_shift + fold(grad)

            zero = jnp.zeros((8, D), F32)
            found = row_loop(S, ROWS, step, (zero, zero, zero))
            found = [jnp.sum(f, axis=0, keepdims=True) for f in found]
            sums[...] = jnp.concatenate(found + [jnp.zeros((5, D), F32)], axis=0)
            turn(d_attn, d_attn_t)

    block = pl.BlockSpec((S, cols), lambda rt, info: (0, part(info, rt, T)))
    rows = fixed((S, D))
    return call(
        kernel, "expand_back", grid, (T,), grid.info, [d_hidden, vec, inv1, *in_hbm(n1, d_two)] + ws.operands,
        [block, fixed(vec.shape), fixed((S, 128)), ANY, ANY] + ws.specs,
        (shape_hbm((S, D), F32), shape((S, D), BF16), shape((D, S), BF16), shape((8, D), F32)),
        (rows, rows, fixed((D, S)), fixed((8, D))),
        ws.scratch + [pltpu.VMEM((S, D), F32)] * 3 + [pltpu.SemaphoreType.DMA((2,))],
        cost(2 * S * D * FF, 2 * D * FF + 2 * S * FF + 20 * S * D),
    )


def attend_out_back(grid, pieces, d_attn):
    T = grid.T
    S, D = d_attn.shape
    tile = D // T
    ws = Weights(grid, D, [(pieces, 3 * tile, tile, 0)])

    def kernel(info, x, *rest):
        refs, (out, w, sem) = rest[: len(ws.specs)], rest[len(ws.specs) :]
        rt = pl.program_id(0)

        @pl.when(rt == 0)
        def _():
            ws.start(info, refs, w, sem)

        ws.wait(info, refs, w, sem, rt, True)
        out[...] = dot(x[...], w[rt]).astype(BF16)

    cols = pl.BlockSpec((S, tile), lambda rt, info: (0, part(info, rt, T)))
    return call(
        kernel, "attend_out_back", grid, (T,), grid.info, [d_attn] + ws.operands, [fixed((S, D))] + ws.specs,
        shape((S, D), BF16), cols, ws.scratch, cost(2 * S * D * D, 2 * D * D + 4 * S * D),
    )


def project_back(grid, pieces, dq, dk, dv, d_one):
    T = grid.T
    S, D = d_one.shape
    tile = D // T
    ws = Weights(grid, D, [(pieces, 0, 3 * tile, 0)])

    def kernel(info, q, k, v, one, *rest):
        refs, (out, w, sem) = rest[: len(ws.specs)], rest[len(ws.specs) :]
        rt = pl.program_id(0)

        @pl.when(rt == 0)
        def _():
            ws.start(info, refs, w, sem)
            out[...] = one[...]

        ws.wait(info, refs, w, sem, rt, True)
        g = nt_dot(q[...], w[rt, :, :tile]) + nt_dot(k[...], w[rt, :, tile : 2 * tile])
        out[...] += g + nt_dot(v[...], w[rt, :, 2 * tile :])

    cols = pl.BlockSpec((S, tile), lambda rt, info: (0, part(info, rt, T)))
    return call(
        kernel, "project_back", grid, (T,), grid.info, [dq, dk, dv, in_hbm(d_one)] + ws.operands,
        [cols, cols, cols, fixed((S, D))] + ws.specs, shape((S, D), F32), fixed((S, D)), ws.scratch,
        cost(6 * S * D * D, 6 * D * D + 14 * S * D),
    )


def weight_grad(grid, lefts, rights, core, received=None, line_first=False, parts=False):
    T, Z = grid.T, grid.Z
    D, S = lefts[0].shape
    R = D // grid.dp
    spans, width = [], 0
    for which, b, lo, count in rights:
        unit = math.gcd(lo, count, b.shape[1] // T)
        spans += [(which, width + i, (lo + i) // unit, unit, b.shape[1] // T // unit, b) for i in range(0, count, unit)]
        width += count

    def kernel(info, *rest):
        left_refs = rest[: len(lefts)]
        right_refs = rest[len(lefts) : len(lefts) + len(spans)]
        rest = rest[len(lefts) + len(spans) :]
        got, rest = (rest[0], rest[1:]) if received is not None else (None, rest)
        *outs, rows = rest
        out, rt = outs[0], pl.program_id(0)

        @pl.when(pl.program_id(0) == 0)
        def _():
            for a in range(len(lefts)):
                for rx in range(2):
                    for z in range(Z):
                        at = (z * 4 + (info[1] ^ rx) * 2 + (info[2] ^ core)) * R
                        to = (z * 2 + rx if line_first else rx * Z + z) * R
                        rows[a, pl.ds(to, R), :] = left_refs[a][pl.ds(pl.multiple_of(at, R), R), :]

        for (which, start, _, count, *_), right in zip(spans, right_refs):
            for lo, n in chunks(count, WIDE):
                to = pl.ds(start + lo, n)
                g = dot(rows[which], right[:, lo : lo + n])
                if not parts:
                    g = g.reshape(out.shape[:-1] + (n,))
                    if received is not None:
                        g = g + got[:, :, :, :, to].astype(F32)
                    out[:, :, :, :, to] = g.astype(BF16)
                    continue
                g = (g.reshape(got.shape[1:-1] + (n,)) + got[0, :, :, :, to].astype(F32)).astype(BF16)
                half = Z // 2

                @pl.when(rt == 0)
                def _(g=g, to=to):
                    outs[0][:, :, to] = g[0]
                    outs[1][half:, :, to] = g[1, :half]
                    outs[2][:, :, to] = g[1, half:]

                @pl.when(rt == 1)
                def _(g=g, to=to):
                    outs[1][:half, :, to] = g[1, :half]
                    outs[3][:half, :, to] = g[1, half:]
                    outs[3][half:, :, to] = g[0, half:]
                    outs[4][:, :, to] = g[0, :half]

    def right_map(which, start, first, count, every, b):
        return lambda rt, info: (0, part(info, rt, T) * every + first)

    if line_first:
        block = pl.BlockSpec((Z, 1, 2, R, width), lambda rt, info: (0, rt, 0, 0, 0))
        dims = (Z, T, 2, R, width)
    else:
        block = pl.BlockSpec((1, 2, Z, R, width), lambda rt, info: (rt, 0, 0, 0, 0))
        dims = (T, 2, Z, R, width)
    in_specs = [fixed((D, S)) for _ in lefts] + [pl.BlockSpec((S, s[3]), right_map(*s)) for s in spans]
    operands = list(lefts) + [s[5] for s in spans]
    if received is not None:
        in_specs.append(block)
        operands.append(received)
    out_shapes, out_specs = shape(dims, BF16), block
    if parts:
        sizes = [(Z, R, width), (Z, R, width), (Z // 2, R, width), (Z, R, width), (Z // 2, R, width)]
        out_shapes, out_specs = tuple(shape(s, BF16) for s in sizes), tuple(fixed(s) for s in sizes)
    return call(
        kernel, "weight_grad", grid, (T,), grid.info, operands, in_specs, out_shapes, out_specs,
        [pltpu.VMEM((len(lefts), D // 2, S), BF16)],
        cost(D * S * width * T, 2 * S * width * T + (1 if received is None else 2) * D * width * T), 32,
    )


def attention_forward(q, k, v, seg_col, seg_row):
    S, D = q.shape
    pairs = D // (2 * HD)

    def kernel(q, k, v, col, row, ctx, probs, bias):
        @pl.when(pl.program_id(0) == 0)
        def _():
            bias[...] = jnp.where(col[...] == row[...], 0.0, MASKED)

        lane = lax.broadcasted_iota(jnp.int32, (S, 2 * HD), 1) < HD
        query = q[...] * jnp.asarray(0.125, BF16)
        zero = jnp.zeros_like(query)
        outs = []
        for h in range(2):
            mine = jnp.where(lane == (h == 0), query, zero)
            s = nt_dot(mine, k[...]) + bias[...]
            e = jnp.exp(s - jnp.max(s, axis=-1, keepdims=True))
            p = (e * (1.0 / jnp.sum(e, axis=-1, keepdims=True))).astype(BF16)
            probs[h] = p
            outs.append(dot(p, v[...]))
        ctx[...] = jnp.where(lane, outs[0], outs[1]).astype(BF16)

    rows = pl.BlockSpec((S, 2 * HD), lambda i: (0, i))
    return pl.pallas_call(
        kernel,
        grid=(pairs,),
        out_shape=(shape((S, D), BF16), shape_hbm((2 * pairs, S, S), BF16)),
        in_specs=[rows, rows, rows, fixed((S, 1)), fixed((1, S))],
        out_specs=(rows, pl.BlockSpec((2, S, S), lambda i: (i, 0, 0))),
        scratch_shapes=[pltpu.VMEM((S, S), F32)],
        cost_estimate=cost(16 * S * S * D, 8 * S * D + 4 * pairs * S * S, 2 * pairs * S * S),
        compiler_params=pltpu.CompilerParams(vmem_limit_bytes=24 << 20),
        name="attention_forward",
    )(q, k, v, seg_col, seg_row)


def attention_backward(q, k, v, ctx, d_ctx, probs):
    S, D = q.shape
    pairs = D // (2 * HD)

    def kernel(q, k, v, ctx, d_ctx, probs, dq, dk, dv, sums):
        lane = lax.broadcasted_iota(jnp.int32, (S, 2 * HD), 1) < HD
        grad = d_ctx[...]
        both = grad.astype(F32) * ctx[...].astype(F32)
        dqs, dks, dvs = [], [], []
        for h in range(2):
            mask = lane == (h == 0)
            inner = jnp.sum(jnp.where(mask, both, 0.0), axis=-1, keepdims=True)
            mine = jnp.where(mask, grad, jnp.zeros_like(grad))
            d_prob = nt_dot(mine, v[...])
            p = probs[h]
            ds = (p.astype(F32) * (d_prob - inner)).astype(BF16)
            dvs.append(lax.dot_general(p, grad, TN, preferred_element_type=F32))
            dqs.append(dot(ds, k[...]))
            dks.append(lax.dot_general(ds, q[...], TN, preferred_element_type=F32))
        a = (jnp.where(lane, dqs[0], dqs[1]) * 0.125).astype(BF16)
        b = jnp.where(lane, dvs[0], dvs[1]).astype(BF16)
        dq[...] = a
        dk[...] = (jnp.where(lane, dks[0], dks[1]) * 0.125).astype(BF16)
        dv[...] = b
        total_a = jnp.sum(a.astype(F32), axis=0, keepdims=True)
        total_b = jnp.sum(b.astype(F32), axis=0, keepdims=True)
        sums[...] = jnp.concatenate([total_a, total_b, jnp.zeros((6, 2 * HD), F32)], axis=0)

    rows = pl.BlockSpec((S, 2 * HD), lambda i: (0, i))
    out = shape((S, D), BF16)
    return pl.pallas_call(
        kernel,
        grid=(pairs,),
        out_shape=(out, out, out, shape((8, D), F32)),
        in_specs=[rows] * 5 + [pl.BlockSpec((2, S, S), lambda i: (i, 0, 0))],
        out_specs=(rows, rows, rows, pl.BlockSpec((8, 2 * HD), lambda i: (0, i))),
        cost_estimate=cost(32 * S * S * D, 16 * S * D + 4 * pairs * S * S),
        compiler_params=pltpu.CompilerParams(vmem_limit_bytes=24 << 20),
        name="attention_backward",
    )(q, k, v, ctx, d_ctx, in_hbm(probs))


def body(
    sizes,
    tokens,
    teacher,
    valid_mask,
    segments,
    loss_scale,
    qkv_weight,
    qv_bias,
    out_weight,
    out_bias,
    first_gain,
    first_shift,
    up_weight,
    up_bias,
    down_weight,
    down_bias,
    second_gain,
    second_shift,
):
    grid = Grid(*sizes)
    grid.here()
    T, dp = grid.T, grid.dp
    S, D = tokens.shape
    assert S == SEQ
    up_cols = up_weight.shape[1]
    FF = up_cols * T
    tile = D // T
    R = D // dp
    cut = up_cols // 2
    keep = valid_mask.astype(F32)

    down_rows = down_weight.T
    down_rows = down_weight.T
    part_of = up_cols - up_cols // 4
    last_own = after(down_rows[:, :part_of])
    vectors = [out_bias, first_gain, first_shift, down_bias, second_gain, second_shift]
    first_own = pack(
        grid, after(qkv_weight, last_own), out_weight.T, [v.T for v in vectors], qv_bias.transpose(0, 2, 1), up_bias.T, valid_mask
    )
    n8, nu = 8 * D // 128, FF // 128
    used = n8 // T + nu // T + 2
    assert used <= R
    middle_own = jnp.concatenate([up_weight, down_rows[:, part_of:]], axis=1)
    first, others = grid.gather(first_own, middle_own, last_own, None)
    table = unpack(grid, first, 4 * tile, R)
    vec = table[:, : n8 // T].reshape(T, 8, tile).transpose(1, 0, 2).reshape(8, D)
    up_b = table[:, n8 // T : n8 // T + nu // T].reshape(1, FF)
    count_all = jnp.sum(table[:, used - 2 : used, 0])
    norm_scale = count_all * D

    mine = lax.dynamic_slice_in_dim(segments, grid.t * S, S)
    tokens_t = tokens.T
    q, k, v = project_qkv(grid, first, after(tokens, tokens_t), vec)
    ctx, probs = attention_forward(q, k, v, mine[:, None], mine[None, :])
    sent, sent_next, middle_of = others(ctx)
    n1, inv1, first_low, first_low_t = attend_out(grid, first, after(ctx, sent), tokens, vec)
    middle, last_of = middle_of(first_low)
    up = Weights(grid, D, [(middle, 0, up_cols, 0)])
    act, slope = expand(grid, up, after(first_low, sent_next), up_b, FF)
    down = Weights(grid, D, [(last_of(act), 0, part_of, 0), (middle, up_cols, up_cols - part_of, part_of)])
    scales = (2.0 * loss_scale / norm_scale).reshape(1)
    out_low, d_two, d_ffn, d_ffn_t, sums_two = contract(grid, down, act, n1, vec, teacher, keep[:, None], scales)

    square = grid.square

    def grads(lefts, rights, line_first=False):
        theirs = weight_grad(grid, lefts, rights, 1, line_first=line_first)

        def ours(*wait):
            got = after(arriving, *wait)
            return weight_grad(grid, lefts, rights, 0, got, line_first, square and not line_first)

        arriving = grid.cs(theirs)
        return theirs, arriving, ours

    if square:
        wg = functools.partial(weight_grad, grid)
        start, go_on, end, z, c = grid.plane_start, grid.plane_middle, grid.plane_end, grid.zs, grid.cs
        hop = grid.line_block
        right_a, right_b = [(0, act, 0, cut)], [(0, act, cut, up_cols - cut)]
        sib_a = wg([d_ffn_t], right_a, 1)
        got_a = c(sib_a)
        sib_b = wg([after(d_ffn_t, sib_a)], right_b, 1)
        got_b = c(sib_b)
        a = wg([d_ffn_t], right_a, 0, after(got_a, sib_b), parts=True)
        a_first = start(a)
        d_hidden, sums_up = contract_back(grid, down, after(d_ffn, a[0]), slope)
        b = wg([d_ffn_t], right_b, 0, after(got_b, d_hidden, *a_first), parts=True)
        a_last = go_on(a, a_first)
        right_u = [(0, after(d_hidden, b[0]), 0, up_cols)]
        sib_u = wg([first_low_t], right_u, 1)
        got_u = c(sib_u)
        b_first = start(b)
        d_one, d_attn, d_attn_t, sums_one = expand_back(
            grid, up, after(d_hidden, sib_u), d_two, n1, inv1, vec
        )
        d_ctx = attend_out_back(grid, first, after(d_attn, *a_last))
        a_own = end(a, a_first, a_last).astype(BF16)
        u = wg([first_low_t], right_u, 0, after(got_u, d_ctx, *b_first), parts=True)
        b_last = go_on(b, b_first)
        az1 = z(hop(a_own, 1))
        u_first = start(u)
        dq, dk, dv, sums_qv = attention_backward(q, k, v, ctx, after(d_ctx, u[0], az1, *b_last), probs)
        b_own = end(b, b_first, b_last).astype(BF16)
        az2, bz1 = z(hop(a_own, 2, az1)), z(hop(b_own, 1))
        lefts = [after(tokens_t, dq, az2, bz1, *u_first), d_attn_t]
        right_l, right_m = [(0, dq, 0, tile), (0, dk, 0, tile)], [(0, dv, 0, tile), (1, ctx, 0, tile)]
        sib_l = wg(lefts[:1], right_l, 1)
        got_l = c(sib_l)
        sib_m = wg([after(lefts[0], sib_l), d_attn_t], right_m, 1)
        got_m = c(sib_m)
        u_last = go_on(u, u_first)
        az3, bz2 = z(hop(a_own, 3, az2)), z(hop(b_own, 2, bz1))
        grad_tokens = project_back(grid, first, after(dq, sib_m), dk, dv, d_one)
        l = wg(lefts[:1], right_l, 0, after(got_l, grad_tokens, az3, bz2, *u_last), parts=True)
        l_first = start(l)
        m = wg(lefts, right_m, 0, after(got_m, l[0]), parts=True)
        m_first = start(m)
        u_own = end(u, u_first, u_last).astype(BF16)
        uz1 = z(hop(after(u_own, m[0]), 1))
        bz3 = z(hop(after(b_own, uz1), 3, bz2))
        uz2 = z(hop(after(u_own, bz3), 2, uz1))
        g_up = grid.line_end(u_own, z(hop(u_own, 3, uz2)))
        l_last, m_last = go_on(l, [after(f, m[0]) for f in l_first]), go_on(m, m_first)
        g_l = grid.line(end(l, l_first, l_last).astype(BF16))
        g_m = grid.line(end(m, m_first, m_last).astype(BF16))
        g_qkv, g_out = jnp.concatenate([g_l, g_m[:, :tile]], axis=1), g_m[:, tile:]
        g_down_a = grid.line_end(after(a_own, *l_last), az3)
        g_down_b = grid.line_end(after(b_own, *l_last), bz3)
        sums_up, sums_two, sums_one, sums_qv = (after(s, m[0], *l_first) for s in (sums_up, sums_two, sums_one, sums_qv))
    else:

        def reduced(lefts, rights):
            g = weight_grad(grid, lefts, rights, 0, grid.cs(weight_grad(grid, lefts, rights, 1)))
            return grid.line(grid.general(g).astype(BF16))

        g_down_a = reduced([d_ffn_t], [(0, act, 0, cut)])
        g_down_b = reduced([d_ffn_t], [(0, act, cut, up_cols - cut)])
        d_hidden, sums_up = contract_back(grid, down, d_ffn, slope)
        g_up = reduced([first_low_t], [(0, d_hidden, 0, up_cols)])
        d_one, d_attn, d_attn_t, sums_one = expand_back(grid, up, d_hidden, d_two, n1, inv1, vec)
        g_out = reduced([d_attn_t], [(0, ctx, 0, tile)])
        d_ctx = attend_out_back(grid, first, d_attn)
        dq, dk, dv, sums_qv = attention_backward(q, k, v, ctx, d_ctx, probs)
        g_qkv = reduced([tokens.T], [(0, dq, 0, tile), (0, dk, 0, tile), (0, dv, 0, tile)])
        grad_tokens = project_back(grid, first, dq, dk, dv, d_one)

    found = jnp.concatenate(
        [
            jnp.concatenate([sums_one[0:3], sums_two[0:3], sums_qv[0:2]]).reshape(-1, 128),
            jnp.sum(sums_up, axis=0).reshape(-1, 128),
            jnp.full((8, 128), jnp.sum(sums_two[3])),
        ]
    )
    found = grid.total_small(found)

    def own(v, rows):
        v = lax.dynamic_slice_in_dim(v, grid.t * rows, rows, v.ndim - 2)
        return lax.dynamic_slice_in_dim(v, grid.d * (HD // dp), HD // dp, v.ndim - 1)

    g8 = own(found[:n8].reshape(8, D // HD, HD), D // HD // T)
    g_up_b = own(found[n8 : n8 + nu].reshape(FF // HD, HD), FF // HD // T)
    loss_value = found[n8 + nu, 0] / norm_scale
    g_down = jnp.concatenate([g_down_a, g_down_b], axis=1)
    return (
        out_low,
        loss_value,
        grad_tokens,
        g_qkv.reshape(R, 3, tile).transpose(1, 0, 2),
        g8[6:8],
        g_out.T,
        g8[0],
        g8[1],
        g8[2],
        g_up,
        g_up_b,
        g_down.T,
        g8[3],
        g8[4],
        g8[5],
    )


def solution(mesh):
    vector = P("tensor", "dp")
    rows = P(("dp", "tensor"), None)
    qkv, qv, cols = P(None, "dp", "tensor"), P(None, "tensor", "dp"), P("dp", "tensor")
    return jax.shard_map(
        functools.partial(body, (mesh.shape["dp"], mesh.shape["tensor"])),
        mesh=mesh,
        in_specs=(
            rows, rows, P(("dp", "tensor")), P("dp"), P(), qkv, qv, vector, vector, vector, vector, cols,
            vector, vector, vector, vector, vector,
        ),
        out_specs=(
            rows, P(), rows, qkv, qv, vector, vector, vector, vector, cols, vector, vector, vector, vector, vector,
        ),
        check_vma=False,
    )
```

```python
import functools
import math

import jax
import jax.numpy as jnp
from jax import lax
from jax.experimental import pallas as pl
from jax.experimental.pallas import tpu as pltpu
from jax.sharding import PartitionSpec as P

HD = 64
SEQ = 512
EPS = 1e-06
MASKED = -1e30
F32 = jnp.float32
BF16 = jnp.bfloat16
ANY = pl.BlockSpec(memory_space=pltpu.HBM)
NT = (((1,), (1,)), ((), ()))
TN = (((0,), (0,)), ((), ()))


def cost(flops, nbytes, trans=0):
    return pl.CostEstimate(flops=int(flops), bytes_accessed=int(nbytes), transcendentals=int(trans))


def nt_dot(a, b):
    return lax.dot_general(a, b, NT, preferred_element_type=F32)


def dot(a, b):
    return jnp.dot(a, b, preferred_element_type=F32)


def after(x, *others):
    return lax.optimization_barrier((x, *others))[0] if others else x


def add(a, b):
    return (a.astype(F32) + b.astype(F32)).astype(BF16)


def in_hbm(*arrays):
    kept = tuple(pltpu.with_memory_space_constraint(a, pltpu.HBM) for a in arrays)
    return kept if len(kept) > 1 else kept[0]


class Pieces:
    def __init__(self, parts):
        self.arrays = [a for a, _ in parts]
        self.places = [p for _, p in parts]


class Grid:
    def __init__(self, dp, tensor):
        self.dp, self.T, self.Z = dp, tensor, dp // 4
        assert dp == self.Z * 4
        Z = self.Z
        self.cycle = [0] + list(range(1, Z, 2)) + list(range(2, Z, 2))[::-1]
        self.place = [self.cycle.index(z) for z in range(Z)]
        after = {self.cycle[i]: self.cycle[(i + 1) % Z] for i in range(Z)}
        cells = [(z, x, c) for z in range(Z) for x in range(2) for c in range(2)]
        self.to_z = [(self.rank(z, x, c), self.rank(after[z], x, c)) for z, x, c in cells]
        self.to_x = [(self.rank(z, x, c), self.rank(z, 1 - x, c)) for z, x, c in cells]
        self.to_c = [(self.rank(z, x, c), self.rank(z, x, 1 - c)) for z, x, c in cells]
        self.to_t = [(t, (t + 1) % tensor) for t in range(tensor)]
        self.square = tensor == 2 and Z == 4

    @staticmethod
    def rank(z, x, c):
        return z * 4 + x * 2 + c

    def here(self):
        d = lax.axis_index("dp")
        self.d, self.z, self.x, self.c, self.t = d, d // 4, (d // 2) % 2, d % 2, lax.axis_index("tensor")
        back = []
        for k in range(self.Z):
            options = [self.cycle[(p - k) % self.Z] for p in self.place]
            back.append(sum(jnp.where(self.z == z, o, 0) for z, o in enumerate(options)))
        self.back = back
        self.info = jnp.stack([v.astype(jnp.int32) for v in [self.t, self.x, self.c, self.z] + back])

    def zs(self, a):
        return lax.ppermute(a, "dp", self.to_z)

    def xs(self, a):
        return lax.ppermute(a, "dp", self.to_x)

    def cs(self, a):
        return lax.ppermute(a, "dp", self.to_c)

    def ts(self, a):
        return lax.ppermute(a, "tensor", self.to_t)

    def both_cores(self, parts, late=(), *hold):
        twins = [(self.cs(a), [(t, x, 1, k) for t, x, _, k in places]) for a, places in parts]
        twins += [(self.cs(after(a, *hold)), [(t, x, 1, k) for t, x, _, k in places]) for a, places in late]
        return Pieces(parts + list(late) + twins)

    def gather_general(self, own):
        ring = [own]
        for _ in range(self.Z - 1):
            ring.append(self.zs(ring[-1]))
        line, slots = jnp.stack(ring), range(self.Z)
        parts = [(line, [(0, 0, 0, k) for k in slots]), (self.xs(line), [(0, 1, 0, k) for k in slots])]
        rows = line
        for rt in range(1, self.T):
            rows = self.ts(rows)
            parts.append((rows, [(rt, 0, 0, k) for k in slots]))
            parts.append((self.xs(rows), [(rt, 1, 0, k) for k in slots]))
        return self.both_cores(parts)

    def gather(self, first, middle, last, hold):
        if not self.square:
            whole = [self.gather_general(a) for a in (first, middle, last)]
            return whole[0], first, lambda *_: (whole[1], first, lambda *_: whole[2])
        half = last.shape[0] // 2
        a0, b0, d = first[None], middle, last
        d_x, d_t = self.xs(d), self.ts(d)
        a1 = self.zs(a0)
        a0_x, a0_t = self.xs(after(a0, d_x)), self.ts(after(a0, d_t))
        a2 = self.zs(after(a1, d_x, d_t))
        d_far = [self.xs(after(d_t[:half], a0_x)), self.ts(after(d_x[half:], a0_t))]
        a1_x, a1_t = self.xs(a1), self.ts(a1)
        a3 = self.zs(after(a2, a0_x, a0_t))
        far_0 = self.xs(after(a0_t, a1_x))
        twin = {}

        def twins(**arrays):
            for name, v in arrays.items():
                twin[name] = self.cs(v)
            return [twin[name] for name in arrays]

        early = twins(a0=a0, a1=a1, a0_x=a0_x, a0_t=a0_t, a1_x=a1_x, a1_t=a1_t, far_0=far_0)
        b1 = self.zs(after(b0, a3, *d_far, *early))
        a23 = jnp.concatenate([a2, a3])
        a23_x, a23_t = self.xs(after(a23, far_0, *d_far)), self.ts(after(a23, *d_far))
        far_1, far_2 = self.xs(after(a1_t, a23_x)), self.ts(a23_x)
        plane = jnp.stack([d, d_x, d_t, jnp.concatenate(d_far)])
        early = twins(a23=after(a23, b1))
        b2 = self.zs(after(b1, a23_x, a23_t))
        early = twins(a23_x=after(a23_x, far_1), a23_t=after(a23_t, far_1), far_1=far_1)
        b3 = self.zs(after(b2, plane, far_1))
        twins(far_2=far_2)
        a_far = [far_0, far_1, far_2]
        line = jnp.stack([b0, b1, b2, b3])
        p1 = self.zs(after(plane, b3))

        def at(t, x, *slots):
            return [(t, x, 0, k) for k in slots]

        a_parts = [
            (a0, at(0, 0, 0)), (a1, at(0, 0, 1)), (a23, at(0, 0, 2, 3)),
            (a0_x, at(0, 1, 0)), (a1_x, at(0, 1, 1)), (a23_x, at(0, 1, 2, 3)),
            (a0_t, at(1, 0, 0)), (a1_t, at(1, 0, 1)), (a23_t, at(1, 0, 2, 3)),
            (a_far[0], at(1, 1, 0)), (a_far[1], at(1, 1, 1)), (a_far[2], at(1, 1, 2, 3)),
        ]

        def others(low):
            b_x, b_t = self.xs(after(line, a_far[1])), self.ts(after(line, a_far[2]))
            p2 = self.zs(p1)
            b_far = [self.xs(after(b_t[:2], low)), self.ts(after(b_x[2:], low))]
            p3 = self.zs(p2)
            b_parts = [
                (line, at(0, 0, 0, 1, 2, 3)), (b_x, at(0, 1, 0, 1, 2, 3)), (b_t, at(1, 0, 0, 1, 2, 3)),
                (b_far[0], at(1, 1, 0, 1)), (b_far[1], at(1, 1, 2, 3)),
            ]
            d_parts = [
                (p, [(0, 0, 0, k), (0, 1, 0, k), (1, 0, 0, k), (1, 1, 0, k)]) for k, p in enumerate([plane, p1, p2, p3])
            ]

            return self.both_cores(b_parts), p2, lambda act: self.both_cores(d_parts[:3], d_parts[3:], act)

        names = "a0 a1 a23 a0_x a1_x a23_x a0_t a1_t a23_t far_0 far_1 far_2".split()
        a_twins = [(twin[n], [(t, x, 1, k) for t, x, _, k in places]) for n, (_, places) in zip(names, a_parts)]
        return Pieces(a_parts + a_twins), p1, others

    def total_small(self, v):
        v = v + self.cs(v)
        held = v
        for _ in range(1, self.Z):
            held = self.zs(held)
            v = v + held
        v = v + self.xs(v)
        held = v
        for _ in range(1, self.T):
            held = self.ts(held)
            v = v + held
        return v

    def line_block(self, own, step, held=None):
        block = lax.dynamic_index_in_dim(own, self.back[step], 0, keepdims=False)
        if held is not None:
            block = block.astype(F32) + held.astype(F32)
        return block.astype(BF16)

    def line_hop(self, own, step, held=None):
        return self.zs(self.line_block(own, step, held))

    def line_end(self, own, held):
        return lax.dynamic_index_in_dim(own, self.z, 0, keepdims=False).astype(F32) + held.astype(F32)

    def line(self, own, held=None, first=1):
        for step in range(first, self.Z):
            held = self.line_hop(own, step, held)
        return self.line_end(own, held)

    def plane_start(self, parts):
        return self.xs(parts[1]), self.ts(parts[3])

    def plane_middle(self, parts, found):
        half = parts[2].shape[0]
        return self.xs(add(parts[2], found[1][:half])), self.ts(add(parts[4], found[0][:half]))

    def plane_end(self, parts, found, last):
        half = parts[2].shape[0]
        own = after(parts[0], *last).astype(F32)
        low = own[:half] + found[0][half:].astype(F32) + last[1].astype(F32)
        high = own[half:] + last[0].astype(F32) + found[1][half:].astype(F32)
        return jnp.concatenate([low, high])

    def general(self, g):
        rows = g[:, 0].astype(F32) + self.xs(g[:, 1]).astype(F32)
        held = None
        for step in range(1, self.T):
            block = rows[(self.T - step) % self.T]
            if held is not None:
                block = block + held.astype(F32)
            held = self.ts(block.astype(BF16))
        return rows[0] + held.astype(F32)


class Weights:
    def __init__(self, grid, D, sources):
        self.T, self.D, self.R = grid.T, D, D // grid.dp
        self.sources = sources
        self.width = sum(s[2] for s in sources)
        seen = []
        for pieces, *_ in sources:
            if pieces not in seen:
                seen.append(pieces)
        self.operands = [pltpu.with_memory_space_constraint(a, pltpu.HBM) for pieces in seen for a in pieces.arrays]
        self.first = {id(p): sum(len(q.arrays) for q in seen[:i]) for i, p in enumerate(seen)}
        self.specs = [ANY] * len(self.operands)
        self.scratch = [pltpu.VMEM((self.T, D, self.width), BF16), pltpu.SemaphoreType.DMA((self.T,))]

    def copies(self, info, refs, w, sem, want):
        out = []
        for pieces, lo, count, to in self.sources:
            base = self.first[id(pieces)]
            for i, places in enumerate(pieces.places):
                for entry, (rt, rx, rc, k) in enumerate(places):
                    if rt != want:
                        continue
                    row = (info[4 + k] * 4 + (info[1] ^ rx) * 2 + (info[2] ^ rc)) * self.R
                    src = refs[base + i].at[entry, :, pl.ds(lo, count)]
                    dst = w.at[rt, pl.ds(pl.multiple_of(row, self.R), self.R), pl.ds(to, count)]
                    out.append(pltpu.make_async_copy(src, dst, sem.at[rt]))
        return out

    def start(self, info, refs, w, sem):
        for rt in range(self.T):
            for copy in self.copies(info, refs, w, sem, rt):
                copy.start()

    def wait(self, info, refs, w, sem, rt, first):
        for want in range(self.T):

            @pl.when((rt == want) & first)
            def _(want=want):
                for copy in self.copies(info, refs, w, sem, want):
                    copy.wait()


def pack(grid, qkv_weight, out_rows, vectors, qv_bias, up_bias, valid_mask):
    R, tile = out_rows.shape
    w, h = vectors[0].shape
    S = valid_mask.shape[0]

    def kernel(info, qkv, out_w, mask, *rest):
        *items, qv, up, out, held = rest
        for i in range(3):
            out[:, i * tile : (i + 1) * tile] = qkv[i]
        out[:, 3 * tile : 4 * tile] = out_w[...]
        held[...] = jnp.zeros_like(held)
        d = info[3] * 4 + info[1] * 2 + info[2]
        lane = lax.broadcasted_iota(jnp.int32, (w, 128), 1) - lax.broadcasted_iota(jnp.int32, (w, 128), 0)
        low, high = (jnp.where(lane == d * w + add, 1.0, 0.0).astype(BF16) for add in (0, HD))
        at = 0
        for item in [v[...] for v in items] + [qv[0], qv[1], up[...]]:
            rows = item.shape[1]
            pick = lax.broadcasted_iota(jnp.int32, (rows // 2, rows), 1) - 2 * lax.broadcasted_iota(jnp.int32, (rows // 2, rows), 0)
            even, odd = (jnp.where(pick == k, 1.0, 0.0).astype(BF16) for k in (0, 1))
            wide = [lax.dot_general(item, e, TN, preferred_element_type=F32).astype(BF16) for e in (low, high)]
            held[at : at + rows // 2, :] = dot(even, wide[0]) + dot(odd, wide[1])
            at += rows // 2
        count = jnp.sum(mask[...].astype(F32), axis=1, keepdims=True).astype(jnp.int32)
        rest_of = jnp.bitwise_and(count, 15)
        held[at : at + 1, :] = jnp.broadcast_to((count - rest_of).astype(F32), (1, 128))
        held[at + 1 : at + 2, :] = jnp.broadcast_to(rest_of.astype(F32), (1, 128))
        out[:, 4 * tile :] = held[...].astype(BF16)

    operands = list(in_hbm(qkv_weight, out_rows, valid_mask.reshape(1, S), *vectors, qv_bias, up_bias))
    return call(
        kernel, "pack", grid, (1,), grid.info, operands, [fixed(a.shape) for a in operands],
        shape((R, 4 * tile + 128), BF16), fixed((R, 4 * tile + 128)), [pltpu.VMEM((R, 128), F32)],
        cost(0, 4 * R * 4 * tile), 16,
    )


def unpack(grid, pieces, first, rows):
    T, Z = grid.T, grid.Z
    arrays = [pltpu.with_memory_space_constraint(a, pltpu.HBM) for a in pieces.arrays]
    places = [(i, j, p) for i, ps in enumerate(pieces.places) for j, p in enumerate(ps)]

    def kernel(info, *rest):
        refs, (out, held, sem) = rest[: len(arrays)], rest[len(arrays) :]
        copies = [
            pltpu.make_async_copy(refs[i].at[j, :rows, pl.ds(first, 128)], held.at[n], sem)
            for n, (i, j, _) in enumerate(places)
        ]
        for copy in copies:
            copy.start()
        for copy in copies:
            copy.wait()
        for rt in range(T):
            mine = [n for n, (_, _, p) in enumerate(places) if p[0] == rt]
            total = held[mine[0]].astype(F32)
            for n in mine[1:]:
                total = total + held[n].astype(F32)
            out[pl.ds(part(info, rt, T), 1)] = total[None]

    return call(
        kernel, "unpack", grid, (1,), grid.info, arrays, [ANY] * len(arrays), shape((T, rows, 128), F32),
        fixed((T, rows, 128)), [pltpu.VMEM((len(places), rows, 128), BF16), pltpu.SemaphoreType.DMA],
        cost(0, 4 * len(places) * rows * 128), 16,
    )


def part(info, rt, T):
    return lax.rem(info[0] - rt + T, T)


def call(kernel, name, grid, steps, info, operands, in_specs, outs, out_specs, scratch, estimate, mib=36):
    return pl.pallas_call(
        kernel,
        out_shape=outs,
        grid_spec=pltpu.PrefetchScalarGridSpec(
            num_scalar_prefetch=1, grid=steps, in_specs=in_specs, out_specs=out_specs, scratch_shapes=scratch
        ),
        cost_estimate=estimate,
        compiler_params=pltpu.CompilerParams(vmem_limit_bytes=mib << 20),
        name=name,
    )(info, *operands)


def shape(dims, dtype):
    return jax.ShapeDtypeStruct(dims, dtype)


def shape_hbm(dims, dtype):
    return pltpu.HBM(dims, dtype)


def fixed(dims):
    return pl.BlockSpec(dims, lambda *_: (0,) * len(dims))


def project_qkv(grid, pieces, tokens, vec):
    T = grid.T
    S, D = tokens.shape
    tile = D // T
    ws = Weights(grid, D, [(pieces, 0, 3 * tile, 0)])

    def kernel(info, x, bias, *rest):
        refs, (q, k, v, w, sem) = rest[: len(ws.specs)], rest[len(ws.specs) :]
        rt = pl.program_id(0)

        @pl.when(rt == 0)
        def _():
            ws.start(info, refs, w, sem)

        ws.wait(info, refs, w, sem, rt, True)
        a, mine = x[...], w.at[rt]
        q[...] = (dot(a, mine[:, :tile]) + bias[6:7, :]).astype(BF16)
        k[...] = dot(a, mine[:, tile : 2 * tile]).astype(BF16)
        v[...] = (dot(a, mine[:, 2 * tile :]) + bias[7:8, :]).astype(BF16)

    cols = pl.BlockSpec((S, tile), lambda rt, info: (0, part(info, rt, T)))
    biases = pl.BlockSpec((vec.shape[0], tile), lambda rt, info: (0, part(info, rt, T)))
    out = shape((S, D), BF16)
    return call(
        kernel, "project_qkv", grid, (T,), grid.info, [tokens, vec] + ws.operands, [fixed((S, D)), biases] + ws.specs,
        (out, out, out), (cols, cols, cols), ws.scratch, cost(6 * S * D * D, 6 * D * D + 8 * S * D),
    )


def row_loop(S, rows, step, start):
    return lax.fori_loop(0, S // rows, lambda i, carry: step(pl.ds(pl.multiple_of(i * rows, rows), rows), carry), start)


def fold(a):
    return jnp.sum(a.reshape(a.shape[0] // 8, 8, a.shape[1]), axis=0)


def turn(src, dst):
    S = src.shape[0]

    def step(i, _):
        at = pl.ds(pl.multiple_of(i * 128, 128), 128)
        dst[:, at] = src[at, :].T
        return 0

    lax.fori_loop(0, S // 128, step, 0)


def normed(r):
    c = r - jnp.mean(r, axis=-1, keepdims=True)
    inv = lax.rsqrt(jnp.mean(c * c, axis=-1, keepdims=True) + EPS)
    return c * inv, inv


def normed_back(d, n, inv):
    return (d - jnp.mean(d, axis=-1, keepdims=True) - n * jnp.mean(d * n, axis=-1, keepdims=True)) * inv


ROWS = 128


def attend_out(grid, pieces, ctx, tokens, vec):
    T = grid.T
    S, D = tokens.shape
    tile = D // T
    ws = Weights(grid, D, [(pieces, 3 * tile, tile, 0)])

    def kernel(info, c, x, vecs, *rest):
        refs, (n1, inv1, low, low_t, w, sem, acc) = rest[: len(ws.specs)], rest[len(ws.specs) :]
        rt = pl.program_id(0)

        @pl.when(rt == 0)
        def _():
            ws.start(info, refs, w, sem)
            acc[...] = jnp.zeros_like(acc)

        ws.wait(info, refs, w, sem, rt, True)
        acc[...] += nt_dot(c[...], w[rt])

        @pl.when(rt == T - 1)
        def _():
            def step(at, carry):
                n, inv = normed(x[at, :].astype(F32) + (acc[at, :] + vecs[0:1, :]))
                n1[at, :] = n
                inv1[at, :] = jnp.broadcast_to(inv, (ROWS, 128))
                low[at, :] = (n * vecs[1:2, :] + vecs[2:3, :]).astype(BF16)
                return carry

            row_loop(S, ROWS, step, 0)
            turn(low, low_t)

    cols = pl.BlockSpec((S, tile), lambda rt, info: (0, part(info, rt, T)))
    return call(
        kernel, "attend_out", grid, (T,), grid.info, [ctx, tokens, vec] + ws.operands,
        [cols, fixed((S, D)), fixed(vec.shape)] + ws.specs,
        (shape_hbm((S, D), F32), shape((S, 128), F32), shape((S, D), BF16), shape((D, S), BF16)),
        (fixed((S, D)), fixed((S, 128)), fixed((S, D)), fixed((D, S))),
        ws.scratch + [pltpu.VMEM((S, D), F32)], cost(2 * S * D * D, 2 * D * D + 12 * S * D),
    )


def chunks(width, size):
    return [(lo, min(size, width - lo)) for lo in range(0, width, size)]


WIDE = 1024


def expand(grid, ws, low, up_b, FF):
    T = grid.T
    S, D = low.shape
    cols = FF // T

    def kernel(info, x, b, *rest):
        refs, (act, slope, w, sem) = rest[: len(ws.specs)], rest[len(ws.specs) :]
        rt = pl.program_id(0)

        @pl.when(rt == 0)
        def _():
            ws.start(info, refs, w, sem)

        ws.wait(info, refs, w, sem, rt, True)
        for lo, n in chunks(cols, WIDE // 2):
            u = dot(x[...], w[rt, :, lo : lo + n]) + b[:, lo : lo + n]
            cdf = 0.5 * (1.0 + lax.erf(u * (2.0**-0.5)))
            act[:, lo : lo + n] = (u * cdf).astype(BF16)
            slope[:, lo : lo + n] = (cdf + u * (jnp.exp(-0.5 * u * u) * 0.3989422804014327)).astype(BF16)

    def at(rt, info):
        return (0, part(info, rt, T))

    block = pl.BlockSpec((S, cols), at)
    out = shape((S, FF), BF16)
    return call(
        kernel, "expand", grid, (T,), grid.info, [low, up_b] + ws.operands,
        [fixed((S, D)), pl.BlockSpec((1, cols), at)] + ws.specs, (shape_hbm((S, FF), BF16), shape_hbm((S, FF), BF16)), (block, block), ws.scratch,
        cost(2 * S * D * FF, 2 * D * FF + 4 * S * FF, 2 * S * FF),
    )


def contract(grid, ws, act, n1, vec, teacher, keep, scales):
    T = grid.T
    S, D = n1.shape
    FF = act.shape[1]
    cols = FF // T

    def kernel(info, scale, a, vecs, kept, n1_any, teacher_any, *rest):
        refs, rest = rest[: len(ws.specs)], rest[len(ws.specs) :]
        low, d_two, d_ffn, d_ffn_t, sums, w, sem, acc, n1_s, teacher_s, own_sem = rest
        rt = pl.program_id(0)
        more = [
            pltpu.make_async_copy(n1_any, n1_s, own_sem.at[0]),
            pltpu.make_async_copy(teacher_any, teacher_s, own_sem.at[1]),
        ]

        @pl.when(rt == 0)
        def _():
            ws.start(info, refs, w, sem)
            for copy in more:
                copy.start()

        ws.wait(info, refs, w, sem, rt, True)

        def product(add):
            for lo, n in chunks(D, WIDE // 2):
                got = nt_dot(a[...], w[rt, lo : lo + n, :])
                acc[:, lo : lo + n] = acc[:, lo : lo + n] + got if add else got

        pl.when(rt == 0)(lambda: product(False))
        pl.when(rt > 0)(lambda: product(True))

        @pl.when(rt == T - 1)
        def _():
            for copy in more:
                copy.wait()

            def step(at, carry):
                s_bias, s_gain, s_shift, s_loss = carry
                first = n1_s[at, :] * vecs[1:2, :] + vecs[2:3, :]
                n, inv = normed(first + (acc[at, :] + vecs[3:4, :]))
                out = n * vecs[4:5, :] + vecs[5:6, :]
                low[at, :] = out.astype(BF16)
                error = out - teacher_s[at, :]
                weighed = kept[at, :] * error
                grad = scale[0] * weighed
                d = normed_back(grad * vecs[4:5, :], n, inv)
                d_two[at, :] = d
                d_ffn[at, :] = d.astype(BF16)
                return (
                    s_bias + fold(d), s_gain + fold(grad * n), s_shift + fold(grad), s_loss + fold(weighed * error),
                )

            zero = jnp.zeros((8, D), F32)
            found = row_loop(S, ROWS, step, (zero, zero, zero, zero))
            found = [jnp.sum(f, axis=0, keepdims=True) for f in found]
            sums[...] = jnp.concatenate(found + [jnp.zeros((4, D), F32)], axis=0)
            turn(d_ffn, d_ffn_t)

    block = pl.BlockSpec((S, cols), lambda rt, info: (0, part(info, rt, T)))
    rows = fixed((S, D))
    return call(
        kernel, "contract", grid, (T,), grid.info, [scales, in_hbm(act), vec, keep, *in_hbm(n1, teacher)] + ws.operands,
        [pl.BlockSpec(memory_space=pltpu.SMEM), block, fixed(vec.shape), fixed((S, 1)), ANY, ANY] + ws.specs,
        (shape_hbm((S, D), BF16), shape_hbm((S, D), F32), shape((S, D), BF16), shape((D, S), BF16), shape((8, D), F32)),
        (rows, rows, rows, fixed((D, S)), fixed((8, D))),
        ws.scratch + [pltpu.VMEM((S, D), F32)] * 3 + [pltpu.SemaphoreType.DMA((2,))],
        cost(2 * S * D * FF, 2 * D * FF + 2 * S * FF + 20 * S * D),
    )


def contract_back(grid, ws, d_ffn, slope):
    T = grid.T
    S, D = d_ffn.shape
    FF = slope.shape[1]
    cols = FF // T

    def kernel(info, x, s, *rest):
        refs, (out, sums, w, sem) = rest[: len(ws.specs)], rest[len(ws.specs) :]
        rt = pl.program_id(0)

        @pl.when(rt == 0)
        def _():
            ws.start(info, refs, w, sem)

        ws.wait(info, refs, w, sem, rt, True)
        for lo, n in chunks(cols, WIDE):
            d = dot(x[...], w[rt, :, lo : lo + n]) * s[:, lo : lo + n].astype(F32)
            d = d.astype(BF16)
            out[:, lo : lo + n] = d
            sums[:, lo : lo + n] = fold(d.astype(F32))

    def at(rt, info):
        return (0, part(info, rt, T))

    block = pl.BlockSpec((S, cols), at)
    return call(
        kernel, "contract_back", grid, (T,), grid.info, [d_ffn, in_hbm(slope)] + ws.operands,
        [fixed((S, D)), block] + ws.specs, (shape((S, FF), BF16), shape((8, FF), F32)),
        (block, pl.BlockSpec((8, cols), at)), ws.scratch, cost(2 * S * D * FF, 2 * D * FF + 4 * S * FF),
    )


def expand_back(grid, ws, d_hidden, d_two, n1, inv1, vec):
    T = grid.T
    S, D = n1.shape
    FF = d_hidden.shape[1]
    cols = FF // T

    def kernel(info, a, vecs, inv, n1_any, d_two_any, *rest):
        refs, rest = rest[: len(ws.specs)], rest[len(ws.specs) :]
        d_one, d_attn, d_attn_t, sums, w, sem, acc, n1_s, d_two_s, own_sem = rest
        rt = pl.program_id(0)
        more = [
            pltpu.make_async_copy(n1_any, n1_s, own_sem.at[0]),
            pltpu.make_async_copy(d_two_any, d_two_s, own_sem.at[1]),
        ]

        @pl.when(rt == 0)
        def _():
            ws.start(info, refs, w, sem)
            for copy in more:
                copy.start()

        ws.wait(info, refs, w, sem, rt, True)

        def product(add):
            for lo, n in chunks(D, WIDE // 2):
                got = nt_dot(a[...], w[rt, lo : lo + n, :])
                acc[:, lo : lo + n] = acc[:, lo : lo + n] + got if add else got

        pl.when(rt == 0)(lambda: product(False))
        pl.when(rt > 0)(lambda: product(True))

        @pl.when(rt == T - 1)
        def _():
            for copy in more:
                copy.wait()

            def step(at, carry):
                s_bias, s_gain, s_shift = carry
                n = n1_s[at, :]
                grad = d_two_s[at, :] + acc[at, :]
                d = normed_back(grad * vecs[1:2, :], n, inv[at, 0:1])
                d_one[at, :] = d
                d_attn[at, :] = d.astype(BF16)
                return s_bias + fold(d), s_gain + fold(grad * n), s_shift + fold(grad)

            zero = jnp.zeros((8, D), F32)
            found = row_loop(S, ROWS, step, (zero, zero, zero))
            found = [jnp.sum(f, axis=0, keepdims=True) for f in found]
            sums[...] = jnp.concatenate(found + [jnp.zeros((5, D), F32)], axis=0)
            turn(d_attn, d_attn_t)

    block = pl.BlockSpec((S, cols), lambda rt, info: (0, part(info, rt, T)))
    rows = fixed((S, D))
    return call(
        kernel, "expand_back", grid, (T,), grid.info, [in_hbm(d_hidden), vec, inv1, *in_hbm(n1, d_two)] + ws.operands,
        [block, fixed(vec.shape), fixed((S, 128)), ANY, ANY] + ws.specs,
        (shape_hbm((S, D), F32), shape((S, D), BF16), shape((D, S), BF16), shape((8, D), F32)),
        (rows, rows, fixed((D, S)), fixed((8, D))),
        ws.scratch + [pltpu.VMEM((S, D), F32)] * 3 + [pltpu.SemaphoreType.DMA((2,))],
        cost(2 * S * D * FF, 2 * D * FF + 2 * S * FF + 20 * S * D),
    )


def attend_out_back(grid, pieces, d_attn):
    T = grid.T
    S, D = d_attn.shape
    tile = D // T
    ws = Weights(grid, D, [(pieces, 3 * tile, tile, 0)])

    def kernel(info, x, *rest):
        refs, (out, w, sem) = rest[: len(ws.specs)], rest[len(ws.specs) :]
        rt = pl.program_id(0)

        @pl.when(rt == 0)
        def _():
            ws.start(info, refs, w, sem)

        ws.wait(info, refs, w, sem, rt, True)
        out[...] = dot(x[...], w[rt]).astype(BF16)

    cols = pl.BlockSpec((S, tile), lambda rt, info: (0, part(info, rt, T)))
    return call(
        kernel, "attend_out_back", grid, (T,), grid.info, [d_attn] + ws.operands, [fixed((S, D))] + ws.specs,
        shape((S, D), BF16), cols, ws.scratch, cost(2 * S * D * D, 2 * D * D + 4 * S * D),
    )


def project_back(grid, pieces, dq, dk, dv, d_one):
    T = grid.T
    S, D = d_one.shape
    tile = D // T
    ws = Weights(grid, D, [(pieces, 0, 3 * tile, 0)])

    def kernel(info, q, k, v, one, *rest):
        refs, (out, w, sem) = rest[: len(ws.specs)], rest[len(ws.specs) :]
        rt = pl.program_id(0)

        @pl.when(rt == 0)
        def _():
            ws.start(info, refs, w, sem)
            out[...] = one[...]

        ws.wait(info, refs, w, sem, rt, True)
        g = nt_dot(q[...], w[rt, :, :tile]) + nt_dot(k[...], w[rt, :, tile : 2 * tile])
        out[...] += g + nt_dot(v[...], w[rt, :, 2 * tile :])

    cols = pl.BlockSpec((S, tile), lambda rt, info: (0, part(info, rt, T)))
    return call(
        kernel, "project_back", grid, (T,), grid.info, [dq, dk, dv, in_hbm(d_one)] + ws.operands,
        [cols, cols, cols, fixed((S, D))] + ws.specs, shape((S, D), F32), fixed((S, D)), ws.scratch,
        cost(6 * S * D * D, 6 * D * D + 14 * S * D),
    )


def weight_grad(grid, lefts, rights, core, received=None, parts=False, extra=None):
    T, Z = grid.T, grid.Z
    D, S = lefts[0].shape
    R = D // grid.dp
    spans, width = [], 0
    for which, b, lo, count in rights:
        unit = math.gcd(lo, count, b.shape[1] // T)
        spans += [(which, width + i, (lo + i) // unit, unit, b.shape[1] // T // unit, b) for i in range(0, count, unit)]
        width += count

    def kernel(info, *rest):
        left_refs = rest[: len(lefts)]
        right_refs = rest[len(lefts) : len(lefts) + len(spans)]
        rest = list(rest[len(lefts) + len(spans) :])
        more = rest.pop(0) if extra is not None else None
        got = rest.pop(0) if received is not None else None
        *outs, rows = rest
        rt, half = pl.program_id(0), Z // 2

        @pl.when(rt == 0)
        def _():
            for a in range(len(lefts)):
                for rx in range(2):
                    for z in range(Z):
                        at = (z * 4 + (info[1] ^ rx) * 2 + (info[2] ^ core)) * R
                        rows[a, pl.ds((rx * Z + z) * R, R), :] = left_refs[a][pl.ds(pl.multiple_of(at, R), R), :]

        def put(g, to):
            if received is not None:
                g = g + got[0, :, :, :, to].astype(F32)
            g = g.astype(BF16)
            if not parts:
                outs[0][0, :, :, :, to] = g
                return

            @pl.when(rt == 0)
            def _():
                outs[0][:, :, to] = g[0]
                outs[1][half:, :, to] = g[1, :half]
                outs[2][:, :, to] = g[1, half:]

            @pl.when(rt == 1)
            def _():
                outs[1][:half, :, to] = g[1, :half]
                outs[3][:half, :, to] = g[1, half:]
                outs[3][half:, :, to] = g[0, half:]
                outs[4][:, :, to] = g[0, :half]

        for (which, first, _, count, *_), right in zip(spans, right_refs):
            for lo, n in chunks(count, WIDE):
                put(dot(rows[which], right[:, lo : lo + n]).reshape(2, Z, R, n), pl.ds(first + lo, n))
        if extra is not None:
            put(jnp.broadcast_to(more[0].astype(F32), (2, Z, R, 128)), pl.ds(width, 128))

    def right_map(which, start, first, count, every, b):
        return lambda rt, info: (0, part(info, rt, T) * every + first)

    full = width + (128 if extra is not None else 0)
    block = pl.BlockSpec((1, 2, Z, R, full), lambda rt, info: (rt, 0, 0, 0, 0))
    in_specs = [fixed((D, S)) for _ in lefts] + [pl.BlockSpec((S, s[3]), right_map(*s)) for s in spans]
    operands = list(lefts) + [s[5] for s in spans]
    if extra is not None:
        in_specs.append(pl.BlockSpec((1, R, 128), lambda rt, info: (part(info, rt, T), 0, 0)))
        operands.append(extra)
    if received is not None:
        in_specs.append(block)
        operands.append(received)
    out_shapes, out_specs = shape((T, 2, Z, R, full), BF16), block
    if parts:
        sizes = [(Z, R, full), (Z, R, full), (Z // 2, R, full), (Z, R, full), (Z // 2, R, full)]
        out_shapes, out_specs = tuple(shape(s, BF16) for s in sizes), tuple(fixed(s) for s in sizes)
    return call(
        kernel, "weight_grad", grid, (T,), grid.info, operands, in_specs, out_shapes, out_specs,
        [pltpu.VMEM((len(lefts), D // 2, S), BF16)],
        cost(D * S * width * T, 2 * S * width * T + (1 if received is None else 2) * D * width * T), 32,
    )


def own_vectors(grid, table, items):
    R, w = table.shape[0], HD // grid.dp
    exact = {"precision": lax.Precision.HIGHEST, "preferred_element_type": F32}

    def kernel(info, t, *outs):
        d = info[3] * 4 + info[1] * 2 + info[2]
        lane = lax.broadcasted_iota(jnp.int32, (w, 128), 1) - lax.broadcasted_iota(jnp.int32, (w, 128), 0)
        low, high = (jnp.where(lane == d * w + add, 1.0, 0.0) for add in (0, HD))
        at = 0
        for rows, out in zip(items, outs):
            n = rows // 2
            pick = lax.broadcasted_iota(jnp.int32, (n, rows), 1) - 2 * lax.broadcasted_iota(jnp.int32, (n, rows), 0)
            mine = t[at : at + n, :]
            total = jnp.zeros((w, rows), F32)
            for k, e in enumerate((low, high)):
                found = lax.dot_general(e, mine, NT, **exact)
                total = total + jnp.dot(found, jnp.where(pick == k, 1.0, 0.0), **exact)
            out[...] = total
            at += n

    return call(
        kernel, "own_vectors", grid, (1,), grid.info, [table], [fixed(table.shape)],
        tuple(shape((w, rows), F32) for rows in items), tuple(fixed((w, rows)) for rows in items), [],
        cost(0, 8 * R * 128), 16,
    )


def attention_forward(q, k, v, seg_col, seg_row):
    S, D = q.shape
    pairs = D // (2 * HD)

    def kernel(q, k, v, col, row, ctx, probs, bias):
        @pl.when(pl.program_id(0) == 0)
        def _():
            bias[...] = jnp.where(col[...] == row[...], 0.0, MASKED)

        lane = lax.broadcasted_iota(jnp.int32, (S, 2 * HD), 1) < HD
        query = q[...] * jnp.asarray(0.125, BF16)
        zero = jnp.zeros_like(query)
        outs = []
        for h in range(2):
            mine = jnp.where(lane == (h == 0), query, zero)
            s = nt_dot(mine, k[...]) + bias[...]
            e = jnp.exp(s - jnp.max(s, axis=-1, keepdims=True))
            p = (e * (1.0 / jnp.sum(e, axis=-1, keepdims=True))).astype(BF16)
            probs[h] = p
            outs.append(dot(p, v[...]))
        ctx[...] = jnp.where(lane, outs[0], outs[1]).astype(BF16)

    rows = pl.BlockSpec((S, 2 * HD), lambda i: (0, i))
    return pl.pallas_call(
        kernel,
        grid=(pairs,),
        out_shape=(shape((S, D), BF16), shape_hbm((2 * pairs, S, S), BF16)),
        in_specs=[rows, rows, rows, fixed((S, 1)), fixed((1, S))],
        out_specs=(rows, pl.BlockSpec((2, S, S), lambda i: (i, 0, 0))),
        scratch_shapes=[pltpu.VMEM((S, S), F32)],
        cost_estimate=cost(16 * S * S * D, 8 * S * D + 4 * pairs * S * S, 2 * pairs * S * S),
        compiler_params=pltpu.CompilerParams(vmem_limit_bytes=24 << 20),
        name="attention_forward",
    )(q, k, v, seg_col, seg_row)


def attention_backward(q, k, v, ctx, d_ctx, probs):
    S, D = q.shape
    pairs = D // (2 * HD)

    def kernel(q, k, v, ctx, d_ctx, probs, dq, dk, dv, sums):
        lane = lax.broadcasted_iota(jnp.int32, (S, 2 * HD), 1) < HD
        grad = d_ctx[...]
        both = grad.astype(F32) * ctx[...].astype(F32)
        dqs, dks, dvs = [], [], []
        for h in range(2):
            mask = lane == (h == 0)
            inner = jnp.sum(jnp.where(mask, both, 0.0), axis=-1, keepdims=True)
            mine = jnp.where(mask, grad, jnp.zeros_like(grad))
            d_prob = nt_dot(mine, v[...])
            p = probs[h]
            ds = (p.astype(F32) * (d_prob - inner)).astype(BF16)
            dvs.append(lax.dot_general(p, grad, TN, preferred_element_type=F32))
            dqs.append(dot(ds, k[...]))
            dks.append(lax.dot_general(ds, q[...], TN, preferred_element_type=F32))
        a = (jnp.where(lane, dqs[0], dqs[1]) * 0.125).astype(BF16)
        b = jnp.where(lane, dvs[0], dvs[1]).astype(BF16)
        dq[...] = a
        dk[...] = (jnp.where(lane, dks[0], dks[1]) * 0.125).astype(BF16)
        dv[...] = b
        total_a = jnp.sum(a.astype(F32), axis=0, keepdims=True)
        total_b = jnp.sum(b.astype(F32), axis=0, keepdims=True)
        sums[...] = jnp.concatenate([total_a, total_b, jnp.zeros((6, 2 * HD), F32)], axis=0)

    rows = pl.BlockSpec((S, 2 * HD), lambda i: (0, i))
    out = shape((S, D), BF16)
    return pl.pallas_call(
        kernel,
        grid=(pairs,),
        out_shape=(out, out, out, shape((8, D), F32)),
        in_specs=[rows] * 5 + [pl.BlockSpec((2, S, S), lambda i: (i, 0, 0))],
        out_specs=(rows, rows, rows, pl.BlockSpec((8, 2 * HD), lambda i: (0, i))),
        cost_estimate=cost(32 * S * S * D, 16 * S * D + 4 * pairs * S * S),
        compiler_params=pltpu.CompilerParams(vmem_limit_bytes=24 << 20),
        name="attention_backward",
    )(q, k, v, ctx, d_ctx, in_hbm(probs))


def body(
    sizes,
    tokens,
    teacher,
    valid_mask,
    segments,
    loss_scale,
    qkv_weight,
    qv_bias,
    out_weight,
    out_bias,
    first_gain,
    first_shift,
    up_weight,
    up_bias,
    down_weight,
    down_bias,
    second_gain,
    second_shift,
):
    grid = Grid(*sizes)
    grid.here()
    T, dp = grid.T, grid.dp
    S, D = tokens.shape
    assert S == SEQ
    up_cols = up_weight.shape[1]
    FF = up_cols * T
    tile = D // T
    R = D // dp
    cut = up_cols // 2
    keep = valid_mask.astype(F32)

    down_rows = down_weight.T
    down_rows = down_weight.T
    part_of = up_cols - up_cols // 4
    last_own = after(down_rows[:, :part_of])
    vectors = [out_bias, first_gain, first_shift, down_bias, second_gain, second_shift]
    first_own = pack(
        grid, after(qkv_weight, last_own), out_weight.T, [v.T for v in vectors], qv_bias.transpose(0, 2, 1), up_bias.T, valid_mask
    )
    n8, nu = 8 * D // 128, FF // 128
    used = n8 // T + nu // T + 2
    assert used <= R
    middle_own = jnp.concatenate([up_weight, down_rows[:, part_of:]], axis=1)
    first, sent, others = grid.gather(first_own, middle_own, last_own, None)
    table = unpack(grid, first, 4 * tile, R)
    vec = table[:, : n8 // T].reshape(T, 8, tile).transpose(1, 0, 2).reshape(8, D)
    up_b = table[:, n8 // T : n8 // T + nu // T].reshape(1, FF)
    count_all = jnp.sum(table[:, used - 2 : used, 0])
    norm_scale = count_all * D

    mine = lax.dynamic_slice_in_dim(segments, grid.t * S, S)
    tokens_t = tokens.T
    q, k, v = project_qkv(grid, first, after(tokens, tokens_t), vec)
    ctx, probs = attention_forward(q, k, v, mine[:, None], mine[None, :])
    n1, inv1, first_low, first_low_t = attend_out(grid, first, after(ctx, sent), tokens, vec)
    middle, sent, last_of = others(first_low)
    scales = (2.0 * loss_scale / norm_scale).reshape(1)
    up = Weights(grid, D, [(middle, 0, up_cols, 0)])
    act, slope = expand(grid, up, after(first_low, sent, scales), up_b, FF)
    down = Weights(grid, D, [(last_of(act), 0, part_of, 0), (middle, up_cols, up_cols - part_of, part_of)])
    out_low, d_two, d_ffn, d_ffn_t, sums_two = contract(grid, down, act, n1, vec, teacher, keep[:, None], scales)

    square = grid.square

    def bit_values():
        return jnp.exp2(31.0 - jnp.arange(64, dtype=F32))

    def rows_of_sums(sums_one, sums_two, sums_qv, sums_up):
        vectors = jnp.concatenate([sums_one[0:3], sums_two[0:3], sums_qv[0:2]])
        vectors = vectors.reshape(8, T, tile // 128, 128).transpose(1, 0, 2, 3).reshape(T, n8 // T, 128)
        rest = jnp.sum(sums_up, axis=0).reshape(T, nu // T, 128)
        above = jnp.floor(jnp.sum(sums_two[3]) / bit_values())
        bits = above - 2.0 * jnp.floor(above * 0.5)
        bits = jnp.broadcast_to(jnp.concatenate([bits, jnp.zeros((64,), F32)]), (T, 1, 128))
        zeros = jnp.zeros((T, R - used + 1, 128), F32)
        return jnp.concatenate([vectors, rest, bits, zeros], axis=1).astype(BF16)

    def grads(lefts, rights, line_first=False):
        theirs = weight_grad(grid, lefts, rights, 1, line_first=line_first)

        def ours(*wait):
            got = after(arriving, *wait)
            return weight_grad(grid, lefts, rights, 0, got, line_first, square and not line_first)

        arriving = grid.cs(theirs)
        return theirs, arriving, ours

    if square:
        wg = functools.partial(weight_grad, grid)
        start, go_on, end, z, c = grid.plane_start, grid.plane_middle, grid.plane_end, grid.zs, grid.cs
        hop = grid.line_block
        right_a, right_b = [(0, act, 0, cut)], [(0, act, cut, up_cols - cut)]
        sib_a = wg([d_ffn_t], right_a, 1)
        got_a = c(sib_a)
        sib_b = wg([after(d_ffn_t, sib_a)], right_b, 1)
        got_b = c(sib_b)
        a = wg([d_ffn_t], right_a, 0, after(got_a, sib_b), parts=True)
        a_first = start(a)
        d_hidden, sums_up = contract_back(grid, down, after(d_ffn, a[0]), slope)
        b = wg([d_ffn_t], right_b, 0, after(got_b, d_hidden, *a_first), parts=True)
        a_last = go_on(a, a_first)
        right_u = [(0, after(d_hidden, b[0]), 0, up_cols)]
        sib_u = wg([first_low_t], right_u, 1)
        got_u = c(sib_u)
        b_first = start([after(v, *a_last) for v in b])
        d_one, d_attn, d_attn_t, sums_one = expand_back(
            grid, up, after(d_hidden, sib_u), d_two, n1, inv1, vec
        )
        d_ctx = attend_out_back(grid, first, after(d_attn, *a_last, *b_first))
        u = wg([first_low_t], right_u, 0, after(got_u, d_ctx), parts=True)
        u_first = start(u)
        dq, dk, dv, sums_qv = attention_backward(q, k, v, ctx, after(d_ctx, u[0]), probs)
        b_last = go_on(b, [after(f, dq) for f in b_first])
        a_own = end((after(a[0], dq), *a[1:]), a_first, a_last).astype(BF16)
        az1 = z(hop(a_own, 1))
        lefts = [after(tokens_t, dq, *u_first), d_attn_t]
        right_l, right_m = [(0, dq, 0, tile), (0, dk, 0, tile)], [(0, dv, 0, tile), (1, ctx, 0, tile)]
        extra = rows_of_sums(sums_one, sums_two, sums_qv, sums_up)
        sib_l = wg(lefts[:1], right_l, 1, extra=extra)
        got_l = c(sib_l)
        sib_m = wg([after(lefts[0], sib_l), d_attn_t], right_m, 1)
        got_m = c(sib_m)
        u_last = go_on(u, u_first)
        l = wg(lefts[:1], right_l, 0, after(got_l, sib_m), parts=True, extra=extra)
        l_first = start(l)
        grad_tokens = project_back(grid, first, after(dq, l[0]), dk, dv, d_one)
        b_own = end(b, b_first, b_last).astype(BF16)
        az2, bz1 = z(hop(a_own, 2, az1)), z(hop(b_own, 1))
        m = wg(lefts, right_m, 0, after(got_m, grad_tokens, *u_last, *l_first), parts=True)
        az3 = z(hop(after(a_own, m[0]), 3, az2))
        l_last = go_on(l, [after(f, m[0]) for f in l_first])
        u_own = end(u, u_first, u_last).astype(BF16)
        uz1 = z(hop(after(u_own, *l_first), 1))
        m_first = start(m)
        uz2 = z(hop(u_own, 2, uz1))
        uz3 = z(hop(after(u_own, m[0]), 3, uz2))
        g_up = grid.line_end(u_own, uz3)
        bz2 = z(hop(after(b_own, uz3), 2, bz1))
        bz3 = z(hop(b_own, 3, bz2))
        m_last = go_on(m, m_first)
        g_l = grid.line(end(l, l_first, l_last).astype(BF16))
        g_m = grid.line(end(m, m_first, m_last).astype(BF16))
        sums, g_l = g_l[:, 2 * tile :], g_l[:, : 2 * tile]
        g_qkv, g_out = jnp.concatenate([g_l, g_m[:, :tile]], axis=1), g_m[:, tile:]
        g_down_a = grid.line_end(after(a_own, *l_last), az3)
        g_down_b = grid.line_end(after(b_own, *l_last), bz3)
    else:

        def reduced(lefts, rights, extra=None):
            theirs = grid.cs(weight_grad(grid, lefts, rights, 1, extra=extra))
            return grid.line(grid.general(weight_grad(grid, lefts, rights, 0, theirs, extra=extra)).astype(BF16))

        g_down_a = reduced([d_ffn_t], [(0, act, 0, cut)])
        g_down_b = reduced([d_ffn_t], [(0, act, cut, up_cols - cut)])
        d_hidden, sums_up = contract_back(grid, down, d_ffn, slope)
        g_up = reduced([first_low_t], [(0, d_hidden, 0, up_cols)])
        d_one, d_attn, d_attn_t, sums_one = expand_back(grid, up, d_hidden, d_two, n1, inv1, vec)
        g_out = reduced([d_attn_t], [(0, ctx, 0, tile)])
        d_ctx = attend_out_back(grid, first, d_attn)
        dq, dk, dv, sums_qv = attention_backward(q, k, v, ctx, d_ctx, probs)
        extra = rows_of_sums(sums_one, sums_two, sums_qv, sums_up)
        g_qkv = reduced([tokens.T], [(0, dq, 0, tile), (0, dk, 0, tile), (0, dv, 0, tile)], extra)
        sums, g_qkv = g_qkv[:, 3 * tile :], g_qkv[:, : 3 * tile]
        grad_tokens = project_back(grid, first, dq, dk, dv, d_one)

    h, hu = D // HD // T, FF // HD // T
    *g8, g_up_b = own_vectors(grid, sums[:used], [h] * 8 + [hu])
    g8, g_up_b = [v.T for v in g8], g_up_b.T
    loss_value = jnp.sum(sums[used - 2, :64] * bit_values()) / norm_scale
    g_down = jnp.concatenate([g_down_a, g_down_b], axis=1)
    return (
        out_low,
        loss_value,
        grad_tokens,
        g_qkv.reshape(R, 3, tile).transpose(1, 0, 2),
        jnp.stack(g8[6:8]),
        g_out.T,
        g8[0],
        g8[1],
        g8[2],
        g_up,
        g_up_b,
        g_down.T,
        g8[3],
        g8[4],
        g8[5],
    )


def solution(mesh):
    vector = P("tensor", "dp")
    rows = P(("dp", "tensor"), None)
    qkv, qv, cols = P(None, "dp", "tensor"), P(None, "tensor", "dp"), P("dp", "tensor")
    return jax.shard_map(
        functools.partial(body, (mesh.shape["dp"], mesh.shape["tensor"])),
        mesh=mesh,
        in_specs=(
            rows, rows, P(("dp", "tensor")), P("dp"), P(), qkv, qv, vector, vector, vector, vector, cols,
            vector, vector, vector, vector, vector,
        ),
        out_specs=(
            rows, P(), rows, qkv, qv, vector, vector, vector, vector, cols, vector, vector, vector, vector, vector,
        ),
        check_vma=False,
    )
```

```python
import functools
import math

import jax
import jax.numpy as jnp
from jax import lax
from jax.experimental import pallas as pl
from jax.experimental.pallas import tpu as pltpu
from jax.sharding import PartitionSpec as P

HD = 64
SEQ = 512
EPS = 1e-06
MASKED = -1e30
F32 = jnp.float32
BF16 = jnp.bfloat16
ANY = pl.BlockSpec(memory_space=pltpu.HBM)
NT = (((1,), (1,)), ((), ()))
TN = (((0,), (0,)), ((), ()))


def cost(flops, nbytes, trans=0):
    return pl.CostEstimate(flops=int(flops), bytes_accessed=int(nbytes), transcendentals=int(trans))


def nt_dot(a, b):
    return lax.dot_general(a, b, NT, preferred_element_type=F32)


def dot(a, b):
    return jnp.dot(a, b, preferred_element_type=F32)


def after(x, *others):
    return lax.optimization_barrier((x, *others))[0] if others else x


def add(a, b):
    return (a.astype(F32) + b.astype(F32)).astype(BF16)


def in_hbm(*arrays):
    kept = tuple(pltpu.with_memory_space_constraint(a, pltpu.HBM) for a in arrays)
    return kept if len(kept) > 1 else kept[0]


class Pieces:
    def __init__(self, parts):
        self.arrays = [a for a, _ in parts]
        self.places = [p for _, p in parts]


class Grid:
    def __init__(self, dp, tensor):
        self.dp, self.T, self.Z = dp, tensor, dp // 4
        assert dp == self.Z * 4
        Z = self.Z
        self.cycle = [0] + list(range(1, Z, 2)) + list(range(2, Z, 2))[::-1]
        self.place = [self.cycle.index(z) for z in range(Z)]
        after = {self.cycle[i]: self.cycle[(i + 1) % Z] for i in range(Z)}
        cells = [(z, x, c) for z in range(Z) for x in range(2) for c in range(2)]
        self.to_z = [(self.rank(z, x, c), self.rank(after[z], x, c)) for z, x, c in cells]
        self.to_x = [(self.rank(z, x, c), self.rank(z, 1 - x, c)) for z, x, c in cells]
        self.to_c = [(self.rank(z, x, c), self.rank(z, x, 1 - c)) for z, x, c in cells]
        self.to_t = [(t, (t + 1) % tensor) for t in range(tensor)]
        self.square = tensor == 2 and Z == 4

    @staticmethod
    def rank(z, x, c):
        return z * 4 + x * 2 + c

    def here(self):
        d = lax.axis_index("dp")
        self.d, self.z, self.x, self.c, self.t = d, d // 4, (d // 2) % 2, d % 2, lax.axis_index("tensor")
        back = []
        for k in range(self.Z):
            options = [self.cycle[(p - k) % self.Z] for p in self.place]
            back.append(sum(jnp.where(self.z == z, o, 0) for z, o in enumerate(options)))
        self.back = back
        self.info = jnp.stack([v.astype(jnp.int32) for v in [self.t, self.x, self.c, self.z] + back])

    def zs(self, a):
        return lax.ppermute(a, "dp", self.to_z)

    def xs(self, a):
        return lax.ppermute(a, "dp", self.to_x)

    def cs(self, a):
        return lax.ppermute(a, "dp", self.to_c)

    def ts(self, a):
        return lax.ppermute(a, "tensor", self.to_t)

    def both_cores(self, parts, late=(), *hold):
        twins = [(self.cs(a), [(t, x, 1, k) for t, x, _, k in places]) for a, places in parts]
        twins += [(self.cs(after(a, *hold)), [(t, x, 1, k) for t, x, _, k in places]) for a, places in late]
        return Pieces(parts + list(late) + twins)

    def gather_general(self, own):
        ring = [own]
        for _ in range(self.Z - 1):
            ring.append(self.zs(ring[-1]))
        line, slots = jnp.stack(ring), range(self.Z)
        parts = [(line, [(0, 0, 0, k) for k in slots]), (self.xs(line), [(0, 1, 0, k) for k in slots])]
        rows = line
        for rt in range(1, self.T):
            rows = self.ts(rows)
            parts.append((rows, [(rt, 0, 0, k) for k in slots]))
            parts.append((self.xs(rows), [(rt, 1, 0, k) for k in slots]))
        return self.both_cores(parts)

    def gather(self, first, middle, last, hold):
        if not self.square:
            whole = [self.gather_general(a) for a in (first, middle, last)]
            return whole[0], first, lambda *_: (whole[1], first, lambda *_: whole[2])
        half = last.shape[0] // 2
        a0, b0, d = first[None], middle, last
        d_x, d_t = self.xs(d), self.ts(d)
        a1 = self.zs(a0)
        a0_x, a0_t = self.xs(after(a0, d_x)), self.ts(after(a0, d_t))
        a2 = self.zs(after(a1, d_x, d_t))
        d_far = [self.xs(after(d_t[:half], a0_x)), self.ts(after(d_x[half:], a0_t))]
        a1_x, a1_t = self.xs(a1), self.ts(a1)
        a3 = self.zs(after(a2, a0_x, a0_t))
        far_0 = self.xs(after(a0_t, a1_x))
        twin = {}

        def twins(**arrays):
            for name, v in arrays.items():
                twin[name] = self.cs(v)
            return [twin[name] for name in arrays]

        early = twins(a0=a0, a1=a1, a0_x=a0_x, a0_t=a0_t, a1_x=a1_x, a1_t=a1_t, far_0=far_0)
        b1 = self.zs(after(b0, a3, *d_far, *early))
        a23 = jnp.concatenate([a2, a3])
        a23_x, a23_t = self.xs(after(a23, far_0, *d_far)), self.ts(after(a23, *d_far))
        far_1, far_2 = self.xs(after(a1_t, a23_x)), self.ts(a23_x)
        plane = jnp.stack([d, d_x, d_t, jnp.concatenate(d_far)])
        early = twins(a23=after(a23, b1))
        b2 = self.zs(after(b1, a23_x, a23_t))
        early = twins(a23_x=after(a23_x, far_1), a23_t=after(a23_t, far_1), far_1=far_1)
        b3 = self.zs(after(b2, plane, far_1))
        twins(far_2=far_2)
        a_far = [far_0, far_1, far_2]
        line = jnp.stack([b0, b1, b2, b3])
        p1 = self.zs(after(plane, b3))

        def at(t, x, *slots):
            return [(t, x, 0, k) for k in slots]

        a_parts = [
            (a0, at(0, 0, 0)), (a1, at(0, 0, 1)), (a23, at(0, 0, 2, 3)),
            (a0_x, at(0, 1, 0)), (a1_x, at(0, 1, 1)), (a23_x, at(0, 1, 2, 3)),
            (a0_t, at(1, 0, 0)), (a1_t, at(1, 0, 1)), (a23_t, at(1, 0, 2, 3)),
            (a_far[0], at(1, 1, 0)), (a_far[1], at(1, 1, 1)), (a_far[2], at(1, 1, 2, 3)),
        ]

        def others(low):
            b_x, b_t = self.xs(after(line, a_far[1])), self.ts(after(line, a_far[2]))
            p2 = self.zs(p1)
            b_far = [self.xs(after(b_t[:2], low)), self.ts(after(b_x[2:], low))]
            p3 = self.zs(p2)
            b_parts = [
                (line, at(0, 0, 0, 1, 2, 3)), (b_x, at(0, 1, 0, 1, 2, 3)), (b_t, at(1, 0, 0, 1, 2, 3)),
                (b_far[0], at(1, 1, 0, 1)), (b_far[1], at(1, 1, 2, 3)),
            ]
            d_parts = [
                (p, [(0, 0, 0, k), (0, 1, 0, k), (1, 0, 0, k), (1, 1, 0, k)]) for k, p in enumerate([plane, p1, p2, p3])
            ]

            return self.both_cores(b_parts), p2, lambda act: self.both_cores(d_parts[:3], d_parts[3:], act)

        names = "a0 a1 a23 a0_x a1_x a23_x a0_t a1_t a23_t far_0 far_1 far_2".split()
        a_twins = [(twin[n], [(t, x, 1, k) for t, x, _, k in places]) for n, (_, places) in zip(names, a_parts)]
        return Pieces(a_parts + a_twins), p1, others

    def total_small(self, v):
        v = v + self.cs(v)
        held = v
        for _ in range(1, self.Z):
            held = self.zs(held)
            v = v + held
        v = v + self.xs(v)
        held = v
        for _ in range(1, self.T):
            held = self.ts(held)
            v = v + held
        return v

    def line_block(self, own, step, held=None):
        block = lax.dynamic_index_in_dim(own, self.back[step], 0, keepdims=False)
        if held is not None:
            block = block.astype(F32) + held.astype(F32)
        return block.astype(BF16)

    def line_hop(self, own, step, held=None):
        return self.zs(self.line_block(own, step, held))

    def line_end(self, own, held):
        return lax.dynamic_index_in_dim(own, self.z, 0, keepdims=False).astype(F32) + held.astype(F32)

    def line(self, own, held=None, first=1):
        for step in range(first, self.Z):
            held = self.line_hop(own, step, held)
        return self.line_end(own, held)

    def plane_start(self, parts):
        return self.xs(parts[1]), self.ts(parts[3])

    def plane_middle(self, parts, found):
        half = parts[2].shape[0]
        return self.xs(add(parts[2], found[1][:half])), self.ts(add(parts[4], found[0][:half]))

    def plane_end(self, parts, found, last):
        half = parts[2].shape[0]
        own = after(parts[0], *last).astype(F32)
        low = own[:half] + found[0][half:].astype(F32) + last[1].astype(F32)
        high = own[half:] + last[0].astype(F32) + found[1][half:].astype(F32)
        return jnp.concatenate([low, high])

    def general(self, g):
        rows = g[:, 0].astype(F32) + self.xs(g[:, 1]).astype(F32)
        held = None
        for step in range(1, self.T):
            block = rows[(self.T - step) % self.T]
            if held is not None:
                block = block + held.astype(F32)
            held = self.ts(block.astype(BF16))
        return rows[0] + held.astype(F32)


class Weights:
    def __init__(self, grid, D, sources):
        self.T, self.D, self.R = grid.T, D, D // grid.dp
        self.sources = sources
        self.width = sum(s[2] for s in sources)
        seen = []
        for pieces, *_ in sources:
            if pieces not in seen:
                seen.append(pieces)
        self.operands = [pltpu.with_memory_space_constraint(a, pltpu.HBM) for pieces in seen for a in pieces.arrays]
        self.first = {id(p): sum(len(q.arrays) for q in seen[:i]) for i, p in enumerate(seen)}
        self.specs = [ANY] * len(self.operands)
        self.scratch = [pltpu.VMEM((self.T, D, self.width), BF16), pltpu.SemaphoreType.DMA((self.T,))]

    def copies(self, info, refs, w, sem, want):
        out = []
        for pieces, lo, count, to in self.sources:
            base = self.first[id(pieces)]
            for i, places in enumerate(pieces.places):
                for entry, (rt, rx, rc, k) in enumerate(places):
                    if rt != want:
                        continue
                    row = (info[4 + k] * 4 + (info[1] ^ rx) * 2 + (info[2] ^ rc)) * self.R
                    src = refs[base + i].at[entry, :, pl.ds(lo, count)]
                    dst = w.at[rt, pl.ds(pl.multiple_of(row, self.R), self.R), pl.ds(to, count)]
                    out.append(pltpu.make_async_copy(src, dst, sem.at[rt]))
        return out

    def start(self, info, refs, w, sem):
        for rt in range(self.T):
            for copy in self.copies(info, refs, w, sem, rt):
                copy.start()

    def wait(self, info, refs, w, sem, rt, first):
        for want in range(self.T):

            @pl.when((rt == want) & first)
            def _(want=want):
                for copy in self.copies(info, refs, w, sem, want):
                    copy.wait()


def pack(grid, qkv_weight, out_rows, vectors, qv_bias, up_bias, valid_mask):
    R, tile = out_rows.shape
    w, h = vectors[0].shape
    S = valid_mask.shape[0]

    def kernel(info, qkv, out_w, mask, *rest):
        *items, qv, up, out, held = rest
        for i in range(3):
            out[:, i * tile : (i + 1) * tile] = qkv[i]
        out[:, 3 * tile : 4 * tile] = out_w[...]
        held[...] = jnp.zeros_like(held)
        d = info[3] * 4 + info[1] * 2 + info[2]
        lane = lax.broadcasted_iota(jnp.int32, (w, 128), 1) - lax.broadcasted_iota(jnp.int32, (w, 128), 0)
        low, high = (jnp.where(lane == d * w + add, 1.0, 0.0).astype(BF16) for add in (0, HD))
        at = 0
        for item in [v[...] for v in items] + [qv[0], qv[1], up[...]]:
            rows = item.shape[1]
            pick = lax.broadcasted_iota(jnp.int32, (rows // 2, rows), 1) - 2 * lax.broadcasted_iota(jnp.int32, (rows // 2, rows), 0)
            even, odd = (jnp.where(pick == k, 1.0, 0.0).astype(BF16) for k in (0, 1))
            wide = [lax.dot_general(item, e, TN, preferred_element_type=F32).astype(BF16) for e in (low, high)]
            held[at : at + rows // 2, :] = dot(even, wide[0]) + dot(odd, wide[1])
            at += rows // 2
        count = jnp.sum(mask[...].astype(F32), axis=1, keepdims=True).astype(jnp.int32)
        rest_of = jnp.bitwise_and(count, 15)
        held[at : at + 1, :] = jnp.broadcast_to((count - rest_of).astype(F32), (1, 128))
        held[at + 1 : at + 2, :] = jnp.broadcast_to(rest_of.astype(F32), (1, 128))
        out[:, 4 * tile :] = held[...].astype(BF16)

    operands = list(in_hbm(qkv_weight, out_rows, valid_mask.reshape(1, S), *vectors, qv_bias, up_bias))
    return call(
        kernel, "pack", grid, (1,), grid.info, operands, [fixed(a.shape) for a in operands],
        shape((R, 4 * tile + 128), BF16), fixed((R, 4 * tile + 128)), [pltpu.VMEM((R, 128), F32)],
        cost(0, 4 * R * 4 * tile), 16,
    )


def unpack(grid, pieces, first, rows):
    T, Z = grid.T, grid.Z
    arrays = [pltpu.with_memory_space_constraint(a, pltpu.HBM) for a in pieces.arrays]
    places = [(i, j, p) for i, ps in enumerate(pieces.places) for j, p in enumerate(ps)]

    def kernel(info, *rest):
        refs, (out, held, sem) = rest[: len(arrays)], rest[len(arrays) :]
        copies = [
            pltpu.make_async_copy(refs[i].at[j, :rows, pl.ds(first, 128)], held.at[n], sem)
            for n, (i, j, _) in enumerate(places)
        ]
        for copy in copies:
            copy.start()
        for copy in copies:
            copy.wait()
        for rt in range(T):
            mine = [n for n, (_, _, p) in enumerate(places) if p[0] == rt]
            total = held[mine[0]].astype(F32)
            for n in mine[1:]:
                total = total + held[n].astype(F32)
            out[pl.ds(part(info, rt, T), 1)] = total[None]

    return call(
        kernel, "unpack", grid, (1,), grid.info, arrays, [ANY] * len(arrays), shape((T, rows, 128), F32),
        fixed((T, rows, 128)), [pltpu.VMEM((len(places), rows, 128), BF16), pltpu.SemaphoreType.DMA],
        cost(0, 4 * len(places) * rows * 128), 16,
    )


def part(info, rt, T):
    return lax.rem(info[0] - rt + T, T)


def call(kernel, name, grid, steps, info, operands, in_specs, outs, out_specs, scratch, estimate, mib=36):
    return pl.pallas_call(
        kernel,
        out_shape=outs,
        grid_spec=pltpu.PrefetchScalarGridSpec(
            num_scalar_prefetch=1, grid=steps, in_specs=in_specs, out_specs=out_specs, scratch_shapes=scratch
        ),
        cost_estimate=estimate,
        compiler_params=pltpu.CompilerParams(vmem_limit_bytes=mib << 20),
        name=name,
    )(info, *operands)


def shape(dims, dtype):
    return jax.ShapeDtypeStruct(dims, dtype)


def shape_hbm(dims, dtype):
    return pltpu.HBM(dims, dtype)


def fixed(dims):
    return pl.BlockSpec(dims, lambda *_: (0,) * len(dims))


def project_qkv(grid, pieces, tokens, vec):
    T = grid.T
    S, D = tokens.shape
    tile = D // T
    ws = Weights(grid, D, [(pieces, 0, 3 * tile, 0)])

    def kernel(info, x, bias, *rest):
        refs, (q, k, v, w, sem) = rest[: len(ws.specs)], rest[len(ws.specs) :]
        rt = pl.program_id(0)

        @pl.when(rt == 0)
        def _():
            ws.start(info, refs, w, sem)

        ws.wait(info, refs, w, sem, rt, True)
        a, mine = x[...], w.at[rt]
        q[...] = (dot(a, mine[:, :tile]) + bias[6:7, :]).astype(BF16)
        k[...] = dot(a, mine[:, tile : 2 * tile]).astype(BF16)
        v[...] = (dot(a, mine[:, 2 * tile :]) + bias[7:8, :]).astype(BF16)

    cols = pl.BlockSpec((S, tile), lambda rt, info: (0, part(info, rt, T)))
    biases = pl.BlockSpec((vec.shape[0], tile), lambda rt, info: (0, part(info, rt, T)))
    out = shape((S, D), BF16)
    return call(
        kernel, "project_qkv", grid, (T,), grid.info, [tokens, vec] + ws.operands, [fixed((S, D)), biases] + ws.specs,
        (out, out, out), (cols, cols, cols), ws.scratch, cost(6 * S * D * D, 6 * D * D + 8 * S * D),
    )


def row_loop(S, rows, step, start):
    return lax.fori_loop(0, S // rows, lambda i, carry: step(pl.ds(pl.multiple_of(i * rows, rows), rows), carry), start)


def fold(a):
    return jnp.sum(a.reshape(a.shape[0] // 8, 8, a.shape[1]), axis=0)


def turn(src, dst):
    S = src.shape[0]

    def step(i, _):
        at = pl.ds(pl.multiple_of(i * 128, 128), 128)
        dst[:, at] = src[at, :].T
        return 0

    lax.fori_loop(0, S // 128, step, 0)


def normed(r):
    c = r - jnp.mean(r, axis=-1, keepdims=True)
    inv = lax.rsqrt(jnp.mean(c * c, axis=-1, keepdims=True) + EPS)
    return c * inv, inv


def normed_back(d, n, inv):
    return (d - jnp.mean(d, axis=-1, keepdims=True) - n * jnp.mean(d * n, axis=-1, keepdims=True)) * inv


ROWS = 128


def attend_out(grid, pieces, ctx, tokens, vec):
    T = grid.T
    S, D = tokens.shape
    tile = D // T
    ws = Weights(grid, D, [(pieces, 3 * tile, tile, 0)])

    def kernel(info, c, x, vecs, *rest):
        refs, (n1, inv1, low, low_t, w, sem, acc) = rest[: len(ws.specs)], rest[len(ws.specs) :]
        rt = pl.program_id(0)

        @pl.when(rt == 0)
        def _():
            ws.start(info, refs, w, sem)
            acc[...] = jnp.zeros_like(acc)

        ws.wait(info, refs, w, sem, rt, True)
        acc[...] += nt_dot(c[...], w[rt])

        @pl.when(rt == T - 1)
        def _():
            def step(at, carry):
                n, inv = normed(x[at, :].astype(F32) + (acc[at, :] + vecs[0:1, :]))
                n1[at, :] = n
                inv1[at, :] = jnp.broadcast_to(inv, (ROWS, 128))
                low[at, :] = (n * vecs[1:2, :] + vecs[2:3, :]).astype(BF16)
                return carry

            row_loop(S, ROWS, step, 0)
            turn(low, low_t)

    cols = pl.BlockSpec((S, tile), lambda rt, info: (0, part(info, rt, T)))
    return call(
        kernel, "attend_out", grid, (T,), grid.info, [ctx, tokens, vec] + ws.operands,
        [cols, fixed((S, D)), fixed(vec.shape)] + ws.specs,
        (shape_hbm((S, D), F32), shape((S, 128), F32), shape((S, D), BF16), shape((D, S), BF16)),
        (fixed((S, D)), fixed((S, 128)), fixed((S, D)), fixed((D, S))),
        ws.scratch + [pltpu.VMEM((S, D), F32)], cost(2 * S * D * D, 2 * D * D + 12 * S * D),
    )


def chunks(width, size):
    return [(lo, min(size, width - lo)) for lo in range(0, width, size)]


WIDE = 1024


def expand(grid, ws, low, up_b, FF):
    T = grid.T
    S, D = low.shape
    cols = FF // T

    def kernel(info, x, b, *rest):
        refs, (act, slope, w, sem) = rest[: len(ws.specs)], rest[len(ws.specs) :]
        rt = pl.program_id(0)

        @pl.when(rt == 0)
        def _():
            ws.start(info, refs, w, sem)

        ws.wait(info, refs, w, sem, rt, True)
        for lo, n in chunks(cols, WIDE // 2):
            u = dot(x[...], w[rt, :, lo : lo + n]) + b[:, lo : lo + n]
            cdf = 0.5 * (1.0 + lax.erf(u * (2.0**-0.5)))
            act[:, lo : lo + n] = (u * cdf).astype(BF16)
            slope[:, lo : lo + n] = (cdf + u * (jnp.exp(-0.5 * u * u) * 0.3989422804014327)).astype(BF16)

    def at(rt, info):
        return (0, part(info, rt, T))

    block = pl.BlockSpec((S, cols), at)
    out = shape((S, FF), BF16)
    return call(
        kernel, "expand", grid, (T,), grid.info, [low, up_b] + ws.operands,
        [fixed((S, D)), pl.BlockSpec((1, cols), at)] + ws.specs, (shape_hbm((S, FF), BF16), shape_hbm((S, FF), BF16)), (block, block), ws.scratch,
        cost(2 * S * D * FF, 2 * D * FF + 4 * S * FF, 2 * S * FF),
    )


def contract(grid, ws, act, n1, vec, teacher, keep, scales):
    T = grid.T
    S, D = n1.shape
    FF = act.shape[1]
    cols = FF // T

    def kernel(info, scale, a, vecs, kept, n1_any, teacher_any, *rest):
        refs, rest = rest[: len(ws.specs)], rest[len(ws.specs) :]
        low, d_two, d_ffn, d_ffn_t, sums, w, sem, acc, n1_s, teacher_s, own_sem = rest
        rt = pl.program_id(0)
        more = [
            pltpu.make_async_copy(n1_any, n1_s, own_sem.at[0]),
            pltpu.make_async_copy(teacher_any, teacher_s, own_sem.at[1]),
        ]

        @pl.when(rt == 0)
        def _():
            ws.start(info, refs, w, sem)
            for copy in more:
                copy.start()

        ws.wait(info, refs, w, sem, rt, True)

        def product(add):
            for lo, n in chunks(D, WIDE // 2):
                got = nt_dot(a[...], w[rt, lo : lo + n, :])
                acc[:, lo : lo + n] = acc[:, lo : lo + n] + got if add else got

        pl.when(rt == 0)(lambda: product(False))
        pl.when(rt > 0)(lambda: product(True))

        @pl.when(rt == T - 1)
        def _():
            for copy in more:
                copy.wait()

            def step(at, carry):
                s_bias, s_gain, s_shift, s_loss = carry
                first = n1_s[at, :] * vecs[1:2, :] + vecs[2:3, :]
                n, inv = normed(first + (acc[at, :] + vecs[3:4, :]))
                out = n * vecs[4:5, :] + vecs[5:6, :]
                low[at, :] = out.astype(BF16)
                error = out - teacher_s[at, :]
                weighed = kept[at, :] * error
                grad = scale[0] * weighed
                d = normed_back(grad * vecs[4:5, :], n, inv)
                d_two[at, :] = d
                d_ffn[at, :] = d.astype(BF16)
                return (
                    s_bias + fold(d), s_gain + fold(grad * n), s_shift + fold(grad), s_loss + fold(weighed * error),
                )

            zero = jnp.zeros((8, D), F32)
            found = row_loop(S, ROWS, step, (zero, zero, zero, zero))
            found = [jnp.sum(f, axis=0, keepdims=True) for f in found]
            sums[...] = jnp.concatenate(found + [jnp.zeros((4, D), F32)], axis=0)
            turn(d_ffn, d_ffn_t)

    block = pl.BlockSpec((S, cols), lambda rt, info: (0, part(info, rt, T)))
    rows = fixed((S, D))
    return call(
        kernel, "contract", grid, (T,), grid.info, [scales, in_hbm(act), vec, keep, *in_hbm(n1, teacher)] + ws.operands,
        [pl.BlockSpec(memory_space=pltpu.SMEM), block, fixed(vec.shape), fixed((S, 1)), ANY, ANY] + ws.specs,
        (shape_hbm((S, D), BF16), shape_hbm((S, D), F32), shape((S, D), BF16), shape((D, S), BF16), shape((8, D), F32)),
        (rows, rows, rows, fixed((D, S)), fixed((8, D))),
        ws.scratch + [pltpu.VMEM((S, D), F32)] * 3 + [pltpu.SemaphoreType.DMA((2,))],
        cost(2 * S * D * FF, 2 * D * FF + 2 * S * FF + 20 * S * D),
    )


def contract_back(grid, ws, d_ffn, slope):
    T = grid.T
    S, D = d_ffn.shape
    FF = slope.shape[1]
    cols = FF // T

    def kernel(info, x, s, *rest):
        refs, (out, sums, w, sem) = rest[: len(ws.specs)], rest[len(ws.specs) :]
        rt = pl.program_id(0)

        @pl.when(rt == 0)
        def _():
            ws.start(info, refs, w, sem)

        ws.wait(info, refs, w, sem, rt, True)
        for lo, n in chunks(cols, WIDE):
            d = dot(x[...], w[rt, :, lo : lo + n]) * s[:, lo : lo + n].astype(F32)
            d = d.astype(BF16)
            out[:, lo : lo + n] = d
            sums[:, lo : lo + n] = fold(d.astype(F32))

    def at(rt, info):
        return (0, part(info, rt, T))

    block = pl.BlockSpec((S, cols), at)
    return call(
        kernel, "contract_back", grid, (T,), grid.info, [d_ffn, in_hbm(slope)] + ws.operands,
        [fixed((S, D)), block] + ws.specs, (shape((S, FF), BF16), shape((8, FF), F32)),
        (block, pl.BlockSpec((8, cols), at)), ws.scratch, cost(2 * S * D * FF, 2 * D * FF + 4 * S * FF),
    )


def expand_back(grid, ws, d_hidden, d_two, n1, inv1, vec):
    T = grid.T
    S, D = n1.shape
    FF = d_hidden.shape[1]
    cols = FF // T

    def kernel(info, a, vecs, inv, n1_any, d_two_any, *rest):
        refs, rest = rest[: len(ws.specs)], rest[len(ws.specs) :]
        d_one, d_attn, d_attn_t, sums, w, sem, acc, n1_s, d_two_s, own_sem = rest
        rt = pl.program_id(0)
        more = [
            pltpu.make_async_copy(n1_any, n1_s, own_sem.at[0]),
            pltpu.make_async_copy(d_two_any, d_two_s, own_sem.at[1]),
        ]

        @pl.when(rt == 0)
        def _():
            ws.start(info, refs, w, sem)
            for copy in more:
                copy.start()

        ws.wait(info, refs, w, sem, rt, True)

        def product(add):
            for lo, n in chunks(D, WIDE // 2):
                got = nt_dot(a[...], w[rt, lo : lo + n, :])
                acc[:, lo : lo + n] = acc[:, lo : lo + n] + got if add else got

        pl.when(rt == 0)(lambda: product(False))
        pl.when(rt > 0)(lambda: product(True))

        @pl.when(rt == T - 1)
        def _():
            for copy in more:
                copy.wait()

            def step(at, carry):
                s_bias, s_gain, s_shift = carry
                n = n1_s[at, :]
                grad = d_two_s[at, :] + acc[at, :]
                d = normed_back(grad * vecs[1:2, :], n, inv[at, 0:1])
                d_one[at, :] = d
                d_attn[at, :] = d.astype(BF16)
                return s_bias + fold(d), s_gain + fold(grad * n), s_shift + fold(grad)

            zero = jnp.zeros((8, D), F32)
            found = row_loop(S, ROWS, step, (zero, zero, zero))
            found = [jnp.sum(f, axis=0, keepdims=True) for f in found]
            sums[...] = jnp.concatenate(found + [jnp.zeros((5, D), F32)], axis=0)
            turn(d_attn, d_attn_t)

    block = pl.BlockSpec((S, cols), lambda rt, info: (0, part(info, rt, T)))
    rows = fixed((S, D))
    return call(
        kernel, "expand_back", grid, (T,), grid.info, [in_hbm(d_hidden), vec, inv1, *in_hbm(n1, d_two)] + ws.operands,
        [block, fixed(vec.shape), fixed((S, 128)), ANY, ANY] + ws.specs,
        (shape_hbm((S, D), F32), shape((S, D), BF16), shape((D, S), BF16), shape((8, D), F32)),
        (rows, rows, fixed((D, S)), fixed((8, D))),
        ws.scratch + [pltpu.VMEM((S, D), F32)] * 3 + [pltpu.SemaphoreType.DMA((2,))],
        cost(2 * S * D * FF, 2 * D * FF + 2 * S * FF + 20 * S * D),
    )


def attend_out_back(grid, pieces, d_attn):
    T = grid.T
    S, D = d_attn.shape
    tile = D // T
    ws = Weights(grid, D, [(pieces, 3 * tile, tile, 0)])

    def kernel(info, x, *rest):
        refs, (out, w, sem) = rest[: len(ws.specs)], rest[len(ws.specs) :]
        rt = pl.program_id(0)

        @pl.when(rt == 0)
        def _():
            ws.start(info, refs, w, sem)

        ws.wait(info, refs, w, sem, rt, True)
        out[...] = dot(x[...], w[rt]).astype(BF16)

    cols = pl.BlockSpec((S, tile), lambda rt, info: (0, part(info, rt, T)))
    return call(
        kernel, "attend_out_back", grid, (T,), grid.info, [d_attn] + ws.operands, [fixed((S, D))] + ws.specs,
        shape((S, D), BF16), cols, ws.scratch, cost(2 * S * D * D, 2 * D * D + 4 * S * D),
    )


def project_back(grid, pieces, dq, dk, dv, d_one):
    T = grid.T
    S, D = d_one.shape
    tile = D // T
    ws = Weights(grid, D, [(pieces, 0, 3 * tile, 0)])

    def kernel(info, q, k, v, one, *rest):
        refs, (out, w, sem) = rest[: len(ws.specs)], rest[len(ws.specs) :]
        rt = pl.program_id(0)

        @pl.when(rt == 0)
        def _():
            ws.start(info, refs, w, sem)
            out[...] = one[...]

        ws.wait(info, refs, w, sem, rt, True)
        g = nt_dot(q[...], w[rt, :, :tile]) + nt_dot(k[...], w[rt, :, tile : 2 * tile])
        out[...] += g + nt_dot(v[...], w[rt, :, 2 * tile :])

    cols = pl.BlockSpec((S, tile), lambda rt, info: (0, part(info, rt, T)))
    return call(
        kernel, "project_back", grid, (T,), grid.info, [dq, dk, dv, in_hbm(d_one)] + ws.operands,
        [cols, cols, cols, fixed((S, D))] + ws.specs, shape((S, D), F32), fixed((S, D)), ws.scratch,
        cost(6 * S * D * D, 6 * D * D + 14 * S * D),
    )


def weight_grad(grid, lefts, rights, core, received=None, parts=False, extra=None):
    T, Z = grid.T, grid.Z
    D, S = lefts[0].shape
    R = D // grid.dp
    spans, width = [], 0
    for which, b, lo, count in rights:
        unit = math.gcd(lo, count, b.shape[1] // T)
        spans += [(which, width + i, (lo + i) // unit, unit, b.shape[1] // T // unit, b) for i in range(0, count, unit)]
        width += count

    def kernel(info, *rest):
        left_refs = rest[: len(lefts)]
        right_refs = rest[len(lefts) : len(lefts) + len(spans)]
        rest = list(rest[len(lefts) + len(spans) :])
        more = rest.pop(0) if extra is not None else None
        got = rest.pop(0) if received is not None else None
        *outs, rows = rest
        rt, half = pl.program_id(0), Z // 2

        @pl.when(rt == 0)
        def _():
            for a in range(len(lefts)):
                for rx in range(2):
                    for z in range(Z):
                        at = (z * 4 + (info[1] ^ rx) * 2 + (info[2] ^ core)) * R
                        rows[a, pl.ds((rx * Z + z) * R, R), :] = left_refs[a][pl.ds(pl.multiple_of(at, R), R), :]

        def put(g, to):
            if received is not None:
                g = g + got[0, :, :, :, to].astype(F32)
            g = g.astype(BF16)
            if not parts:
                outs[0][0, :, :, :, to] = g
                return

            @pl.when(rt == 0)
            def _():
                outs[0][:, :, to] = g[0]
                outs[1][half:, :, to] = g[1, :half]
                outs[2][:, :, to] = g[1, half:]

            @pl.when(rt == 1)
            def _():
                outs[1][:half, :, to] = g[1, :half]
                outs[3][:half, :, to] = g[1, half:]
                outs[3][half:, :, to] = g[0, half:]
                outs[4][:, :, to] = g[0, :half]

        for (which, first, _, count, *_), right in zip(spans, right_refs):
            for lo, n in chunks(count, WIDE):
                put(dot(rows[which], right[:, lo : lo + n]).reshape(2, Z, R, n), pl.ds(first + lo, n))
        if extra is not None:
            put(jnp.broadcast_to(more[0].astype(F32), (2, Z, R, 128)), pl.ds(width, 128))

    def right_map(which, start, first, count, every, b):
        return lambda rt, info: (0, part(info, rt, T) * every + first)

    full = width + (128 if extra is not None else 0)
    block = pl.BlockSpec((1, 2, Z, R, full), lambda rt, info: (rt, 0, 0, 0, 0))
    in_specs = [fixed((D, S)) for _ in lefts] + [pl.BlockSpec((S, s[3]), right_map(*s)) for s in spans]
    operands = list(lefts) + [s[5] for s in spans]
    if extra is not None:
        in_specs.append(pl.BlockSpec((1, R, 128), lambda rt, info: (part(info, rt, T), 0, 0)))
        operands.append(extra)
    if received is not None:
        in_specs.append(block)
        operands.append(received)
    out_shapes, out_specs = shape((T, 2, Z, R, full), BF16), block
    if parts:
        sizes = [(Z, R, full), (Z, R, full), (Z // 2, R, full), (Z, R, full), (Z // 2, R, full)]
        out_shapes, out_specs = tuple(shape(s, BF16) for s in sizes), tuple(fixed(s) for s in sizes)
    return call(
        kernel, "weight_grad", grid, (T,), grid.info, operands, in_specs, out_shapes, out_specs,
        [pltpu.VMEM((len(lefts), D // 2, S), BF16)],
        cost(D * S * width * T, 2 * S * width * T + (1 if received is None else 2) * D * width * T), 32,
    )


def own_vectors(grid, table, items):
    R, w = table.shape[0], HD // grid.dp
    exact = {"precision": lax.Precision.HIGHEST, "preferred_element_type": F32}

    def kernel(info, t, *outs):
        d = info[3] * 4 + info[1] * 2 + info[2]
        lane = lax.broadcasted_iota(jnp.int32, (w, 128), 1) - lax.broadcasted_iota(jnp.int32, (w, 128), 0)
        low, high = (jnp.where(lane == d * w + add, 1.0, 0.0) for add in (0, HD))
        at = 0
        for rows, out in zip(items, outs):
            n = rows // 2
            pick = lax.broadcasted_iota(jnp.int32, (n, rows), 1) - 2 * lax.broadcasted_iota(jnp.int32, (n, rows), 0)
            mine = t[at : at + n, :]
            total = jnp.zeros((w, rows), F32)
            for k, e in enumerate((low, high)):
                found = lax.dot_general(e, mine, NT, **exact)
                total = total + jnp.dot(found, jnp.where(pick == k, 1.0, 0.0), **exact)
            out[...] = total
            at += n

    return call(
        kernel, "own_vectors", grid, (1,), grid.info, [table], [fixed(table.shape)],
        tuple(shape((w, rows), F32) for rows in items), tuple(fixed((w, rows)) for rows in items), [],
        cost(0, 8 * R * 128), 16,
    )


def attention_forward(q, k, v, seg_col, seg_row):
    S, D = q.shape
    pairs = D // (2 * HD)

    def kernel(q, k, v, col, row, ctx, probs, bias):
        @pl.when(pl.program_id(0) == 0)
        def _():
            bias[...] = jnp.where(col[...] == row[...], 0.0, MASKED)

        lane = lax.broadcasted_iota(jnp.int32, (S, 2 * HD), 1) < HD
        query = q[...] * jnp.asarray(0.125, BF16)
        zero = jnp.zeros_like(query)
        outs = []
        for h in range(2):
            mine = jnp.where(lane == (h == 0), query, zero)
            s = nt_dot(mine, k[...]) + bias[...]
            e = jnp.exp(s - jnp.max(s, axis=-1, keepdims=True))
            p = (e * (1.0 / jnp.sum(e, axis=-1, keepdims=True))).astype(BF16)
            probs[h] = p
            outs.append(dot(p, v[...]))
        ctx[...] = jnp.where(lane, outs[0], outs[1]).astype(BF16)

    rows = pl.BlockSpec((S, 2 * HD), lambda i: (0, i))
    return pl.pallas_call(
        kernel,
        grid=(pairs,),
        out_shape=(shape((S, D), BF16), shape_hbm((2 * pairs, S, S), BF16)),
        in_specs=[rows, rows, rows, fixed((S, 1)), fixed((1, S))],
        out_specs=(rows, pl.BlockSpec((2, S, S), lambda i: (i, 0, 0))),
        scratch_shapes=[pltpu.VMEM((S, S), F32)],
        cost_estimate=cost(16 * S * S * D, 8 * S * D + 4 * pairs * S * S, 2 * pairs * S * S),
        compiler_params=pltpu.CompilerParams(vmem_limit_bytes=24 << 20),
        name="attention_forward",
    )(q, k, v, seg_col, seg_row)


def attention_backward(q, k, v, ctx, d_ctx, probs):
    S, D = q.shape
    pairs = D // (2 * HD)

    def kernel(q, k, v, ctx, d_ctx, probs, dq, dk, dv, sums):
        lane = lax.broadcasted_iota(jnp.int32, (S, 2 * HD), 1) < HD
        grad = d_ctx[...]
        both = grad.astype(F32) * ctx[...].astype(F32)
        dqs, dks, dvs = [], [], []
        for h in range(2):
            mask = lane == (h == 0)
            inner = jnp.sum(jnp.where(mask, both, 0.0), axis=-1, keepdims=True)
            mine = jnp.where(mask, grad, jnp.zeros_like(grad))
            d_prob = nt_dot(mine, v[...])
            p = probs[h]
            ds = (p.astype(F32) * (d_prob - inner)).astype(BF16)
            dvs.append(lax.dot_general(p, grad, TN, preferred_element_type=F32))
            dqs.append(dot(ds, k[...]))
            dks.append(lax.dot_general(ds, q[...], TN, preferred_element_type=F32))
        a = (jnp.where(lane, dqs[0], dqs[1]) * 0.125).astype(BF16)
        b = jnp.where(lane, dvs[0], dvs[1]).astype(BF16)
        dq[...] = a
        dk[...] = (jnp.where(lane, dks[0], dks[1]) * 0.125).astype(BF16)
        dv[...] = b
        total_a = jnp.sum(a.astype(F32), axis=0, keepdims=True)
        total_b = jnp.sum(b.astype(F32), axis=0, keepdims=True)
        sums[...] = jnp.concatenate([total_a, total_b, jnp.zeros((6, 2 * HD), F32)], axis=0)

    rows = pl.BlockSpec((S, 2 * HD), lambda i: (0, i))
    out = shape((S, D), BF16)
    return pl.pallas_call(
        kernel,
        grid=(pairs,),
        out_shape=(out, out, out, shape((8, D), F32)),
        in_specs=[rows] * 5 + [pl.BlockSpec((2, S, S), lambda i: (i, 0, 0))],
        out_specs=(rows, rows, rows, pl.BlockSpec((8, 2 * HD), lambda i: (0, i))),
        cost_estimate=cost(32 * S * S * D, 16 * S * D + 4 * pairs * S * S),
        compiler_params=pltpu.CompilerParams(vmem_limit_bytes=24 << 20),
        name="attention_backward",
    )(q, k, v, ctx, d_ctx, in_hbm(probs))


def body(
    sizes,
    tokens,
    teacher,
    valid_mask,
    segments,
    loss_scale,
    qkv_weight,
    qv_bias,
    out_weight,
    out_bias,
    first_gain,
    first_shift,
    up_weight,
    up_bias,
    down_weight,
    down_bias,
    second_gain,
    second_shift,
):
    grid = Grid(*sizes)
    grid.here()
    T, dp = grid.T, grid.dp
    S, D = tokens.shape
    assert S == SEQ
    up_cols = up_weight.shape[1]
    FF = up_cols * T
    tile = D // T
    R = D // dp
    cut = up_cols // 2
    keep = valid_mask.astype(F32)

    down_rows = down_weight.T
    down_rows = down_weight.T
    part_of = up_cols - up_cols // 4
    last_own = after(down_rows[:, :part_of])
    vectors = [out_bias, first_gain, first_shift, down_bias, second_gain, second_shift]
    first_own = pack(
        grid, after(qkv_weight, last_own), out_weight.T, [v.T for v in vectors], qv_bias.transpose(0, 2, 1), up_bias.T, valid_mask
    )
    n8, nu = 8 * D // 128, FF // 128
    used = n8 // T + nu // T + 2
    assert used <= R
    middle_own = jnp.concatenate([up_weight, down_rows[:, part_of:]], axis=1)
    first, sent, others = grid.gather(first_own, middle_own, last_own, None)
    table = unpack(grid, first, 4 * tile, R)
    vec = table[:, : n8 // T].reshape(T, 8, tile).transpose(1, 0, 2).reshape(8, D)
    up_b = table[:, n8 // T : n8 // T + nu // T].reshape(1, FF)
    count_all = jnp.sum(table[:, used - 2 : used, 0])
    norm_scale = count_all * D

    mine = lax.dynamic_slice_in_dim(segments, grid.t * S, S)
    tokens_t = tokens.T
    q, k, v = project_qkv(grid, first, after(tokens, tokens_t), vec)
    ctx, probs = attention_forward(q, k, v, mine[:, None], mine[None, :])
    n1, inv1, first_low, first_low_t = attend_out(grid, first, after(ctx, sent), tokens, vec)
    middle, sent, last_of = others(first_low)
    scales = (2.0 * loss_scale / norm_scale).reshape(1)
    up = Weights(grid, D, [(middle, 0, up_cols, 0)])
    act, slope = expand(grid, up, after(first_low, sent, scales), up_b, FF)
    down = Weights(grid, D, [(last_of(act), 0, part_of, 0), (middle, up_cols, up_cols - part_of, part_of)])
    out_low, d_two, d_ffn, d_ffn_t, sums_two = contract(grid, down, act, n1, vec, teacher, keep[:, None], scales)

    square = grid.square

    def bit_values():
        return jnp.exp2(31.0 - jnp.arange(64, dtype=F32))

    def rows_of_sums(sums_one, sums_two, sums_qv, sums_up):
        vectors = jnp.concatenate([sums_one[0:3], sums_two[0:3], sums_qv[0:2]])
        vectors = vectors.reshape(8, T, tile // 128, 128).transpose(1, 0, 2, 3).reshape(T, n8 // T, 128)
        rest = jnp.sum(sums_up, axis=0).reshape(T, nu // T, 128)
        above = jnp.floor(jnp.sum(sums_two[3]) / bit_values())
        bits = above - 2.0 * jnp.floor(above * 0.5)
        bits = jnp.broadcast_to(jnp.concatenate([bits, jnp.zeros((64,), F32)]), (T, 1, 128))
        zeros = jnp.zeros((T, R - used + 1, 128), F32)
        return jnp.concatenate([vectors, rest, bits, zeros], axis=1).astype(BF16)

    def grads(lefts, rights, line_first=False):
        theirs = weight_grad(grid, lefts, rights, 1, line_first=line_first)

        def ours(*wait):
            got = after(arriving, *wait)
            return weight_grad(grid, lefts, rights, 0, got, line_first, square and not line_first)

        arriving = grid.cs(theirs)
        return theirs, arriving, ours

    if square:
        wg = functools.partial(weight_grad, grid)
        start, go_on, end, z, c = grid.plane_start, grid.plane_middle, grid.plane_end, grid.zs, grid.cs
        hop = grid.line_block
        right_a, right_b = [(0, act, 0, cut)], [(0, act, cut, up_cols - cut)]
        sib_a = wg([d_ffn_t], right_a, 1)
        got_a = c(sib_a)
        sib_b = wg([after(d_ffn_t, sib_a)], right_b, 1)
        got_b = c(sib_b)
        a = wg([d_ffn_t], right_a, 0, after(got_a, sib_b), parts=True)
        a_first = start(a)
        d_hidden, sums_up = contract_back(grid, down, after(d_ffn, a[0]), slope)
        b = wg([d_ffn_t], right_b, 0, after(got_b, d_hidden, *a_first), parts=True)
        a_last = go_on(a, a_first)
        right_u = [(0, after(d_hidden, b[0]), 0, up_cols)]
        sib_u = wg([first_low_t], right_u, 1)
        got_u = c(sib_u)
        b_first = start([after(v, *a_last) for v in b])
        d_one, d_attn, d_attn_t, sums_one = expand_back(
            grid, up, after(d_hidden, sib_u), d_two, n1, inv1, vec
        )
        d_ctx = attend_out_back(grid, first, after(d_attn, *a_last, *b_first))
        u = wg([first_low_t], right_u, 0, after(got_u, d_ctx), parts=True)
        u_first = start(u)
        dq, dk, dv, sums_qv = attention_backward(q, k, v, ctx, after(d_ctx, u[0]), probs)
        b_last = go_on(b, [after(f, dq) for f in b_first])
        lefts = [after(tokens_t, dq, *u_first), d_attn_t]
        right_l, right_m = [(0, dq, 0, tile), (0, dk, 0, tile)], [(0, dv, 0, tile), (1, ctx, 0, tile)]
        extra = rows_of_sums(sums_one, sums_two, sums_qv, sums_up)
        sib_l = wg(lefts[:1], right_l, 1, extra=extra)
        got_l = c(sib_l)
        sib_m = wg([after(lefts[0], sib_l, *b_last), d_attn_t], right_m, 1)
        got_m = c(sib_m)
        got_l, got_m = lax.optimization_barrier((got_l, got_m))
        l = wg(lefts[:1], right_l, 0, after(got_l, sib_m), parts=True, extra=extra)
        u_last = go_on(u, [after(f, l[0]) for f in u_first])
        l_first = start(l)
        ab_own = [end((after(p[0], dq), *p[1:]), f, e) for p, f, e in ((a, a_first, a_last), (b, b_first, b_last))]
        ab_own = jnp.concatenate(ab_own, axis=2).astype(BF16)
        abz1 = z(hop(ab_own, 1))
        abz2 = z(hop(after(ab_own, l[0]), 2, abz1))
        u_own = end(u, u_first, u_last).astype(BF16)
        uz1 = z(hop(after(u_own, abz2), 1))
        grad_tokens = project_back(grid, first, after(dq, u_own), dk, dv, d_one)
        m = wg(lefts, right_m, 0, after(got_m, grad_tokens, uz1, *l_first), parts=True)
        l_last = go_on(l, l_first)
        abz3 = z(hop(after(ab_own, uz1), 3, abz2))
        m_first = start(m)
        l_own = end(l, l_first, l_last).astype(BF16)
        uz2 = z(hop(after(u_own, m[0]), 2, uz1))
        lz1 = z(hop(l_own, 1))
        uz3 = z(hop(after(u_own, *m_first), 3, uz2))
        m_last = go_on(m, m_first)
        lz2 = z(hop(after(l_own, *m_first), 2, lz1))
        lz3 = z(hop(l_own, 3, lz2))
        g_up = grid.line_end(u_own, uz3)
        g_l = grid.line_end(l_own, lz3)
        g_ab = grid.line_end(ab_own, abz3)
        g_down_a, g_down_b = g_ab[:, :cut], g_ab[:, cut:]
        g_m = grid.line(end(m, m_first, m_last).astype(BF16))
        sums, g_l = g_l[:, 2 * tile :], g_l[:, : 2 * tile]
        g_qkv, g_out = jnp.concatenate([g_l, g_m[:, :tile]], axis=1), g_m[:, tile:]
    else:

        def reduced(lefts, rights, extra=None):
            theirs = grid.cs(weight_grad(grid, lefts, rights, 1, extra=extra))
            return grid.line(grid.general(weight_grad(grid, lefts, rights, 0, theirs, extra=extra)).astype(BF16))

        g_down_a = reduced([d_ffn_t], [(0, act, 0, cut)])
        g_down_b = reduced([d_ffn_t], [(0, act, cut, up_cols - cut)])
        d_hidden, sums_up = contract_back(grid, down, d_ffn, slope)
        g_up = reduced([first_low_t], [(0, d_hidden, 0, up_cols)])
        d_one, d_attn, d_attn_t, sums_one = expand_back(grid, up, d_hidden, d_two, n1, inv1, vec)
        g_out = reduced([d_attn_t], [(0, ctx, 0, tile)])
        d_ctx = attend_out_back(grid, first, d_attn)
        dq, dk, dv, sums_qv = attention_backward(q, k, v, ctx, d_ctx, probs)
        extra = rows_of_sums(sums_one, sums_two, sums_qv, sums_up)
        g_qkv = reduced([tokens.T], [(0, dq, 0, tile), (0, dk, 0, tile), (0, dv, 0, tile)], extra)
        sums, g_qkv = g_qkv[:, 3 * tile :], g_qkv[:, : 3 * tile]
        grad_tokens = project_back(grid, first, dq, dk, dv, d_one)

    h, hu = D // HD // T, FF // HD // T
    *g8, g_up_b = own_vectors(grid, sums[:used], [h] * 8 + [hu])
    g8, g_up_b = [v.T for v in g8], g_up_b.T
    loss_value = jnp.sum(sums[used - 2, :64] * bit_values()) / norm_scale
    g_down = jnp.concatenate([g_down_a, g_down_b], axis=1)
    return (
        out_low,
        loss_value,
        grad_tokens,
        g_qkv.reshape(R, 3, tile).transpose(1, 0, 2),
        jnp.stack(g8[6:8]),
        g_out.T,
        g8[0],
        g8[1],
        g8[2],
        g_up,
        g_up_b,
        g_down.T,
        g8[3],
        g8[4],
        g8[5],
    )


def solution(mesh):
    vector = P("tensor", "dp")
    rows = P(("dp", "tensor"), None)
    qkv, qv, cols = P(None, "dp", "tensor"), P(None, "tensor", "dp"), P("dp", "tensor")
    return jax.shard_map(
        functools.partial(body, (mesh.shape["dp"], mesh.shape["tensor"])),
        mesh=mesh,
        in_specs=(
            rows, rows, P(("dp", "tensor")), P("dp"), P(), qkv, qv, vector, vector, vector, vector, cols,
            vector, vector, vector, vector, vector,
        ),
        out_specs=(
            rows, P(), rows, qkv, qv, vector, vector, vector, vector, cols, vector, vector, vector, vector, vector,
        ),
        check_vma=False,
    )
```

```python
import functools
import math

import jax
import jax.numpy as jnp
from jax import lax
from jax.experimental import pallas as pl
from jax.experimental.pallas import tpu as pltpu
from jax.sharding import PartitionSpec as P

HD = 64
SEQ = 512
EPS = 1e-06
MASKED = -1e30
F32 = jnp.float32
BF16 = jnp.bfloat16
ANY = pl.BlockSpec(memory_space=pltpu.HBM)
NT = (((1,), (1,)), ((), ()))
TN = (((0,), (0,)), ((), ()))


def cost(flops, nbytes, trans=0):
    return pl.CostEstimate(flops=int(flops), bytes_accessed=int(nbytes), transcendentals=int(trans))


def nt_dot(a, b):
    return lax.dot_general(a, b, NT, preferred_element_type=F32)


def dot(a, b):
    return jnp.dot(a, b, preferred_element_type=F32)


def after(x, *others):
    return lax.optimization_barrier((x, *others))[0] if others else x


def add(a, b):
    return (a.astype(F32) + b.astype(F32)).astype(BF16)


def in_hbm(*arrays):
    kept = tuple(pltpu.with_memory_space_constraint(a, pltpu.HBM) for a in arrays)
    return kept if len(kept) > 1 else kept[0]


class Pieces:
    def __init__(self, parts):
        self.arrays = [a for a, _ in parts]
        self.places = [p for _, p in parts]


class Grid:
    def __init__(self, dp, tensor):
        self.dp, self.T, self.Z = dp, tensor, dp // 4
        assert dp == self.Z * 4
        Z = self.Z
        self.cycle = [0] + list(range(1, Z, 2)) + list(range(2, Z, 2))[::-1]
        self.place = [self.cycle.index(z) for z in range(Z)]
        after = {self.cycle[i]: self.cycle[(i + 1) % Z] for i in range(Z)}
        cells = [(z, x, c) for z in range(Z) for x in range(2) for c in range(2)]
        self.to_z = [(self.rank(z, x, c), self.rank(after[z], x, c)) for z, x, c in cells]
        self.to_x = [(self.rank(z, x, c), self.rank(z, 1 - x, c)) for z, x, c in cells]
        self.to_c = [(self.rank(z, x, c), self.rank(z, x, 1 - c)) for z, x, c in cells]
        self.to_t = [(t, (t + 1) % tensor) for t in range(tensor)]
        self.square = tensor == 2 and Z == 4

    @staticmethod
    def rank(z, x, c):
        return z * 4 + x * 2 + c

    def here(self):
        d = lax.axis_index("dp")
        self.d, self.z, self.x, self.c, self.t = d, d // 4, (d // 2) % 2, d % 2, lax.axis_index("tensor")
        back = []
        for k in range(self.Z):
            options = [self.cycle[(p - k) % self.Z] for p in self.place]
            back.append(sum(jnp.where(self.z == z, o, 0) for z, o in enumerate(options)))
        self.back = back
        self.info = jnp.stack([v.astype(jnp.int32) for v in [self.t, self.x, self.c, self.z] + back])

    def zs(self, a):
        return lax.ppermute(a, "dp", self.to_z)

    def xs(self, a):
        return lax.ppermute(a, "dp", self.to_x)

    def cs(self, a):
        return lax.ppermute(a, "dp", self.to_c)

    def ts(self, a):
        return lax.ppermute(a, "tensor", self.to_t)

    def both_cores(self, parts, late=(), *hold):
        twins = [(self.cs(a), [(t, x, 1, k) for t, x, _, k in places]) for a, places in parts]
        twins += [(self.cs(after(a, *hold)), [(t, x, 1, k) for t, x, _, k in places]) for a, places in late]
        return Pieces(parts + list(late) + twins)

    def gather_general(self, own):
        ring = [own]
        for _ in range(self.Z - 1):
            ring.append(self.zs(ring[-1]))
        line, slots = jnp.stack(ring), range(self.Z)
        parts = [(line, [(0, 0, 0, k) for k in slots]), (self.xs(line), [(0, 1, 0, k) for k in slots])]
        rows = line
        for rt in range(1, self.T):
            rows = self.ts(rows)
            parts.append((rows, [(rt, 0, 0, k) for k in slots]))
            parts.append((self.xs(rows), [(rt, 1, 0, k) for k in slots]))
        return self.both_cores(parts)

    def gather(self, first, middle, last, hold):
        if not self.square:
            whole = [self.gather_general(a) for a in (first, middle, last)]
            return whole[0], first, lambda *_: (whole[1], first, lambda *_: whole[2])
        half = last.shape[0] // 2
        a0, b0, d = first[None], middle, last
        d_x, d_t = self.xs(d), self.ts(d)
        a1 = self.zs(a0)
        a0_x, a0_t = self.xs(after(a0, d_x)), self.ts(after(a0, d_t))
        a2 = self.zs(after(a1, d_x, d_t))
        d_far = [self.xs(after(d_t[:half], a0_x)), self.ts(after(d_x[half:], a0_t))]
        a1_x, a1_t = self.xs(a1), self.ts(a1)
        a3 = self.zs(after(a2, a0_x, a0_t))
        far_0 = self.xs(after(a0_t, a1_x))
        twin = {}

        def twins(**arrays):
            for name, v in arrays.items():
                twin[name] = self.cs(v)
            return [twin[name] for name in arrays]

        early = twins(a0=a0, a1=a1, a0_x=a0_x, a0_t=a0_t, a1_x=a1_x, a1_t=a1_t, far_0=far_0)
        b1 = self.zs(after(b0, a3, *d_far, *early))
        a23 = jnp.concatenate([a2, a3])
        a23_x, a23_t = self.xs(after(a23, far_0, *d_far)), self.ts(after(a23, *d_far))
        far_1, far_2 = self.xs(after(a1_t, a23_x)), self.ts(a23_x)
        plane = jnp.stack([d, d_x, d_t, jnp.concatenate(d_far)])
        early = twins(a23=after(a23, b1))
        b2 = self.zs(after(b1, a23_x, a23_t))
        early = twins(a23_x=after(a23_x, far_1), a23_t=after(a23_t, far_1), far_1=far_1)
        b3 = self.zs(after(b2, plane, far_1))
        twins(far_2=far_2)
        a_far = [far_0, far_1, far_2]
        line = jnp.stack([b0, b1, b2, b3])
        p1 = self.zs(after(plane, b3))

        def at(t, x, *slots):
            return [(t, x, 0, k) for k in slots]

        a_parts = [
            (a0, at(0, 0, 0)), (a1, at(0, 0, 1)), (a23, at(0, 0, 2, 3)),
            (a0_x, at(0, 1, 0)), (a1_x, at(0, 1, 1)), (a23_x, at(0, 1, 2, 3)),
            (a0_t, at(1, 0, 0)), (a1_t, at(1, 0, 1)), (a23_t, at(1, 0, 2, 3)),
            (a_far[0], at(1, 1, 0)), (a_far[1], at(1, 1, 1)), (a_far[2], at(1, 1, 2, 3)),
        ]

        def others(low):
            b_x, b_t = self.xs(after(line, a_far[1])), self.ts(after(line, a_far[2]))
            p2 = self.zs(p1)
            b_far = [self.xs(after(b_t[:2], low)), self.ts(after(b_x[2:], low))]
            p3 = self.zs(p2)
            b_parts = [
                (line, at(0, 0, 0, 1, 2, 3)), (b_x, at(0, 1, 0, 1, 2, 3)), (b_t, at(1, 0, 0, 1, 2, 3)),
                (b_far[0], at(1, 1, 0, 1)), (b_far[1], at(1, 1, 2, 3)),
            ]
            d_parts = [
                (p, [(0, 0, 0, k), (0, 1, 0, k), (1, 0, 0, k), (1, 1, 0, k)]) for k, p in enumerate([plane, p1, p2, p3])
            ]

            return self.both_cores(b_parts), p2, lambda act: self.both_cores(d_parts[:3], d_parts[3:], act)

        names = "a0 a1 a23 a0_x a1_x a23_x a0_t a1_t a23_t far_0 far_1 far_2".split()
        a_twins = [(twin[n], [(t, x, 1, k) for t, x, _, k in places]) for n, (_, places) in zip(names, a_parts)]
        return Pieces(a_parts + a_twins), p1, others

    def total_small(self, v):
        v = v + self.cs(v)
        held = v
        for _ in range(1, self.Z):
            held = self.zs(held)
            v = v + held
        v = v + self.xs(v)
        held = v
        for _ in range(1, self.T):
            held = self.ts(held)
            v = v + held
        return v

    def line_block(self, own, step, held=None):
        block = lax.dynamic_index_in_dim(own, self.back[step], 0, keepdims=False)
        if held is not None:
            block = block.astype(F32) + held.astype(F32)
        return block.astype(BF16)

    def line_hop(self, own, step, held=None):
        return self.zs(self.line_block(own, step, held))

    def line_end(self, own, held):
        return lax.dynamic_index_in_dim(own, self.z, 0, keepdims=False).astype(F32) + held.astype(F32)

    def line(self, own, held=None, first=1):
        for step in range(first, self.Z):
            held = self.line_hop(own, step, held)
        return self.line_end(own, held)

    def plane_start(self, parts):
        return self.xs(parts[1]), self.ts(parts[3])

    def plane_middle(self, parts, found):
        half = parts[2].shape[0]
        return self.xs(add(parts[2], found[1][:half])), self.ts(add(parts[4], found[0][:half]))

    def plane_end(self, parts, found, last):
        half = parts[2].shape[0]
        own = after(parts[0], *last).astype(F32)
        low = own[:half] + found[0][half:].astype(F32) + last[1].astype(F32)
        high = own[half:] + last[0].astype(F32) + found[1][half:].astype(F32)
        return jnp.concatenate([low, high])

    def general(self, g):
        rows = g[:, 0].astype(F32) + self.xs(g[:, 1]).astype(F32)
        held = None
        for step in range(1, self.T):
            block = rows[(self.T - step) % self.T]
            if held is not None:
                block = block + held.astype(F32)
            held = self.ts(block.astype(BF16))
        return rows[0] + held.astype(F32)


class Weights:
    def __init__(self, grid, D, sources):
        self.T, self.D, self.R = grid.T, D, D // grid.dp
        self.sources = sources
        self.width = sum(s[2] for s in sources)
        seen = []
        for pieces, *_ in sources:
            if pieces not in seen:
                seen.append(pieces)
        self.operands = [pltpu.with_memory_space_constraint(a, pltpu.HBM) for pieces in seen for a in pieces.arrays]
        self.first = {id(p): sum(len(q.arrays) for q in seen[:i]) for i, p in enumerate(seen)}
        self.specs = [ANY] * len(self.operands)
        self.scratch = [pltpu.VMEM((self.T, D, self.width), BF16), pltpu.SemaphoreType.DMA((self.T,))]

    def copies(self, info, refs, w, sem, want):
        out = []
        for pieces, lo, count, to in self.sources:
            base = self.first[id(pieces)]
            for i, places in enumerate(pieces.places):
                for entry, (rt, rx, rc, k) in enumerate(places):
                    if rt != want:
                        continue
                    row = (info[4 + k] * 4 + (info[1] ^ rx) * 2 + (info[2] ^ rc)) * self.R
                    src = refs[base + i].at[entry, :, pl.ds(lo, count)]
                    dst = w.at[rt, pl.ds(pl.multiple_of(row, self.R), self.R), pl.ds(to, count)]
                    out.append(pltpu.make_async_copy(src, dst, sem.at[rt]))
        return out

    def start(self, info, refs, w, sem):
        for rt in range(self.T):
            for copy in self.copies(info, refs, w, sem, rt):
                copy.start()

    def wait(self, info, refs, w, sem, rt, first):
        for want in range(self.T):

            @pl.when((rt == want) & first)
            def _(want=want):
                for copy in self.copies(info, refs, w, sem, want):
                    copy.wait()


def pack(grid, qkv_weight, out_rows, vectors, qv_bias, up_bias, valid_mask):
    R, tile = out_rows.shape
    w, h = vectors[0].shape
    S = valid_mask.shape[0]

    def kernel(info, qkv, out_w, mask, *rest):
        *items, qv, up, out, held = rest
        for i in range(3):
            out[:, i * tile : (i + 1) * tile] = qkv[i]
        out[:, 3 * tile : 4 * tile] = out_w[...]
        held[...] = jnp.zeros_like(held)
        d = info[3] * 4 + info[1] * 2 + info[2]
        lane = lax.broadcasted_iota(jnp.int32, (w, 128), 1) - lax.broadcasted_iota(jnp.int32, (w, 128), 0)
        low, high = (jnp.where(lane == d * w + add, 1.0, 0.0).astype(BF16) for add in (0, HD))
        at = 0
        for item in [v[...] for v in items] + [qv[0], qv[1], up[...]]:
            rows = item.shape[1]
            pick = lax.broadcasted_iota(jnp.int32, (rows // 2, rows), 1) - 2 * lax.broadcasted_iota(jnp.int32, (rows // 2, rows), 0)
            even, odd = (jnp.where(pick == k, 1.0, 0.0).astype(BF16) for k in (0, 1))
            wide = [lax.dot_general(item, e, TN, preferred_element_type=F32).astype(BF16) for e in (low, high)]
            held[at : at + rows // 2, :] = dot(even, wide[0]) + dot(odd, wide[1])
            at += rows // 2
        count = jnp.sum(mask[...].astype(F32), axis=1, keepdims=True).astype(jnp.int32)
        rest_of = jnp.bitwise_and(count, 15)
        held[at : at + 1, :] = jnp.broadcast_to((count - rest_of).astype(F32), (1, 128))
        held[at + 1 : at + 2, :] = jnp.broadcast_to(rest_of.astype(F32), (1, 128))
        out[:, 4 * tile :] = held[...].astype(BF16)

    operands = list(in_hbm(qkv_weight, out_rows, valid_mask.reshape(1, S), *vectors, qv_bias, up_bias))
    return call(
        kernel, "pack", grid, (1,), grid.info, operands, [fixed(a.shape) for a in operands],
        shape((R, 4 * tile + 128), BF16), fixed((R, 4 * tile + 128)), [pltpu.VMEM((R, 128), F32)],
        cost(0, 4 * R * 4 * tile), 16,
    )


def unpack(grid, pieces, first, rows):
    T, Z = grid.T, grid.Z
    arrays = [pltpu.with_memory_space_constraint(a, pltpu.HBM) for a in pieces.arrays]
    places = [(i, j, p) for i, ps in enumerate(pieces.places) for j, p in enumerate(ps)]

    def kernel(info, *rest):
        refs, (out, held, sem) = rest[: len(arrays)], rest[len(arrays) :]
        copies = [
            pltpu.make_async_copy(refs[i].at[j, :rows, pl.ds(first, 128)], held.at[n], sem)
            for n, (i, j, _) in enumerate(places)
        ]
        for copy in copies:
            copy.start()
        for copy in copies:
            copy.wait()
        for rt in range(T):
            mine = [n for n, (_, _, p) in enumerate(places) if p[0] == rt]
            total = held[mine[0]].astype(F32)
            for n in mine[1:]:
                total = total + held[n].astype(F32)
            out[pl.ds(part(info, rt, T), 1)] = total[None]

    return call(
        kernel, "unpack", grid, (1,), grid.info, arrays, [ANY] * len(arrays), shape((T, rows, 128), F32),
        fixed((T, rows, 128)), [pltpu.VMEM((len(places), rows, 128), BF16), pltpu.SemaphoreType.DMA],
        cost(0, 4 * len(places) * rows * 128), 16,
    )


def part(info, rt, T):
    return lax.rem(info[0] - rt + T, T)


def call(kernel, name, grid, steps, info, operands, in_specs, outs, out_specs, scratch, estimate, mib=36):
    return pl.pallas_call(
        kernel,
        out_shape=outs,
        grid_spec=pltpu.PrefetchScalarGridSpec(
            num_scalar_prefetch=1, grid=steps, in_specs=in_specs, out_specs=out_specs, scratch_shapes=scratch
        ),
        cost_estimate=estimate,
        compiler_params=pltpu.CompilerParams(vmem_limit_bytes=mib << 20),
        name=name,
    )(info, *operands)


def shape(dims, dtype):
    return jax.ShapeDtypeStruct(dims, dtype)


def shape_hbm(dims, dtype):
    return pltpu.HBM(dims, dtype)


def fixed(dims):
    return pl.BlockSpec(dims, lambda *_: (0,) * len(dims))


def project_qkv(grid, pieces, tokens, vec):
    T = grid.T
    S, D = tokens.shape
    tile = D // T
    ws = Weights(grid, D, [(pieces, 0, 3 * tile, 0)])

    def kernel(info, x, bias, *rest):
        refs, (q, k, v, w, sem) = rest[: len(ws.specs)], rest[len(ws.specs) :]
        rt = pl.program_id(0)

        @pl.when(rt == 0)
        def _():
            ws.start(info, refs, w, sem)

        ws.wait(info, refs, w, sem, rt, True)
        a, mine = x[...], w.at[rt]
        q[...] = (dot(a, mine[:, :tile]) + bias[6:7, :]).astype(BF16)
        k[...] = dot(a, mine[:, tile : 2 * tile]).astype(BF16)
        v[...] = (dot(a, mine[:, 2 * tile :]) + bias[7:8, :]).astype(BF16)

    cols = pl.BlockSpec((S, tile), lambda rt, info: (0, part(info, rt, T)))
    biases = pl.BlockSpec((vec.shape[0], tile), lambda rt, info: (0, part(info, rt, T)))
    out = shape((S, D), BF16)
    return call(
        kernel, "project_qkv", grid, (T,), grid.info, [tokens, vec] + ws.operands, [fixed((S, D)), biases] + ws.specs,
        (out, out, out), (cols, cols, cols), ws.scratch, cost(6 * S * D * D, 6 * D * D + 8 * S * D),
    )


def row_loop(S, rows, step, start):
    return lax.fori_loop(0, S // rows, lambda i, carry: step(pl.ds(pl.multiple_of(i * rows, rows), rows), carry), start)


def fold(a):
    return jnp.sum(a.reshape(a.shape[0] // 8, 8, a.shape[1]), axis=0)


def turn(src, dst):
    S = src.shape[0]

    def step(i, _):
        at = pl.ds(pl.multiple_of(i * 128, 128), 128)
        dst[:, at] = src[at, :].T
        return 0

    lax.fori_loop(0, S // 128, step, 0)


def normed(r):
    c = r - jnp.mean(r, axis=-1, keepdims=True)
    inv = lax.rsqrt(jnp.mean(c * c, axis=-1, keepdims=True) + EPS)
    return c * inv, inv


def normed_back(d, n, inv):
    return (d - jnp.mean(d, axis=-1, keepdims=True) - n * jnp.mean(d * n, axis=-1, keepdims=True)) * inv


ROWS = 128


def attend_out(grid, pieces, ctx, tokens, vec):
    T = grid.T
    S, D = tokens.shape
    tile = D // T
    ws = Weights(grid, D, [(pieces, 3 * tile, tile, 0)])

    def kernel(info, c, x, vecs, *rest):
        refs, (n1, inv1, low, low_t, w, sem, acc) = rest[: len(ws.specs)], rest[len(ws.specs) :]
        rt = pl.program_id(0)

        @pl.when(rt == 0)
        def _():
            ws.start(info, refs, w, sem)
            acc[...] = jnp.zeros_like(acc)

        ws.wait(info, refs, w, sem, rt, True)

        def chunk(lo, n):
            at = pl.ds(lo, n)
            acc[:, at] += nt_dot(c[...], w[rt, at, :])

        each_chunk(D, WIDE // 2, chunk)

        @pl.when(rt == T - 1)
        def _():
            def step(at, carry):
                n, inv = normed(x[at, :].astype(F32) + (acc[at, :] + vecs[0:1, :]))
                n1[at, :] = n
                inv1[at, :] = jnp.broadcast_to(inv, (ROWS, 128))
                low[at, :] = (n * vecs[1:2, :] + vecs[2:3, :]).astype(BF16)
                return carry

            row_loop(S, ROWS, step, 0)
            turn(low, low_t)

    cols = pl.BlockSpec((S, tile), lambda rt, info: (0, part(info, rt, T)))
    return call(
        kernel, "attend_out", grid, (T,), grid.info, [ctx, tokens, vec] + ws.operands,
        [cols, fixed((S, D)), fixed(vec.shape)] + ws.specs,
        (shape_hbm((S, D), F32), shape((S, 128), F32), shape((S, D), BF16), shape((D, S), BF16)),
        (fixed((S, D)), fixed((S, 128)), fixed((S, D)), fixed((D, S))),
        ws.scratch + [pltpu.VMEM((S, D), F32)], cost(2 * S * D * D, 2 * D * D + 12 * S * D),
    )


def each_chunk(width, size, step):
    n = math.gcd(width, size)

    def body(i, carry):
        step(pl.multiple_of(i * n, n), n)
        return carry

    lax.fori_loop(0, width // n, body, 0)


WIDE = 1024


def expand(grid, ws, low, up_b, FF):
    T = grid.T
    S, D = low.shape
    cols = FF // T

    def kernel(info, x, b, *rest):
        refs, (act, slope, w, sem) = rest[: len(ws.specs)], rest[len(ws.specs) :]
        rt = pl.program_id(0)

        @pl.when(rt == 0)
        def _():
            ws.start(info, refs, w, sem)

        ws.wait(info, refs, w, sem, rt, True)
        def one(lo, n):
            at = pl.ds(lo, n)
            u = dot(x[...], w[rt, :, at]) + b[:, at]
            cdf = 0.5 * (1.0 + lax.erf(u * (2.0**-0.5)))
            act[:, at] = (u * cdf).astype(BF16)
            slope[:, at] = (cdf + u * (jnp.exp(-0.5 * u * u) * 0.3989422804014327)).astype(BF16)

        each_chunk(cols, WIDE // 2, one)

    def at(rt, info):
        return (0, part(info, rt, T))

    block = pl.BlockSpec((S, cols), at)
    out = shape((S, FF), BF16)
    return call(
        kernel, "expand", grid, (T,), grid.info, [low, up_b] + ws.operands,
        [fixed((S, D)), pl.BlockSpec((1, cols), at)] + ws.specs, (shape_hbm((S, FF), BF16), shape_hbm((S, FF), BF16)), (block, block), ws.scratch,
        cost(2 * S * D * FF, 2 * D * FF + 4 * S * FF, 2 * S * FF),
    )


def contract(grid, ws, act, n1, vec, teacher, keep, scales):
    T = grid.T
    S, D = n1.shape
    FF = act.shape[1]
    cols = FF // T

    def kernel(info, scale, a, vecs, kept, n1_any, teacher_any, *rest):
        refs, rest = rest[: len(ws.specs)], rest[len(ws.specs) :]
        low, d_two, d_ffn, d_ffn_t, sums, w, sem, acc, n1_s, teacher_s, own_sem = rest
        rt = pl.program_id(0)
        more = [
            pltpu.make_async_copy(n1_any, n1_s, own_sem.at[0]),
            pltpu.make_async_copy(teacher_any, teacher_s, own_sem.at[1]),
        ]

        @pl.when(rt == 0)
        def _():
            ws.start(info, refs, w, sem)
            for copy in more:
                copy.start()
            acc[...] = jnp.zeros_like(acc)

        ws.wait(info, refs, w, sem, rt, True)

        def one(lo, n):
            at = pl.ds(lo, n)
            acc[:, at] += nt_dot(a[...], w[rt, at, :])

        each_chunk(D, WIDE // 2, one)

        @pl.when(rt == T - 1)
        def _():
            for copy in more:
                copy.wait()

            def step(at, carry):
                s_bias, s_gain, s_shift, s_loss = carry
                first = n1_s[at, :] * vecs[1:2, :] + vecs[2:3, :]
                n, inv = normed(first + (acc[at, :] + vecs[3:4, :]))
                out = n * vecs[4:5, :] + vecs[5:6, :]
                low[at, :] = out.astype(BF16)
                error = out - teacher_s[at, :]
                weighed = kept[at, :] * error
                grad = scale[0] * weighed
                d = normed_back(grad * vecs[4:5, :], n, inv)
                d_two[at, :] = d
                d_ffn[at, :] = d.astype(BF16)
                return (
                    s_bias + fold(d), s_gain + fold(grad * n), s_shift + fold(grad), s_loss + fold(weighed * error),
                )

            zero = jnp.zeros((8, D), F32)
            found = row_loop(S, ROWS, step, (zero, zero, zero, zero))
            found = [jnp.sum(f, axis=0, keepdims=True) for f in found]
            sums[...] = jnp.concatenate(found + [jnp.zeros((4, D), F32)], axis=0)
            turn(d_ffn, d_ffn_t)

    block = pl.BlockSpec((S, cols), lambda rt, info: (0, part(info, rt, T)))
    rows = fixed((S, D))
    return call(
        kernel, "contract", grid, (T,), grid.info, [scales, in_hbm(act), vec, keep, *in_hbm(n1, teacher)] + ws.operands,
        [pl.BlockSpec(memory_space=pltpu.SMEM), block, fixed(vec.shape), fixed((S, 1)), ANY, ANY] + ws.specs,
        (shape_hbm((S, D), BF16), shape_hbm((S, D), F32), shape((S, D), BF16), shape((D, S), BF16), shape((8, D), F32)),
        (rows, rows, rows, fixed((D, S)), fixed((8, D))),
        ws.scratch + [pltpu.VMEM((S, D), F32)] * 3 + [pltpu.SemaphoreType.DMA((2,))],
        cost(2 * S * D * FF, 2 * D * FF + 2 * S * FF + 20 * S * D),
    )


def contract_back(grid, ws, d_ffn, slope):
    T = grid.T
    S, D = d_ffn.shape
    FF = slope.shape[1]
    cols = FF // T

    def kernel(info, x, s, *rest):
        refs, (out, sums, w, sem) = rest[: len(ws.specs)], rest[len(ws.specs) :]
        rt = pl.program_id(0)

        @pl.when(rt == 0)
        def _():
            ws.start(info, refs, w, sem)

        ws.wait(info, refs, w, sem, rt, True)
        def one(lo, n):
            at = pl.ds(lo, n)
            d = (dot(x[...], w[rt, :, at]) * s[:, at].astype(F32)).astype(BF16)
            out[:, at] = d
            sums[:, at] = fold(d.astype(F32))

        each_chunk(cols, WIDE, one)

    def at(rt, info):
        return (0, part(info, rt, T))

    block = pl.BlockSpec((S, cols), at)
    return call(
        kernel, "contract_back", grid, (T,), grid.info, [d_ffn, in_hbm(slope)] + ws.operands,
        [fixed((S, D)), block] + ws.specs, (shape((S, FF), BF16), shape((8, FF), F32)),
        (block, pl.BlockSpec((8, cols), at)), ws.scratch, cost(2 * S * D * FF, 2 * D * FF + 4 * S * FF),
    )


def expand_back(grid, ws, d_hidden, d_two, n1, inv1, vec):
    T = grid.T
    S, D = n1.shape
    FF = d_hidden.shape[1]
    cols = FF // T

    def kernel(info, a, vecs, inv, n1_any, d_two_any, *rest):
        refs, rest = rest[: len(ws.specs)], rest[len(ws.specs) :]
        d_one, d_attn, d_attn_t, sums, w, sem, acc, n1_s, d_two_s, own_sem = rest
        rt = pl.program_id(0)
        more = [
            pltpu.make_async_copy(n1_any, n1_s, own_sem.at[0]),
            pltpu.make_async_copy(d_two_any, d_two_s, own_sem.at[1]),
        ]

        @pl.when(rt == 0)
        def _():
            ws.start(info, refs, w, sem)
            for copy in more:
                copy.start()
            acc[...] = jnp.zeros_like(acc)

        ws.wait(info, refs, w, sem, rt, True)

        def one(lo, n):
            at = pl.ds(lo, n)
            acc[:, at] += nt_dot(a[...], w[rt, at, :])

        each_chunk(D, WIDE // 2, one)

        @pl.when(rt == T - 1)
        def _():
            for copy in more:
                copy.wait()

            def step(at, carry):
                s_bias, s_gain, s_shift = carry
                n = n1_s[at, :]
                grad = d_two_s[at, :] + acc[at, :]
                d = normed_back(grad * vecs[1:2, :], n, inv[at, 0:1])
                d_one[at, :] = d
                d_attn[at, :] = d.astype(BF16)
                return s_bias + fold(d), s_gain + fold(grad * n), s_shift + fold(grad)

            zero = jnp.zeros((8, D), F32)
            found = row_loop(S, ROWS, step, (zero, zero, zero))
            found = [jnp.sum(f, axis=0, keepdims=True) for f in found]
            sums[...] = jnp.concatenate(found + [jnp.zeros((5, D), F32)], axis=0)
            turn(d_attn, d_attn_t)

    block = pl.BlockSpec((S, cols), lambda rt, info: (0, part(info, rt, T)))
    rows = fixed((S, D))
    return call(
        kernel, "expand_back", grid, (T,), grid.info, [in_hbm(d_hidden), vec, inv1, *in_hbm(n1, d_two)] + ws.operands,
        [block, fixed(vec.shape), fixed((S, 128)), ANY, ANY] + ws.specs,
        (shape_hbm((S, D), F32), shape((S, D), BF16), shape((D, S), BF16), shape((8, D), F32)),
        (rows, rows, fixed((D, S)), fixed((8, D))),
        ws.scratch + [pltpu.VMEM((S, D), F32)] * 3 + [pltpu.SemaphoreType.DMA((2,))],
        cost(2 * S * D * FF, 2 * D * FF + 2 * S * FF + 20 * S * D),
    )


def attend_out_back(grid, pieces, d_attn):
    T = grid.T
    S, D = d_attn.shape
    tile = D // T
    ws = Weights(grid, D, [(pieces, 3 * tile, tile, 0)])

    def kernel(info, x, *rest):
        refs, (out, w, sem) = rest[: len(ws.specs)], rest[len(ws.specs) :]
        rt = pl.program_id(0)

        @pl.when(rt == 0)
        def _():
            ws.start(info, refs, w, sem)

        ws.wait(info, refs, w, sem, rt, True)
        out[...] = dot(x[...], w[rt]).astype(BF16)

    cols = pl.BlockSpec((S, tile), lambda rt, info: (0, part(info, rt, T)))
    return call(
        kernel, "attend_out_back", grid, (T,), grid.info, [d_attn] + ws.operands, [fixed((S, D))] + ws.specs,
        shape((S, D), BF16), cols, ws.scratch, cost(2 * S * D * D, 2 * D * D + 4 * S * D),
    )


def project_back(grid, pieces, dq, dk, dv, d_one):
    T = grid.T
    S, D = d_one.shape
    tile = D // T
    ws = Weights(grid, D, [(pieces, 0, 3 * tile, 0)])

    def kernel(info, q, k, v, one, *rest):
        refs, (out, w, sem) = rest[: len(ws.specs)], rest[len(ws.specs) :]
        rt = pl.program_id(0)

        @pl.when(rt == 0)
        def _():
            ws.start(info, refs, w, sem)
            out[...] = one[...]

        ws.wait(info, refs, w, sem, rt, True)
        def chunk(lo, n):
            at = pl.ds(lo, n)
            g = nt_dot(q[...], w[rt, at, :tile]) + nt_dot(k[...], w[rt, at, tile : 2 * tile])
            out[:, at] += g + nt_dot(v[...], w[rt, at, 2 * tile :])

        each_chunk(D, WIDE // 2, chunk)

    cols = pl.BlockSpec((S, tile), lambda rt, info: (0, part(info, rt, T)))
    return call(
        kernel, "project_back", grid, (T,), grid.info, [dq, dk, dv, in_hbm(d_one)] + ws.operands,
        [cols, cols, cols, fixed((S, D))] + ws.specs, shape((S, D), F32), fixed((S, D)), ws.scratch,
        cost(6 * S * D * D, 6 * D * D + 14 * S * D),
    )


def weight_grad(grid, lefts, rights, core, received=None, parts=False, extra=None):
    T, Z = grid.T, grid.Z
    D, S = lefts[0].shape
    R = D // grid.dp
    spans, width = [], 0
    for which, b, lo, count in rights:
        unit = math.gcd(lo, count, b.shape[1] // T)
        spans += [(which, width + i, (lo + i) // unit, unit, b.shape[1] // T // unit, b) for i in range(0, count, unit)]
        width += count

    def kernel(info, *rest):
        left_refs = rest[: len(lefts)]
        right_refs = rest[len(lefts) : len(lefts) + len(spans)]
        rest = list(rest[len(lefts) + len(spans) :])
        more = rest.pop(0) if extra is not None else None
        got = rest.pop(0) if received is not None else None
        *outs, rows = rest
        rt, half = pl.program_id(0), Z // 2

        @pl.when(rt == 0)
        def _():
            for a in range(len(lefts)):
                for rx in range(2):
                    for z in range(Z):
                        at = (z * 4 + (info[1] ^ rx) * 2 + (info[2] ^ core)) * R
                        rows[a, pl.ds((rx * Z + z) * R, R), :] = left_refs[a][pl.ds(pl.multiple_of(at, R), R), :]

        def put(g, to):
            if received is not None:
                g = g + got[0, :, :, :, to].astype(F32)
            g = g.astype(BF16)
            if not parts:
                outs[0][0, :, :, :, to] = g
                return

            @pl.when(rt == 0)
            def _():
                outs[0][:, :, to] = g[0]
                outs[1][half:, :, to] = g[1, :half]
                outs[2][:, :, to] = g[1, half:]

            @pl.when(rt == 1)
            def _():
                outs[1][:half, :, to] = g[1, :half]
                outs[3][:half, :, to] = g[1, half:]
                outs[3][half:, :, to] = g[0, half:]
                outs[4][:, :, to] = g[0, :half]

        for (which, first, _, count, *_), right in zip(spans, right_refs):

            def one(lo, n, which=which, first=first, right=right):
                put(dot(rows[which], right[:, pl.ds(lo, n)]).reshape(2, Z, R, n), pl.ds(first + lo, n))

            each_chunk(count, WIDE, one)
        if extra is not None:
            put(jnp.broadcast_to(more[0].astype(F32), (2, Z, R, 128)), pl.ds(width, 128))

    def right_map(which, start, first, count, every, b):
        return lambda rt, info: (0, part(info, rt, T) * every + first)

    full = width + (128 if extra is not None else 0)
    block = pl.BlockSpec((1, 2, Z, R, full), lambda rt, info: (rt, 0, 0, 0, 0))
    in_specs = [fixed((D, S)) for _ in lefts] + [pl.BlockSpec((S, s[3]), right_map(*s)) for s in spans]
    operands = list(lefts) + [s[5] for s in spans]
    if extra is not None:
        in_specs.append(pl.BlockSpec((1, R, 128), lambda rt, info: (part(info, rt, T), 0, 0)))
        operands.append(extra)
    if received is not None:
        in_specs.append(block)
        operands.append(received)
    out_shapes, out_specs = shape((T, 2, Z, R, full), BF16), block
    if parts:
        sizes = [(Z, R, full), (Z, R, full), (Z // 2, R, full), (Z, R, full), (Z // 2, R, full)]
        out_shapes, out_specs = tuple(shape(s, BF16) for s in sizes), tuple(fixed(s) for s in sizes)
    return call(
        kernel, "weight_grad", grid, (T,), grid.info, operands, in_specs, out_shapes, out_specs,
        [pltpu.VMEM((len(lefts), D // 2, S), BF16)],
        cost(D * S * width * T, 2 * S * width * T + (1 if received is None else 2) * D * width * T), 32,
    )


def own_vectors(grid, table, items):
    R, w = table.shape[0], HD // grid.dp
    exact = {"precision": lax.Precision.HIGHEST, "preferred_element_type": F32}

    def kernel(info, t, *outs):
        d = info[3] * 4 + info[1] * 2 + info[2]
        lane = lax.broadcasted_iota(jnp.int32, (w, 128), 1) - lax.broadcasted_iota(jnp.int32, (w, 128), 0)
        low, high = (jnp.where(lane == d * w + add, 1.0, 0.0) for add in (0, HD))
        at = 0
        for rows, out in zip(items, outs):
            n = rows // 2
            pick = lax.broadcasted_iota(jnp.int32, (n, rows), 1) - 2 * lax.broadcasted_iota(jnp.int32, (n, rows), 0)
            mine = t[at : at + n, :]
            total = jnp.zeros((w, rows), F32)
            for k, e in enumerate((low, high)):
                found = lax.dot_general(e, mine, NT, **exact)
                total = total + jnp.dot(found, jnp.where(pick == k, 1.0, 0.0), **exact)
            out[...] = total
            at += n

    return call(
        kernel, "own_vectors", grid, (1,), grid.info, [table], [fixed(table.shape)],
        tuple(shape((w, rows), F32) for rows in items), tuple(fixed((w, rows)) for rows in items), [],
        cost(0, 8 * R * 128), 16,
    )


def attention_forward(q, k, v, seg_col, seg_row):
    S, D = q.shape
    pairs = D // (2 * HD)

    def kernel(q, k, v, col, row, ctx, probs, bias):
        @pl.when(pl.program_id(0) == 0)
        def _():
            bias[...] = jnp.where(col[...] == row[...], 0.0, MASKED)

        lane = lax.broadcasted_iota(jnp.int32, (S, 2 * HD), 1) < HD
        query = q[...] * jnp.asarray(0.125, BF16)
        zero = jnp.zeros_like(query)
        outs = []
        for h in range(2):
            mine = jnp.where(lane == (h == 0), query, zero)
            s = nt_dot(mine, k[...]) + bias[...]
            e = jnp.exp(s - jnp.max(s, axis=-1, keepdims=True))
            p = (e * (1.0 / jnp.sum(e, axis=-1, keepdims=True))).astype(BF16)
            probs[h] = p
            outs.append(dot(p, v[...]))
        ctx[...] = jnp.where(lane, outs[0], outs[1]).astype(BF16)

    rows = pl.BlockSpec((S, 2 * HD), lambda i: (0, i))
    return pl.pallas_call(
        kernel,
        grid=(pairs,),
        out_shape=(shape((S, D), BF16), shape_hbm((2 * pairs, S, S), BF16)),
        in_specs=[rows, rows, rows, fixed((S, 1)), fixed((1, S))],
        out_specs=(rows, pl.BlockSpec((2, S, S), lambda i: (i, 0, 0))),
        scratch_shapes=[pltpu.VMEM((S, S), F32)],
        cost_estimate=cost(16 * S * S * D, 8 * S * D + 4 * pairs * S * S, 2 * pairs * S * S),
        compiler_params=pltpu.CompilerParams(vmem_limit_bytes=24 << 20),
        name="attention_forward",
    )(q, k, v, seg_col, seg_row)


def attention_backward(q, k, v, ctx, d_ctx, probs):
    S, D = q.shape
    pairs = D // (2 * HD)

    def kernel(q, k, v, ctx, d_ctx, probs, dq, dk, dv, sums):
        lane = lax.broadcasted_iota(jnp.int32, (S, 2 * HD), 1) < HD
        grad = d_ctx[...]
        both = grad.astype(F32) * ctx[...].astype(F32)
        dqs, dks, dvs = [], [], []
        for h in range(2):
            mask = lane == (h == 0)
            inner = jnp.sum(jnp.where(mask, both, 0.0), axis=-1, keepdims=True)
            mine = jnp.where(mask, grad, jnp.zeros_like(grad))
            d_prob = nt_dot(mine, v[...])
            p = probs[h]
            ds = (p.astype(F32) * (d_prob - inner)).astype(BF16)
            dvs.append(lax.dot_general(p, grad, TN, preferred_element_type=F32))
            dqs.append(dot(ds, k[...]))
            dks.append(lax.dot_general(ds, q[...], TN, preferred_element_type=F32))
        a = (jnp.where(lane, dqs[0], dqs[1]) * 0.125).astype(BF16)
        b = jnp.where(lane, dvs[0], dvs[1]).astype(BF16)
        dq[...] = a
        dk[...] = (jnp.where(lane, dks[0], dks[1]) * 0.125).astype(BF16)
        dv[...] = b
        total_a = jnp.sum(a.astype(F32), axis=0, keepdims=True)
        total_b = jnp.sum(b.astype(F32), axis=0, keepdims=True)
        sums[...] = jnp.concatenate([total_a, total_b, jnp.zeros((6, 2 * HD), F32)], axis=0)

    rows = pl.BlockSpec((S, 2 * HD), lambda i: (0, i))
    out = shape((S, D), BF16)
    return pl.pallas_call(
        kernel,
        grid=(pairs,),
        out_shape=(out, out, out, shape((8, D), F32)),
        in_specs=[rows] * 5 + [pl.BlockSpec((2, S, S), lambda i: (i, 0, 0))],
        out_specs=(rows, rows, rows, pl.BlockSpec((8, 2 * HD), lambda i: (0, i))),
        cost_estimate=cost(32 * S * S * D, 16 * S * D + 4 * pairs * S * S),
        compiler_params=pltpu.CompilerParams(vmem_limit_bytes=24 << 20),
        name="attention_backward",
    )(q, k, v, ctx, d_ctx, in_hbm(probs))


def body(
    sizes,
    tokens,
    teacher,
    valid_mask,
    segments,
    loss_scale,
    qkv_weight,
    qv_bias,
    out_weight,
    out_bias,
    first_gain,
    first_shift,
    up_weight,
    up_bias,
    down_weight,
    down_bias,
    second_gain,
    second_shift,
):
    grid = Grid(*sizes)
    grid.here()
    T, dp = grid.T, grid.dp
    S, D = tokens.shape
    assert S == SEQ
    up_cols = up_weight.shape[1]
    FF = up_cols * T
    tile = D // T
    R = D // dp
    cut = up_cols // 2
    keep = valid_mask.astype(F32)

    down_rows = down_weight.T
    down_rows = down_weight.T
    part_of = up_cols - up_cols // 4
    last_own = after(down_rows[:, :part_of])
    vectors = [out_bias, first_gain, first_shift, down_bias, second_gain, second_shift]
    first_own = pack(
        grid, after(qkv_weight, last_own), out_weight.T, [v.T for v in vectors], qv_bias.transpose(0, 2, 1), up_bias.T, valid_mask
    )
    n8, nu = 8 * D // 128, FF // 128
    used = n8 // T + nu // T + 2
    assert used <= R
    middle_own = jnp.concatenate([up_weight, down_rows[:, part_of:]], axis=1)
    first, sent, others = grid.gather(first_own, middle_own, last_own, None)
    table = unpack(grid, first, 4 * tile, R)
    vec = table[:, : n8 // T].reshape(T, 8, tile).transpose(1, 0, 2).reshape(8, D)
    up_b = table[:, n8 // T : n8 // T + nu // T].reshape(1, FF)
    count_all = jnp.sum(table[:, used - 2 : used, 0])
    norm_scale = count_all * D

    mine = lax.dynamic_slice_in_dim(segments, grid.t * S, S)
    tokens_t = tokens.T
    q, k, v = project_qkv(grid, first, after(tokens, tokens_t), vec)
    ctx, probs = attention_forward(q, k, v, mine[:, None], mine[None, :])
    n1, inv1, first_low, first_low_t = attend_out(grid, first, after(ctx, sent), tokens, vec)
    middle, sent, last_of = others(first_low)
    scales = (2.0 * loss_scale / norm_scale).reshape(1)
    up = Weights(grid, D, [(middle, 0, up_cols, 0)])
    act, slope = expand(grid, up, after(first_low, sent, scales), up_b, FF)
    down = Weights(grid, D, [(last_of(act), 0, part_of, 0), (middle, up_cols, up_cols - part_of, part_of)])
    out_low, d_two, d_ffn, d_ffn_t, sums_two = contract(grid, down, act, n1, vec, teacher, keep[:, None], scales)

    square = grid.square

    def bit_values():
        return jnp.exp2(31.0 - jnp.arange(64, dtype=F32))

    def rows_of_sums(sums_one, sums_two, sums_qv, sums_up):
        vectors = jnp.concatenate([sums_one[0:3], sums_two[0:3], sums_qv[0:2]])
        vectors = vectors.reshape(8, T, tile // 128, 128).transpose(1, 0, 2, 3).reshape(T, n8 // T, 128)
        rest = jnp.sum(sums_up, axis=0).reshape(T, nu // T, 128)
        above = jnp.floor(jnp.sum(sums_two[3]) / bit_values())
        bits = above - 2.0 * jnp.floor(above * 0.5)
        bits = jnp.broadcast_to(jnp.concatenate([bits, jnp.zeros((64,), F32)]), (T, 1, 128))
        zeros = jnp.zeros((T, R - used + 1, 128), F32)
        return jnp.concatenate([vectors, rest, bits, zeros], axis=1).astype(BF16)

    def grads(lefts, rights, line_first=False):
        theirs = weight_grad(grid, lefts, rights, 1, line_first=line_first)

        def ours(*wait):
            got = after(arriving, *wait)
            return weight_grad(grid, lefts, rights, 0, got, line_first, square and not line_first)

        arriving = grid.cs(theirs)
        return theirs, arriving, ours

    if square:
        wg = functools.partial(weight_grad, grid)
        start, go_on, end, z, c = grid.plane_start, grid.plane_middle, grid.plane_end, grid.zs, grid.cs
        hop = grid.line_block
        right_a, right_b = [(0, act, 0, cut)], [(0, act, cut, up_cols - cut)]
        sib_a = wg([d_ffn_t], right_a, 1)
        got_a = c(sib_a)
        sib_b = wg([after(d_ffn_t, sib_a)], right_b, 1)
        got_b = c(sib_b)
        a = wg([d_ffn_t], right_a, 0, after(got_a, sib_b), parts=True)
        a_first = start(a)
        d_hidden, sums_up = contract_back(grid, down, after(d_ffn, a[0]), slope)
        b = wg([d_ffn_t], right_b, 0, after(got_b, d_hidden, *a_first), parts=True)
        a_last = go_on(a, a_first)
        right_u = [(0, after(d_hidden, b[0]), 0, up_cols)]
        sib_u = wg([first_low_t], right_u, 1)
        got_u = c(sib_u)
        b_first = start([after(v, *a_last) for v in b])
        d_one, d_attn, d_attn_t, sums_one = expand_back(
            grid, up, after(d_hidden, sib_u), d_two, n1, inv1, vec
        )
        d_ctx = attend_out_back(grid, first, after(d_attn, *a_last, *b_first))
        u = wg([first_low_t], right_u, 0, after(got_u, d_ctx), parts=True)
        u_first = start(u)
        dq, dk, dv, sums_qv = attention_backward(q, k, v, ctx, after(d_ctx, u[0]), probs)
        b_last = go_on(b, [after(f, dq) for f in b_first])
        lefts = [after(tokens_t, dq, *u_first), d_attn_t]
        right_l, right_m = [(0, dq, 0, tile), (0, dk, 0, tile)], [(0, dv, 0, tile), (1, ctx, 0, tile)]
        extra = rows_of_sums(sums_one, sums_two, sums_qv, sums_up)
        sib_l = wg(lefts[:1], right_l, 1, extra=extra)
        got_l = c(sib_l)
        sib_m = wg([after(lefts[0], sib_l, *b_last), d_attn_t], right_m, 1)
        got_m = c(sib_m)
        got_l, got_m = lax.optimization_barrier((got_l, got_m))
        l = wg(lefts[:1], right_l, 0, after(got_l, sib_m), parts=True, extra=extra)
        u_last = go_on(u, [after(f, l[0]) for f in u_first])
        l_first = start(l)
        ab_own = [end((after(p[0], dq), *p[1:]), f, e) for p, f, e in ((a, a_first, a_last), (b, b_first, b_last))]
        ab_own = jnp.concatenate(ab_own, axis=2).astype(BF16)
        abz1 = z(hop(ab_own, 1))
        abz2 = z(hop(after(ab_own, l[0]), 2, abz1))
        u_own = end(u, u_first, u_last).astype(BF16)
        uz1 = z(hop(after(u_own, abz2), 1))
        grad_tokens = project_back(grid, first, after(dq, u_own), dk, dv, d_one)
        m = wg(lefts, right_m, 0, after(got_m, grad_tokens, uz1, *l_first), parts=True)
        l_last = go_on(l, l_first)
        abz3 = z(hop(after(ab_own, uz1), 3, abz2))
        m_first = start(m)
        l_own = end(l, l_first, l_last).astype(BF16)
        uz2 = z(hop(after(u_own, m[0]), 2, uz1))
        lz1 = z(hop(l_own, 1))
        uz3 = z(hop(after(u_own, *m_first), 3, uz2))
        m_last = go_on(m, m_first)
        lz2 = z(hop(after(l_own, *m_first), 2, lz1))
        lz3 = z(hop(l_own, 3, lz2))
        g_up = grid.line_end(u_own, uz3)
        g_l = grid.line_end(l_own, lz3)
        g_ab = grid.line_end(ab_own, abz3)
        g_down_a, g_down_b = g_ab[:, :cut], g_ab[:, cut:]
        g_m = grid.line(end(m, m_first, m_last).astype(BF16))
        sums, g_l = g_l[:, 2 * tile :], g_l[:, : 2 * tile]
        g_qkv, g_out = jnp.concatenate([g_l, g_m[:, :tile]], axis=1), g_m[:, tile:]
    else:

        def reduced(lefts, rights, extra=None):
            theirs = grid.cs(weight_grad(grid, lefts, rights, 1, extra=extra))
            return grid.line(grid.general(weight_grad(grid, lefts, rights, 0, theirs, extra=extra)).astype(BF16))

        g_down_a = reduced([d_ffn_t], [(0, act, 0, cut)])
        g_down_b = reduced([d_ffn_t], [(0, act, cut, up_cols - cut)])
        d_hidden, sums_up = contract_back(grid, down, d_ffn, slope)
        g_up = reduced([first_low_t], [(0, d_hidden, 0, up_cols)])
        d_one, d_attn, d_attn_t, sums_one = expand_back(grid, up, d_hidden, d_two, n1, inv1, vec)
        g_out = reduced([d_attn_t], [(0, ctx, 0, tile)])
        d_ctx = attend_out_back(grid, first, d_attn)
        dq, dk, dv, sums_qv = attention_backward(q, k, v, ctx, d_ctx, probs)
        extra = rows_of_sums(sums_one, sums_two, sums_qv, sums_up)
        g_qkv = reduced([tokens.T], [(0, dq, 0, tile), (0, dk, 0, tile), (0, dv, 0, tile)], extra)
        sums, g_qkv = g_qkv[:, 3 * tile :], g_qkv[:, : 3 * tile]
        grad_tokens = project_back(grid, first, dq, dk, dv, d_one)

    h, hu = D // HD // T, FF // HD // T
    *g8, g_up_b = own_vectors(grid, sums[:used], [h] * 8 + [hu])
    g8, g_up_b = [v.T for v in g8], g_up_b.T
    loss_value = jnp.sum(sums[used - 2, :64] * bit_values()) / norm_scale
    g_down = jnp.concatenate([g_down_a, g_down_b], axis=1)
    return (
        out_low,
        loss_value,
        grad_tokens,
        g_qkv.reshape(R, 3, tile).transpose(1, 0, 2),
        jnp.stack(g8[6:8]),
        g_out.T,
        g8[0],
        g8[1],
        g8[2],
        g_up,
        g_up_b,
        g_down.T,
        g8[3],
        g8[4],
        g8[5],
    )


def solution(mesh):
    vector = P("tensor", "dp")
    rows = P(("dp", "tensor"), None)
    qkv, qv, cols = P(None, "dp", "tensor"), P(None, "tensor", "dp"), P("dp", "tensor")
    return jax.shard_map(
        functools.partial(body, (mesh.shape["dp"], mesh.shape["tensor"])),
        mesh=mesh,
        in_specs=(
            rows, rows, P(("dp", "tensor")), P("dp"), P(), qkv, qv, vector, vector, vector, vector, cols,
            vector, vector, vector, vector, vector,
        ),
        out_specs=(
            rows, P(), rows, qkv, qv, vector, vector, vector, vector, cols, vector, vector, vector, vector, vector,
        ),
        check_vma=False,
    )
```

```python
import functools
import math

import jax
import jax.numpy as jnp
from jax import lax
from jax.experimental import pallas as pl
from jax.experimental.pallas import tpu as pltpu
from jax.sharding import PartitionSpec as P

HD = 64
SEQ = 512
EPS = 1e-06
MASKED = -1e30
F32 = jnp.float32
BF16 = jnp.bfloat16
ANY = pl.BlockSpec(memory_space=pltpu.HBM)
NT = (((1,), (1,)), ((), ()))
TN = (((0,), (0,)), ((), ()))


def cost(flops, nbytes, trans=0):
    return pl.CostEstimate(flops=int(flops), bytes_accessed=int(nbytes), transcendentals=int(trans))


def nt_dot(a, b):
    return lax.dot_general(a, b, NT, preferred_element_type=F32)


def dot(a, b):
    return jnp.dot(a, b, preferred_element_type=F32)


def after(x, *others):
    return lax.optimization_barrier((x, *others))[0] if others else x


def add(a, b):
    return (a.astype(F32) + b.astype(F32)).astype(BF16)


def in_hbm(*arrays):
    kept = tuple(pltpu.with_memory_space_constraint(a, pltpu.HBM) for a in arrays)
    return kept if len(kept) > 1 else kept[0]


class Pieces:
    def __init__(self, parts):
        self.arrays = [a for a, _ in parts]
        self.places = [p for _, p in parts]


class Grid:
    def __init__(self, dp, tensor):
        self.dp, self.T, self.Z = dp, tensor, dp // 4
        assert dp == self.Z * 4
        Z = self.Z
        self.cycle = [0] + list(range(1, Z, 2)) + list(range(2, Z, 2))[::-1]
        self.place = [self.cycle.index(z) for z in range(Z)]
        after = {self.cycle[i]: self.cycle[(i + 1) % Z] for i in range(Z)}
        cells = [(z, x, c) for z in range(Z) for x in range(2) for c in range(2)]
        self.to_z = [(self.rank(z, x, c), self.rank(after[z], x, c)) for z, x, c in cells]
        self.to_x = [(self.rank(z, x, c), self.rank(z, 1 - x, c)) for z, x, c in cells]
        self.to_c = [(self.rank(z, x, c), self.rank(z, x, 1 - c)) for z, x, c in cells]
        self.to_t = [(t, (t + 1) % tensor) for t in range(tensor)]
        self.square = tensor == 2 and Z == 4

    @staticmethod
    def rank(z, x, c):
        return z * 4 + x * 2 + c

    def here(self):
        d = lax.axis_index("dp")
        self.d, self.z, self.x, self.c, self.t = d, d // 4, (d // 2) % 2, d % 2, lax.axis_index("tensor")
        back = []
        for k in range(self.Z):
            options = [self.cycle[(p - k) % self.Z] for p in self.place]
            back.append(sum(jnp.where(self.z == z, o, 0) for z, o in enumerate(options)))
        self.back = back
        self.info = jnp.stack([v.astype(jnp.int32) for v in [self.t, self.x, self.c, self.z] + back])

    def zs(self, a):
        return lax.ppermute(a, "dp", self.to_z)

    def xs(self, a):
        return lax.ppermute(a, "dp", self.to_x)

    def cs(self, a):
        return lax.ppermute(a, "dp", self.to_c)

    def ts(self, a):
        return lax.ppermute(a, "tensor", self.to_t)

    def both_cores(self, parts, late=(), *hold):
        twins = [(self.cs(a), [(t, x, 1, k) for t, x, _, k in places]) for a, places in parts]
        twins += [(self.cs(after(a, *hold)), [(t, x, 1, k) for t, x, _, k in places]) for a, places in late]
        return Pieces(parts + list(late) + twins)

    def gather_general(self, own):
        ring = [own]
        for _ in range(self.Z - 1):
            ring.append(self.zs(ring[-1]))
        line, slots = jnp.stack(ring), range(self.Z)
        parts = [(line, [(0, 0, 0, k) for k in slots]), (self.xs(line), [(0, 1, 0, k) for k in slots])]
        rows = line
        for rt in range(1, self.T):
            rows = self.ts(rows)
            parts.append((rows, [(rt, 0, 0, k) for k in slots]))
            parts.append((self.xs(rows), [(rt, 1, 0, k) for k in slots]))
        return self.both_cores(parts)

    def gather(self, first, middle, last, hold):
        if not self.square:
            whole = [self.gather_general(a) for a in (first, middle, last)]
            return whole[0], first, lambda *_: (whole[1], first, lambda *_: whole[2])
        half = last.shape[0] // 2
        a0, b0, d = first[None], middle, last
        d_x, d_t = self.xs(d), self.ts(d)
        a1 = self.zs(a0)
        a0_x, a0_t = self.xs(after(a0, d_x)), self.ts(after(a0, d_t))
        a2 = self.zs(after(a1, d_x, d_t))
        d_far = [self.xs(after(d_t[:half], a0_x)), self.ts(after(d_x[half:], a0_t))]
        a1_x, a1_t = self.xs(a1), self.ts(a1)
        a3 = self.zs(after(a2, a0_x, a0_t))
        far_0 = self.xs(after(a0_t, a1_x))
        twin = {}

        def twins(**arrays):
            for name, v in arrays.items():
                twin[name] = self.cs(v)
            return [twin[name] for name in arrays]

        early = twins(a0=a0, a1=a1, a0_x=a0_x, a0_t=a0_t, a1_x=a1_x, a1_t=a1_t, far_0=far_0)
        b1 = self.zs(after(b0, a3, *d_far, *early))
        a23 = jnp.concatenate([a2, a3])
        a23_x, a23_t = self.xs(after(a23, far_0, *d_far)), self.ts(after(a23, *d_far))
        far_1, far_2 = self.xs(after(a1_t, a23_x)), self.ts(a23_x)
        plane = jnp.stack([d, d_x, d_t, jnp.concatenate(d_far)])
        early = twins(a23=after(a23, b1))
        b2 = self.zs(after(b1, a23_x, a23_t))
        early = twins(a23_x=after(a23_x, far_1), a23_t=after(a23_t, far_1), far_1=far_1)
        b3 = self.zs(after(b2, plane, far_1))
        twins(far_2=far_2)
        a_far = [far_0, far_1, far_2]
        line = jnp.stack([b0, b1, b2, b3])
        p1 = self.zs(after(plane, b3))

        def at(t, x, *slots):
            return [(t, x, 0, k) for k in slots]

        a_parts = [
            (a0, at(0, 0, 0)), (a1, at(0, 0, 1)), (a23, at(0, 0, 2, 3)),
            (a0_x, at(0, 1, 0)), (a1_x, at(0, 1, 1)), (a23_x, at(0, 1, 2, 3)),
            (a0_t, at(1, 0, 0)), (a1_t, at(1, 0, 1)), (a23_t, at(1, 0, 2, 3)),
            (a_far[0], at(1, 1, 0)), (a_far[1], at(1, 1, 1)), (a_far[2], at(1, 1, 2, 3)),
        ]

        def others(low):
            b_x, b_t = self.xs(after(line, a_far[1])), self.ts(after(line, a_far[2]))
            p2 = self.zs(p1)
            b_far = [self.xs(after(b_t[:2], low)), self.ts(after(b_x[2:], low))]
            p3 = self.zs(p2)
            b_parts = [
                (line, at(0, 0, 0, 1, 2, 3)), (b_x, at(0, 1, 0, 1, 2, 3)), (b_t, at(1, 0, 0, 1, 2, 3)),
                (b_far[0], at(1, 1, 0, 1)), (b_far[1], at(1, 1, 2, 3)),
            ]
            d_parts = [
                (p, [(0, 0, 0, k), (0, 1, 0, k), (1, 0, 0, k), (1, 1, 0, k)]) for k, p in enumerate([plane, p1, p2, p3])
            ]

            return self.both_cores(b_parts), p2, lambda act: self.both_cores(d_parts[:3], d_parts[3:], act)

        names = "a0 a1 a23 a0_x a1_x a23_x a0_t a1_t a23_t far_0 far_1 far_2".split()
        a_twins = [(twin[n], [(t, x, 1, k) for t, x, _, k in places]) for n, (_, places) in zip(names, a_parts)]
        return Pieces(a_parts + a_twins), p1, others

    def total_small(self, v):
        v = v + self.cs(v)
        held = v
        for _ in range(1, self.Z):
            held = self.zs(held)
            v = v + held
        v = v + self.xs(v)
        held = v
        for _ in range(1, self.T):
            held = self.ts(held)
            v = v + held
        return v

    def line_block(self, own, step, held=None):
        block = lax.dynamic_index_in_dim(own, self.back[step], 0, keepdims=False)
        if held is not None:
            block = block.astype(F32) + held.astype(F32)
        return block.astype(BF16)

    def line_hop(self, own, step, held=None):
        return self.zs(self.line_block(own, step, held))

    def line_end(self, own, held):
        return lax.dynamic_index_in_dim(own, self.z, 0, keepdims=False).astype(F32) + held.astype(F32)

    def line(self, own, held=None, first=1):
        for step in range(first, self.Z):
            held = self.line_hop(own, step, held)
        return self.line_end(own, held)

    def plane_start(self, parts):
        return self.xs(parts[1]), self.ts(parts[3])

    def plane_middle(self, parts, found):
        half = parts[2].shape[0]
        return self.xs(add(parts[2], found[1][:half])), self.ts(add(parts[4], found[0][:half]))

    def plane_end(self, parts, found, last):
        half = parts[2].shape[0]
        own = after(parts[0], *last).astype(F32)
        low = own[:half] + found[0][half:].astype(F32) + last[1].astype(F32)
        high = own[half:] + last[0].astype(F32) + found[1][half:].astype(F32)
        return jnp.concatenate([low, high])

    def general(self, g):
        rows = g[:, 0].astype(F32) + self.xs(g[:, 1]).astype(F32)
        held = None
        for step in range(1, self.T):
            block = rows[(self.T - step) % self.T]
            if held is not None:
                block = block + held.astype(F32)
            held = self.ts(block.astype(BF16))
        return rows[0] + held.astype(F32)


class Weights:
    def __init__(self, grid, D, sources):
        self.T, self.D, self.R = grid.T, D, D // grid.dp
        self.sources = sources
        self.width = sum(s[2] for s in sources)
        seen = []
        for pieces, *_ in sources:
            if pieces not in seen:
                seen.append(pieces)
        self.operands = [pltpu.with_memory_space_constraint(a, pltpu.HBM) for pieces in seen for a in pieces.arrays]
        self.first = {id(p): sum(len(q.arrays) for q in seen[:i]) for i, p in enumerate(seen)}
        self.specs = [ANY] * len(self.operands)
        self.scratch = [pltpu.VMEM((self.T, D, self.width), BF16), pltpu.SemaphoreType.DMA((self.T,))]

    def copies(self, info, refs, w, sem, want):
        out = []
        for pieces, lo, count, to in self.sources:
            base = self.first[id(pieces)]
            for i, places in enumerate(pieces.places):
                for entry, (rt, rx, rc, k) in enumerate(places):
                    if rt != want:
                        continue
                    row = (info[4 + k] * 4 + (info[1] ^ rx) * 2 + (info[2] ^ rc)) * self.R
                    src = refs[base + i].at[entry, :, pl.ds(lo, count)]
                    dst = w.at[rt, pl.ds(pl.multiple_of(row, self.R), self.R), pl.ds(to, count)]
                    out.append(pltpu.make_async_copy(src, dst, sem.at[rt]))
        return out

    def start(self, info, refs, w, sem):
        for rt in range(self.T):
            for copy in self.copies(info, refs, w, sem, rt):
                copy.start()

    def wait(self, info, refs, w, sem, rt, first):
        for want in range(self.T):

            @pl.when((rt == want) & first)
            def _(want=want):
                for copy in self.copies(info, refs, w, sem, want):
                    copy.wait()


def pack(grid, qkv_weight, out_rows, vectors, qv_bias, up_bias, valid_mask):
    R, tile = out_rows.shape
    w, h = vectors[0].shape
    S = valid_mask.shape[0]

    def kernel(info, qkv, out_w, mask, *rest):
        *items, qv, up, out, held = rest
        for i in range(3):
            out[:, i * tile : (i + 1) * tile] = qkv[i]
        out[:, 3 * tile : 4 * tile] = out_w[...]
        held[...] = jnp.zeros_like(held)
        d = info[3] * 4 + info[1] * 2 + info[2]
        lane = lax.broadcasted_iota(jnp.int32, (w, 128), 1) - lax.broadcasted_iota(jnp.int32, (w, 128), 0)
        low, high = (jnp.where(lane == d * w + add, 1.0, 0.0).astype(BF16) for add in (0, HD))
        at = 0
        for item in [v[...] for v in items] + [qv[0], qv[1], up[...]]:
            rows = item.shape[1]
            pick = lax.broadcasted_iota(jnp.int32, (rows // 2, rows), 1) - 2 * lax.broadcasted_iota(jnp.int32, (rows // 2, rows), 0)
            even, odd = (jnp.where(pick == k, 1.0, 0.0).astype(BF16) for k in (0, 1))
            wide = [lax.dot_general(item, e, TN, preferred_element_type=F32).astype(BF16) for e in (low, high)]
            held[at : at + rows // 2, :] = dot(even, wide[0]) + dot(odd, wide[1])
            at += rows // 2
        count = jnp.sum(mask[...].astype(F32), axis=1, keepdims=True).astype(jnp.int32)
        rest_of = jnp.bitwise_and(count, 15)
        held[at : at + 1, :] = jnp.broadcast_to((count - rest_of).astype(F32), (1, 128))
        held[at + 1 : at + 2, :] = jnp.broadcast_to(rest_of.astype(F32), (1, 128))
        out[:, 4 * tile :] = held[...].astype(BF16)

    operands = list(in_hbm(qkv_weight, out_rows, valid_mask.reshape(1, S), *vectors, qv_bias, up_bias))
    return call(
        kernel, "pack", grid, (1,), grid.info, operands, [fixed(a.shape) for a in operands],
        shape((R, 4 * tile + 128), BF16), fixed((R, 4 * tile + 128)), [pltpu.VMEM((R, 128), F32)],
        cost(0, 4 * R * 4 * tile), 16,
    )


def unpack(grid, pieces, first, rows):
    T, Z = grid.T, grid.Z
    arrays = [pltpu.with_memory_space_constraint(a, pltpu.HBM) for a in pieces.arrays]
    places = [(i, j, p) for i, ps in enumerate(pieces.places) for j, p in enumerate(ps)]

    def kernel(info, *rest):
        refs, (out, held, sem) = rest[: len(arrays)], rest[len(arrays) :]
        copies = [
            pltpu.make_async_copy(refs[i].at[j, :rows, pl.ds(first, 128)], held.at[n], sem)
            for n, (i, j, _) in enumerate(places)
        ]
        for copy in copies:
            copy.start()
        for copy in copies:
            copy.wait()
        for rt in range(T):
            mine = [n for n, (_, _, p) in enumerate(places) if p[0] == rt]
            total = held[mine[0]].astype(F32)
            for n in mine[1:]:
                total = total + held[n].astype(F32)
            out[pl.ds(part(info, rt, T), 1)] = total[None]

    return call(
        kernel, "unpack", grid, (1,), grid.info, arrays, [ANY] * len(arrays), shape((T, rows, 128), F32),
        fixed((T, rows, 128)), [pltpu.VMEM((len(places), rows, 128), BF16), pltpu.SemaphoreType.DMA],
        cost(0, 4 * len(places) * rows * 128), 16,
    )


def part(info, rt, T):
    return lax.rem(info[0] - rt + T, T)


def call(kernel, name, grid, steps, info, operands, in_specs, outs, out_specs, scratch, estimate, mib=36):
    return pl.pallas_call(
        kernel,
        out_shape=outs,
        grid_spec=pltpu.PrefetchScalarGridSpec(
            num_scalar_prefetch=1, grid=steps, in_specs=in_specs, out_specs=out_specs, scratch_shapes=scratch
        ),
        cost_estimate=estimate,
        compiler_params=pltpu.CompilerParams(vmem_limit_bytes=mib << 20),
        name=name,
    )(info, *operands)


def shape(dims, dtype):
    return jax.ShapeDtypeStruct(dims, dtype)


def shape_hbm(dims, dtype):
    return pltpu.HBM(dims, dtype)


def fixed(dims):
    return pl.BlockSpec(dims, lambda *_: (0,) * len(dims))


def project_qkv(grid, pieces, tokens, vec):
    T = grid.T
    S, D = tokens.shape
    tile = D // T
    ws = Weights(grid, D, [(pieces, 0, 3 * tile, 0)])

    def kernel(info, x, bias, *rest):
        refs, (q, k, v, w, sem) = rest[: len(ws.specs)], rest[len(ws.specs) :]
        rt = pl.program_id(0)

        @pl.when(rt == 0)
        def _():
            ws.start(info, refs, w, sem)

        ws.wait(info, refs, w, sem, rt, True)
        a, mine = x[...], w.at[rt]
        q[...] = (dot(a, mine[:, :tile]) + bias[6:7, :]).astype(BF16)
        k[...] = dot(a, mine[:, tile : 2 * tile]).astype(BF16)
        v[...] = (dot(a, mine[:, 2 * tile :]) + bias[7:8, :]).astype(BF16)

    cols = pl.BlockSpec((S, tile), lambda rt, info: (0, part(info, rt, T)))
    biases = pl.BlockSpec((vec.shape[0], tile), lambda rt, info: (0, part(info, rt, T)))
    out = shape((S, D), BF16)
    return call(
        kernel, "project_qkv", grid, (T,), grid.info, [tokens, vec] + ws.operands, [fixed((S, D)), biases] + ws.specs,
        (out, out, out), (cols, cols, cols), ws.scratch, cost(6 * S * D * D, 6 * D * D + 8 * S * D),
    )


def row_loop(S, rows, step, start):
    return lax.fori_loop(0, S // rows, lambda i, carry: step(pl.ds(pl.multiple_of(i * rows, rows), rows), carry), start)


def fold(a):
    return jnp.sum(a.reshape(a.shape[0] // 8, 8, a.shape[1]), axis=0)


def turn(src, dst):
    S = src.shape[0]

    def step(i, _):
        at = pl.ds(pl.multiple_of(i * 128, 128), 128)
        dst[:, at] = src[at, :].T
        return 0

    lax.fori_loop(0, S // 128, step, 0)


def normed(r):
    c = r - jnp.mean(r, axis=-1, keepdims=True)
    inv = lax.rsqrt(jnp.mean(c * c, axis=-1, keepdims=True) + EPS)
    return c * inv, inv


def normed_back(d, n, inv):
    return (d - jnp.mean(d, axis=-1, keepdims=True) - n * jnp.mean(d * n, axis=-1, keepdims=True)) * inv


ROWS = 128


def attend_out(grid, pieces, ctx, tokens, vec):
    T = grid.T
    S, D = tokens.shape
    tile = D // T
    ws = Weights(grid, D, [(pieces, 3 * tile, tile, 0)])

    def kernel(info, c, x, vecs, *rest):
        refs, (n1, inv1, low, low_t, w, sem, acc) = rest[: len(ws.specs)], rest[len(ws.specs) :]
        rt = pl.program_id(0)

        @pl.when(rt == 0)
        def _():
            ws.start(info, refs, w, sem)
            acc[...] = jnp.zeros_like(acc)

        ws.wait(info, refs, w, sem, rt, True)

        def chunk(lo, n):
            at = pl.ds(lo, n)
            acc[:, at] += nt_dot(c[...], w[rt, at, :])

        each_chunk(D, WIDE // 2, chunk)

        @pl.when(rt == T - 1)
        def _():
            def step(at, carry):
                n, inv = normed(x[at, :].astype(F32) + (acc[at, :] + vecs[0:1, :]))
                n1[at, :] = n
                inv1[at, :] = jnp.broadcast_to(inv, (ROWS, 128))
                low[at, :] = (n * vecs[1:2, :] + vecs[2:3, :]).astype(BF16)
                return carry

            row_loop(S, ROWS, step, 0)
            turn(low, low_t)

    cols = pl.BlockSpec((S, tile), lambda rt, info: (0, part(info, rt, T)))
    return call(
        kernel, "attend_out", grid, (T,), grid.info, [ctx, tokens, vec] + ws.operands,
        [cols, fixed((S, D)), fixed(vec.shape)] + ws.specs,
        (shape_hbm((S, D), F32), shape((S, 128), F32), shape((S, D), BF16), shape((D, S), BF16)),
        (fixed((S, D)), fixed((S, 128)), fixed((S, D)), fixed((D, S))),
        ws.scratch + [pltpu.VMEM((S, D), F32)], cost(2 * S * D * D, 2 * D * D + 12 * S * D),
    )


def each_chunk(width, size, step):
    n = math.gcd(width, size)

    def body(i, carry):
        step(pl.multiple_of(i * n, n), n)
        return carry

    lax.fori_loop(0, width // n, body, 0)


WIDE = 1024


def expand(grid, ws, low, up_b, FF):
    T = grid.T
    S, D = low.shape
    cols = FF // T

    def kernel(info, x, b, *rest):
        refs, (act, slope, w, sem) = rest[: len(ws.specs)], rest[len(ws.specs) :]
        rt = pl.program_id(0)

        @pl.when(rt == 0)
        def _():
            ws.start(info, refs, w, sem)

        ws.wait(info, refs, w, sem, rt, True)
        def one(lo, n):
            at = pl.ds(lo, n)
            u = dot(x[...], w[rt, :, at]) + b[:, at]
            cdf = 0.5 * (1.0 + lax.erf(u * (2.0**-0.5)))
            act[:, at] = (u * cdf).astype(BF16)
            slope[:, at] = (cdf + u * (jnp.exp(-0.5 * u * u) * 0.3989422804014327)).astype(BF16)

        each_chunk(cols, WIDE // 2, one)

    def at(rt, info):
        return (0, part(info, rt, T))

    block = pl.BlockSpec((S, cols), at)
    out = shape((S, FF), BF16)
    return call(
        kernel, "expand", grid, (T,), grid.info, [low, up_b] + ws.operands,
        [fixed((S, D)), pl.BlockSpec((1, cols), at)] + ws.specs, (shape_hbm((S, FF), BF16), shape_hbm((S, FF), BF16)), (block, block), ws.scratch,
        cost(2 * S * D * FF, 2 * D * FF + 4 * S * FF, 2 * S * FF),
    )


def contract(grid, ws, act, n1, vec, teacher, keep, scales):
    T = grid.T
    S, D = n1.shape
    FF = act.shape[1]
    cols = FF // T

    def kernel(info, scale, a, vecs, kept, n1_any, teacher_any, *rest):
        refs, rest = rest[: len(ws.specs)], rest[len(ws.specs) :]
        low, d_two, d_ffn, d_ffn_t, sums, w, sem, acc, n1_s, teacher_s, own_sem = rest
        rt = pl.program_id(0)
        more = [
            pltpu.make_async_copy(n1_any, n1_s, own_sem.at[0]),
            pltpu.make_async_copy(teacher_any, teacher_s, own_sem.at[1]),
        ]

        @pl.when(rt == 0)
        def _():
            ws.start(info, refs, w, sem)
            for copy in more:
                copy.start()
            acc[...] = jnp.zeros_like(acc)

        ws.wait(info, refs, w, sem, rt, True)

        def one(lo, n):
            at = pl.ds(lo, n)
            acc[:, at] += nt_dot(a[...], w[rt, at, :])

        each_chunk(D, WIDE // 2, one)

        @pl.when(rt == T - 1)
        def _():
            for copy in more:
                copy.wait()

            def step(at, carry):
                s_bias, s_gain, s_shift, s_loss = carry
                first = n1_s[at, :] * vecs[1:2, :] + vecs[2:3, :]
                n, inv = normed(first + (acc[at, :] + vecs[3:4, :]))
                out = n * vecs[4:5, :] + vecs[5:6, :]
                low[at, :] = out.astype(BF16)
                error = out - teacher_s[at, :]
                weighed = kept[at, :] * error
                grad = scale[0] * weighed
                d = normed_back(grad * vecs[4:5, :], n, inv)
                d_two[at, :] = d
                d_ffn[at, :] = d.astype(BF16)
                return (
                    s_bias + fold(d), s_gain + fold(grad * n), s_shift + fold(grad), s_loss + fold(weighed * error),
                )

            zero = jnp.zeros((8, D), F32)
            found = row_loop(S, ROWS, step, (zero, zero, zero, zero))
            found = [jnp.sum(f, axis=0, keepdims=True) for f in found]
            sums[...] = jnp.concatenate(found + [jnp.zeros((4, D), F32)], axis=0)
            turn(d_ffn, d_ffn_t)

    block = pl.BlockSpec((S, cols), lambda rt, info: (0, part(info, rt, T)))
    rows = fixed((S, D))
    return call(
        kernel, "contract", grid, (T,), grid.info, [scales, in_hbm(act), vec, keep, *in_hbm(n1, teacher)] + ws.operands,
        [pl.BlockSpec(memory_space=pltpu.SMEM), block, fixed(vec.shape), fixed((S, 1)), ANY, ANY] + ws.specs,
        (shape_hbm((S, D), BF16), shape_hbm((S, D), F32), shape((S, D), BF16), shape((D, S), BF16), shape((8, D), F32)),
        (rows, rows, rows, fixed((D, S)), fixed((8, D))),
        ws.scratch + [pltpu.VMEM((S, D), F32)] * 3 + [pltpu.SemaphoreType.DMA((2,))],
        cost(2 * S * D * FF, 2 * D * FF + 2 * S * FF + 20 * S * D),
    )


def contract_back(grid, ws, d_ffn, slope):
    T = grid.T
    S, D = d_ffn.shape
    FF = slope.shape[1]
    cols = FF // T

    def kernel(info, x, s, *rest):
        refs, (out, sums, w, sem) = rest[: len(ws.specs)], rest[len(ws.specs) :]
        rt = pl.program_id(0)

        @pl.when(rt == 0)
        def _():
            ws.start(info, refs, w, sem)

        ws.wait(info, refs, w, sem, rt, True)
        def one(lo, n):
            at = pl.ds(lo, n)
            d = (dot(x[...], w[rt, :, at]) * s[:, at].astype(F32)).astype(BF16)
            out[:, at] = d
            sums[:, at] = fold(d.astype(F32))

        each_chunk(cols, WIDE, one)

    def at(rt, info):
        return (0, part(info, rt, T))

    block = pl.BlockSpec((S, cols), at)
    return call(
        kernel, "contract_back", grid, (T,), grid.info, [d_ffn, in_hbm(slope)] + ws.operands,
        [fixed((S, D)), block] + ws.specs, (shape((S, FF), BF16), shape((8, FF), F32)),
        (block, pl.BlockSpec((8, cols), at)), ws.scratch, cost(2 * S * D * FF, 2 * D * FF + 4 * S * FF),
    )


def expand_back(grid, ws, d_hidden, d_two, n1, inv1, vec):
    T = grid.T
    S, D = n1.shape
    FF = d_hidden.shape[1]
    cols = FF // T

    def kernel(info, a, vecs, inv, n1_any, d_two_any, *rest):
        refs, rest = rest[: len(ws.specs)], rest[len(ws.specs) :]
        d_one, d_attn, d_attn_t, sums, w, sem, acc, n1_s, d_two_s, own_sem = rest
        rt = pl.program_id(0)
        more = [
            pltpu.make_async_copy(n1_any, n1_s, own_sem.at[0]),
            pltpu.make_async_copy(d_two_any, d_two_s, own_sem.at[1]),
        ]

        @pl.when(rt == 0)
        def _():
            ws.start(info, refs, w, sem)
            for copy in more:
                copy.start()
            acc[...] = jnp.zeros_like(acc)

        ws.wait(info, refs, w, sem, rt, True)

        def one(lo, n):
            at = pl.ds(lo, n)
            acc[:, at] += nt_dot(a[...], w[rt, at, :])

        each_chunk(D, WIDE // 2, one)

        @pl.when(rt == T - 1)
        def _():
            for copy in more:
                copy.wait()

            def step(at, carry):
                s_bias, s_gain, s_shift = carry
                n = n1_s[at, :]
                grad = d_two_s[at, :] + acc[at, :]
                d = normed_back(grad * vecs[1:2, :], n, inv[at, 0:1])
                d_one[at, :] = d
                d_attn[at, :] = d.astype(BF16)
                return s_bias + fold(d), s_gain + fold(grad * n), s_shift + fold(grad)

            zero = jnp.zeros((8, D), F32)
            found = row_loop(S, ROWS, step, (zero, zero, zero))
            found = [jnp.sum(f, axis=0, keepdims=True) for f in found]
            sums[...] = jnp.concatenate(found + [jnp.zeros((5, D), F32)], axis=0)
            turn(d_attn, d_attn_t)

    block = pl.BlockSpec((S, cols), lambda rt, info: (0, part(info, rt, T)))
    rows = fixed((S, D))
    return call(
        kernel, "expand_back", grid, (T,), grid.info, [in_hbm(d_hidden), vec, inv1, *in_hbm(n1, d_two)] + ws.operands,
        [block, fixed(vec.shape), fixed((S, 128)), ANY, ANY] + ws.specs,
        (shape_hbm((S, D), F32), shape((S, D), BF16), shape((D, S), BF16), shape((8, D), F32)),
        (rows, rows, fixed((D, S)), fixed((8, D))),
        ws.scratch + [pltpu.VMEM((S, D), F32)] * 3 + [pltpu.SemaphoreType.DMA((2,))],
        cost(2 * S * D * FF, 2 * D * FF + 2 * S * FF + 20 * S * D),
    )


def attend_out_back(grid, pieces, d_attn):
    T = grid.T
    S, D = d_attn.shape
    tile = D // T
    ws = Weights(grid, D, [(pieces, 3 * tile, tile, 0)])

    def kernel(info, x, *rest):
        refs, (out, w, sem) = rest[: len(ws.specs)], rest[len(ws.specs) :]
        rt = pl.program_id(0)

        @pl.when(rt == 0)
        def _():
            ws.start(info, refs, w, sem)

        ws.wait(info, refs, w, sem, rt, True)
        out[...] = dot(x[...], w[rt]).astype(BF16)

    cols = pl.BlockSpec((S, tile), lambda rt, info: (0, part(info, rt, T)))
    return call(
        kernel, "attend_out_back", grid, (T,), grid.info, [d_attn] + ws.operands, [fixed((S, D))] + ws.specs,
        shape((S, D), BF16), cols, ws.scratch, cost(2 * S * D * D, 2 * D * D + 4 * S * D),
    )


def project_back(grid, pieces, dq, dk, dv, d_one):
    T = grid.T
    S, D = d_one.shape
    tile = D // T
    ws = Weights(grid, D, [(pieces, 0, 3 * tile, 0)])

    def kernel(info, q, k, v, one, *rest):
        refs, (out, w, sem) = rest[: len(ws.specs)], rest[len(ws.specs) :]
        rt = pl.program_id(0)

        @pl.when(rt == 0)
        def _():
            ws.start(info, refs, w, sem)
            out[...] = one[...]

        ws.wait(info, refs, w, sem, rt, True)
        def chunk(lo, n):
            at = pl.ds(lo, n)
            g = nt_dot(q[...], w[rt, at, :tile]) + nt_dot(k[...], w[rt, at, tile : 2 * tile])
            out[:, at] += g + nt_dot(v[...], w[rt, at, 2 * tile :])

        each_chunk(D, WIDE // 2, chunk)

    cols = pl.BlockSpec((S, tile), lambda rt, info: (0, part(info, rt, T)))
    return call(
        kernel, "project_back", grid, (T,), grid.info, [dq, dk, dv, in_hbm(d_one)] + ws.operands,
        [cols, cols, cols, fixed((S, D))] + ws.specs, shape((S, D), F32), fixed((S, D)), ws.scratch,
        cost(6 * S * D * D, 6 * D * D + 14 * S * D),
    )


def weight_grad(grid, lefts, rights, core, received=None, parts=False, extra=None):
    T, Z = grid.T, grid.Z
    D, S = lefts[0].shape
    R = D // grid.dp
    spans, width = [], 0
    for which, b, lo, count in rights:
        unit = math.gcd(lo, count, b.shape[1] // T)
        spans += [(which, width + i, (lo + i) // unit, unit, b.shape[1] // T // unit, b) for i in range(0, count, unit)]
        width += count

    def kernel(info, *rest):
        left_refs = rest[: len(lefts)]
        right_refs = rest[len(lefts) : len(lefts) + len(spans)]
        rest = list(rest[len(lefts) + len(spans) :])
        more = rest.pop(0) if extra is not None else None
        got = rest.pop(0) if received is not None else None
        *outs, rows = rest
        rt, half = pl.program_id(0), Z // 2

        @pl.when(rt == 0)
        def _():
            for a in range(len(lefts)):
                for rx in range(2):
                    for z in range(Z):
                        at = (z * 4 + (info[1] ^ rx) * 2 + (info[2] ^ core)) * R
                        rows[a, pl.ds((rx * Z + z) * R, R), :] = left_refs[a][pl.ds(pl.multiple_of(at, R), R), :]

        def put(g, to):
            if received is not None:
                g = g + got[0, :, :, :, to].astype(F32)
            g = g.astype(BF16)
            if not parts:
                outs[0][0, :, :, :, to] = g
                return

            @pl.when(rt == 0)
            def _():
                outs[0][:, :, to] = g[0]
                outs[1][half:, :, to] = g[1, :half]
                outs[2][:, :, to] = g[1, half:]

            @pl.when(rt == 1)
            def _():
                outs[1][:half, :, to] = g[1, :half]
                outs[3][:half, :, to] = g[1, half:]
                outs[3][half:, :, to] = g[0, half:]
                outs[4][:, :, to] = g[0, :half]

        for (which, first, _, count, *_), right in zip(spans, right_refs):

            def one(lo, n, which=which, first=first, right=right):
                put(dot(rows[which], right[:, pl.ds(lo, n)]).reshape(2, Z, R, n), pl.ds(first + lo, n))

            each_chunk(count, WIDE, one)
        if extra is not None:
            put(jnp.broadcast_to(more[0].astype(F32), (2, Z, R, 128)), pl.ds(width, 128))

    def right_map(which, start, first, count, every, b):
        return lambda rt, info: (0, part(info, rt, T) * every + first)

    full = width + (128 if extra is not None else 0)
    block = pl.BlockSpec((1, 2, Z, R, full), lambda rt, info: (rt, 0, 0, 0, 0))
    in_specs = [fixed((D, S)) for _ in lefts] + [pl.BlockSpec((S, s[3]), right_map(*s)) for s in spans]
    operands = list(lefts) + [s[5] for s in spans]
    if extra is not None:
        in_specs.append(pl.BlockSpec((1, R, 128), lambda rt, info: (part(info, rt, T), 0, 0)))
        operands.append(extra)
    if received is not None:
        in_specs.append(block)
        operands.append(received)
    out_shapes, out_specs = shape((T, 2, Z, R, full), BF16), block
    if parts:
        sizes = [(Z, R, full), (Z, R, full), (Z // 2, R, full), (Z, R, full), (Z // 2, R, full)]
        out_shapes, out_specs = tuple(shape(s, BF16) for s in sizes), tuple(fixed(s) for s in sizes)
    return call(
        kernel, "weight_grad", grid, (T,), grid.info, operands, in_specs, out_shapes, out_specs,
        [pltpu.VMEM((len(lefts), D // 2, S), BF16)],
        cost(D * S * width * T, 2 * S * width * T + (1 if received is None else 2) * D * width * T), 32,
    )


def own_vectors(grid, table, items):
    R, w = table.shape[0], HD // grid.dp
    exact = {"precision": lax.Precision.HIGHEST, "preferred_element_type": F32}

    def kernel(info, t, *outs):
        d = info[3] * 4 + info[1] * 2 + info[2]
        lane = lax.broadcasted_iota(jnp.int32, (w, 128), 1) - lax.broadcasted_iota(jnp.int32, (w, 128), 0)
        low, high = (jnp.where(lane == d * w + add, 1.0, 0.0) for add in (0, HD))
        at = 0
        for rows, out in zip(items, outs):
            n = rows // 2
            pick = lax.broadcasted_iota(jnp.int32, (n, rows), 1) - 2 * lax.broadcasted_iota(jnp.int32, (n, rows), 0)
            mine = t[at : at + n, :]
            total = jnp.zeros((w, rows), F32)
            for k, e in enumerate((low, high)):
                found = lax.dot_general(e, mine, NT, **exact)
                total = total + jnp.dot(found, jnp.where(pick == k, 1.0, 0.0), **exact)
            out[...] = total
            at += n

    return call(
        kernel, "own_vectors", grid, (1,), grid.info, [table], [fixed(table.shape)],
        tuple(shape((w, rows), F32) for rows in items), tuple(fixed((w, rows)) for rows in items), [],
        cost(0, 8 * R * 128), 16,
    )


def attention_forward(q, k, v, seg_col, seg_row):
    S, D = q.shape
    pairs = D // (2 * HD)

    def kernel(q, k, v, col, row, ctx, probs, bias):
        @pl.when(pl.program_id(0) == 0)
        def _():
            bias[...] = jnp.where(col[...] == row[...], 0.0, MASKED)

        lane = lax.broadcasted_iota(jnp.int32, (S, 2 * HD), 1) < HD
        query = q[...] * jnp.asarray(0.125, BF16)
        zero = jnp.zeros_like(query)
        outs = []
        for h in range(2):
            mine = jnp.where(lane == (h == 0), query, zero)
            s = nt_dot(mine, k[...]) + bias[...]
            e = jnp.exp(s - jnp.max(s, axis=-1, keepdims=True))
            p = (e * (1.0 / jnp.sum(e, axis=-1, keepdims=True))).astype(BF16)
            probs[h] = p
            outs.append(dot(p, v[...]))
        ctx[...] = jnp.where(lane, outs[0], outs[1]).astype(BF16)

    rows = pl.BlockSpec((S, 2 * HD), lambda i: (0, i))
    return pl.pallas_call(
        kernel,
        grid=(pairs,),
        out_shape=(shape((S, D), BF16), shape_hbm((2 * pairs, S, S), BF16)),
        in_specs=[rows, rows, rows, fixed((S, 1)), fixed((1, S))],
        out_specs=(rows, pl.BlockSpec((2, S, S), lambda i: (i, 0, 0))),
        scratch_shapes=[pltpu.VMEM((S, S), F32)],
        cost_estimate=cost(16 * S * S * D, 8 * S * D + 4 * pairs * S * S, 2 * pairs * S * S),
        compiler_params=pltpu.CompilerParams(vmem_limit_bytes=24 << 20),
        name="attention_forward",
    )(q, k, v, seg_col, seg_row)


def attention_backward(q, k, v, ctx, d_ctx, probs):
    S, D = q.shape
    pairs = D // (2 * HD)

    def kernel(q, k, v, ctx, d_ctx, probs, dq, dk, dv, sums):
        lane = lax.broadcasted_iota(jnp.int32, (S, 2 * HD), 1) < HD
        grad = d_ctx[...]
        both = grad.astype(F32) * ctx[...].astype(F32)
        dqs, dks, dvs = [], [], []
        for h in range(2):
            mask = lane == (h == 0)
            inner = jnp.sum(jnp.where(mask, both, 0.0), axis=-1, keepdims=True)
            mine = jnp.where(mask, grad, jnp.zeros_like(grad))
            d_prob = nt_dot(mine, v[...])
            p = probs[h]
            ds = (p.astype(F32) * (d_prob - inner)).astype(BF16)
            dvs.append(lax.dot_general(p, grad, TN, preferred_element_type=F32))
            dqs.append(dot(ds, k[...]))
            dks.append(lax.dot_general(ds, q[...], TN, preferred_element_type=F32))
        a = (jnp.where(lane, dqs[0], dqs[1]) * 0.125).astype(BF16)
        b = jnp.where(lane, dvs[0], dvs[1]).astype(BF16)
        dq[...] = a
        dk[...] = (jnp.where(lane, dks[0], dks[1]) * 0.125).astype(BF16)
        dv[...] = b
        total_a = jnp.sum(a.astype(F32), axis=0, keepdims=True)
        total_b = jnp.sum(b.astype(F32), axis=0, keepdims=True)
        sums[...] = jnp.concatenate([total_a, total_b, jnp.zeros((6, 2 * HD), F32)], axis=0)

    rows = pl.BlockSpec((S, 2 * HD), lambda i: (0, i))
    out = shape((S, D), BF16)
    return pl.pallas_call(
        kernel,
        grid=(pairs,),
        out_shape=(out, out, out, shape((8, D), F32)),
        in_specs=[rows] * 5 + [pl.BlockSpec((2, S, S), lambda i: (i, 0, 0))],
        out_specs=(rows, rows, rows, pl.BlockSpec((8, 2 * HD), lambda i: (0, i))),
        cost_estimate=cost(32 * S * S * D, 16 * S * D + 4 * pairs * S * S),
        compiler_params=pltpu.CompilerParams(vmem_limit_bytes=24 << 20),
        name="attention_backward",
    )(q, k, v, ctx, d_ctx, in_hbm(probs))


def body(
    sizes,
    tokens,
    teacher,
    valid_mask,
    segments,
    loss_scale,
    qkv_weight,
    qv_bias,
    out_weight,
    out_bias,
    first_gain,
    first_shift,
    up_weight,
    up_bias,
    down_weight,
    down_bias,
    second_gain,
    second_shift,
):
    grid = Grid(*sizes)
    grid.here()
    T, dp = grid.T, grid.dp
    S, D = tokens.shape
    assert S == SEQ
    up_cols = up_weight.shape[1]
    FF = up_cols * T
    tile = D // T
    R = D // dp
    cut = up_cols // 2
    keep = valid_mask.astype(F32)

    down_rows = down_weight.T
    down_rows = down_weight.T
    part_of = up_cols - up_cols // 4
    last_own = after(down_rows[:, :part_of])
    vectors = [out_bias, first_gain, first_shift, down_bias, second_gain, second_shift]
    first_own = pack(
        grid, after(qkv_weight, last_own), out_weight.T, [v.T for v in vectors], qv_bias.transpose(0, 2, 1), up_bias.T, valid_mask
    )
    n8, nu = 8 * D // 128, FF // 128
    used = n8 // T + nu // T + 2
    assert used <= R
    middle_own = jnp.concatenate([up_weight, down_rows[:, part_of:]], axis=1)
    first, sent, others = grid.gather(first_own, middle_own, last_own, None)
    table = unpack(grid, first, 4 * tile, R)
    vec = table[:, : n8 // T].reshape(T, 8, tile).transpose(1, 0, 2).reshape(8, D)
    up_b = table[:, n8 // T : n8 // T + nu // T].reshape(1, FF)
    count_all = jnp.sum(table[:, used - 2 : used, 0])
    norm_scale = count_all * D

    mine = lax.dynamic_slice_in_dim(segments, grid.t * S, S)
    tokens_t = tokens.T
    q, k, v = project_qkv(grid, first, after(tokens, tokens_t), vec)
    ctx, probs = attention_forward(q, k, v, mine[:, None], mine[None, :])
    n1, inv1, first_low, first_low_t = attend_out(grid, first, after(ctx, sent), tokens, vec)
    middle, sent, last_of = others(first_low)
    scales = (2.0 * loss_scale / norm_scale).reshape(1)
    up = Weights(grid, D, [(middle, 0, up_cols, 0)])
    act, slope = expand(grid, up, after(first_low, sent, scales), up_b, FF)
    down = Weights(grid, D, [(last_of(act), 0, part_of, 0), (middle, up_cols, up_cols - part_of, part_of)])
    out_low, d_two, d_ffn, d_ffn_t, sums_two = contract(grid, down, act, n1, vec, teacher, keep[:, None], scales)

    square = grid.square

    def bit_values():
        return jnp.exp2(31.0 - jnp.arange(64, dtype=F32))

    def rows_of_sums(sums_one, sums_two, sums_qv, sums_up):
        vectors = jnp.concatenate([sums_one[0:3], sums_two[0:3], sums_qv[0:2]])
        vectors = vectors.reshape(8, T, tile // 128, 128).transpose(1, 0, 2, 3).reshape(T, n8 // T, 128)
        rest = jnp.sum(sums_up, axis=0).reshape(T, nu // T, 128)
        above = jnp.floor(jnp.sum(sums_two[3]) / bit_values())
        bits = above - 2.0 * jnp.floor(above * 0.5)
        bits = jnp.broadcast_to(jnp.concatenate([bits, jnp.zeros((64,), F32)]), (T, 1, 128))
        zeros = jnp.zeros((T, R - used + 1, 128), F32)
        return jnp.concatenate([vectors, rest, bits, zeros], axis=1).astype(BF16)

    def grads(lefts, rights, line_first=False):
        theirs = weight_grad(grid, lefts, rights, 1, line_first=line_first)

        def ours(*wait):
            got = after(arriving, *wait)
            return weight_grad(grid, lefts, rights, 0, got, line_first, square and not line_first)

        arriving = grid.cs(theirs)
        return theirs, arriving, ours

    if square:
        wg = functools.partial(weight_grad, grid)
        start, go_on, end, z, c = grid.plane_start, grid.plane_middle, grid.plane_end, grid.zs, grid.cs
        hop = grid.line_block
        right_a, right_b = [(0, act, 0, cut)], [(0, act, cut, up_cols - cut)]
        sib_a = wg([d_ffn_t], right_a, 1)
        got_a = c(sib_a)
        sib_b = wg([after(d_ffn_t, sib_a)], right_b, 1)
        got_b = c(sib_b)
        a = wg([d_ffn_t], right_a, 0, after(got_a, sib_b), parts=True)
        a_first = start(a)
        d_hidden, sums_up = contract_back(grid, down, after(d_ffn, a[0]), slope)
        b = wg([d_ffn_t], right_b, 0, after(got_b, d_hidden, *a_first), parts=True)
        a_last = go_on(a, a_first)
        right_u = [(0, after(d_hidden, b[0]), 0, up_cols)]
        sib_u = wg([first_low_t], right_u, 1)
        got_u = c(sib_u)
        b_first = start(b)
        d_one, d_attn, d_attn_t, sums_one = expand_back(
            grid, up, after(d_hidden, sib_u), d_two, n1, inv1, vec
        )
        d_ctx = attend_out_back(grid, first, after(d_attn, *a_last, *b_first))
        u = wg([first_low_t], right_u, 0, after(got_u, d_ctx), parts=True)
        u_first = start(u)
        dq, dk, dv, sums_qv = attention_backward(q, k, v, ctx, after(d_ctx, u[0]), probs)
        b_last = go_on(b, [after(f, dq) for f in b_first])
        lefts = [after(tokens_t, dq, *u_first), d_attn_t]
        right_l, right_m = [(0, dq, 0, tile), (0, dk, 0, tile)], [(0, dv, 0, tile), (1, ctx, 0, tile)]
        extra = rows_of_sums(sums_one, sums_two, sums_qv, sums_up)
        sib_l = wg(lefts[:1], right_l, 1, extra=extra)
        got_l = c(sib_l)
        sib_m = wg([after(lefts[0], sib_l, *b_last), d_attn_t], right_m, 1)
        got_m = c(sib_m)
        got_l, got_m = lax.optimization_barrier((got_l, got_m))
        l = wg(lefts[:1], right_l, 0, after(got_l, sib_m), parts=True, extra=extra)
        u_last = go_on(u, [after(f, l[0]) for f in u_first])
        l_first = start(l)
        ab_own = [end((after(p[0], dq), *p[1:]), f, e) for p, f, e in ((a, a_first, a_last), (b, b_first, b_last))]
        ab_own = jnp.concatenate(ab_own, axis=2).astype(BF16)
        abz1 = z(hop(ab_own, 1))
        abz2 = z(hop(after(ab_own, l[0]), 2, abz1))
        u_own = end(u, u_first, u_last).astype(BF16)
        uz1 = z(hop(after(u_own, abz2), 1))
        grad_tokens = project_back(grid, first, after(dq, u_own), dk, dv, d_one)
        m = wg(lefts, right_m, 0, after(got_m, grad_tokens, uz1, *l_first), parts=True)
        l_last = go_on(l, l_first)
        abz3 = z(hop(after(ab_own, uz1), 3, abz2))
        m_first = start(m)
        l_own = end(l, l_first, l_last).astype(BF16)
        uz2 = z(hop(after(u_own, m[0]), 2, uz1))
        lz1 = z(hop(l_own, 1))
        uz3 = z(hop(after(u_own, *m_first), 3, uz2))
        m_last = go_on(m, m_first)
        lz2 = z(hop(after(l_own, *m_first), 2, lz1))
        lz3 = z(hop(l_own, 3, lz2))
        g_up = grid.line_end(u_own, uz3)
        g_l = grid.line_end(l_own, lz3)
        g_ab = grid.line_end(ab_own, abz3)
        g_down_a, g_down_b = g_ab[:, :cut], g_ab[:, cut:]
        g_m = grid.line(end(m, m_first, m_last).astype(BF16))
        sums, g_l = g_l[:, 2 * tile :], g_l[:, : 2 * tile]
        g_qkv, g_out = jnp.concatenate([g_l, g_m[:, :tile]], axis=1), g_m[:, tile:]
    else:

        def reduced(lefts, rights, extra=None):
            theirs = grid.cs(weight_grad(grid, lefts, rights, 1, extra=extra))
            return grid.line(grid.general(weight_grad(grid, lefts, rights, 0, theirs, extra=extra)).astype(BF16))

        g_down_a = reduced([d_ffn_t], [(0, act, 0, cut)])
        g_down_b = reduced([d_ffn_t], [(0, act, cut, up_cols - cut)])
        d_hidden, sums_up = contract_back(grid, down, d_ffn, slope)
        g_up = reduced([first_low_t], [(0, d_hidden, 0, up_cols)])
        d_one, d_attn, d_attn_t, sums_one = expand_back(grid, up, d_hidden, d_two, n1, inv1, vec)
        g_out = reduced([d_attn_t], [(0, ctx, 0, tile)])
        d_ctx = attend_out_back(grid, first, d_attn)
        dq, dk, dv, sums_qv = attention_backward(q, k, v, ctx, d_ctx, probs)
        extra = rows_of_sums(sums_one, sums_two, sums_qv, sums_up)
        g_qkv = reduced([tokens.T], [(0, dq, 0, tile), (0, dk, 0, tile), (0, dv, 0, tile)], extra)
        sums, g_qkv = g_qkv[:, 3 * tile :], g_qkv[:, : 3 * tile]
        grad_tokens = project_back(grid, first, dq, dk, dv, d_one)

    h, hu = D // HD // T, FF // HD // T
    *g8, g_up_b = own_vectors(grid, sums[:used], [h] * 8 + [hu])
    g8, g_up_b = [v.T for v in g8], g_up_b.T
    loss_value = jnp.sum(sums[used - 2, :64] * bit_values()) / norm_scale
    g_down = jnp.concatenate([g_down_a, g_down_b], axis=1)
    return (
        out_low,
        loss_value,
        grad_tokens,
        g_qkv.reshape(R, 3, tile).transpose(1, 0, 2),
        jnp.stack(g8[6:8]),
        g_out.T,
        g8[0],
        g8[1],
        g8[2],
        g_up,
        g_up_b,
        g_down.T,
        g8[3],
        g8[4],
        g8[5],
    )


def solution(mesh):
    vector = P("tensor", "dp")
    rows = P(("dp", "tensor"), None)
    qkv, qv, cols = P(None, "dp", "tensor"), P(None, "tensor", "dp"), P("dp", "tensor")
    return jax.shard_map(
        functools.partial(body, (mesh.shape["dp"], mesh.shape["tensor"])),
        mesh=mesh,
        in_specs=(
            rows, rows, P(("dp", "tensor")), P("dp"), P(), qkv, qv, vector, vector, vector, vector, cols,
            vector, vector, vector, vector, vector,
        ),
        out_specs=(
            rows, P(), rows, qkv, qv, vector, vector, vector, vector, cols, vector, vector, vector, vector, vector,
        ),
        check_vma=False,
    )
```
